32 devices in a mesh: gx: 2 (over x), gy: 4 (over z), gz: 4 (over y, core).
Axes of the slice: x: 2, y: 2, z: 4, core: 2. Of those that a mesh axis runs over, the one named last changes fastest.
Arguments:
- density: float32 [4, 32, 96, 256], P('gz', 'gy', None, 'gx'), may hold values from 0.2 to 1
- bone: int32 [4, 32, 96, 256], P('gz', 'gy', None, 'gx'), may hold values 0 or 1
- fixed: int32 [4, 32, 96, 256], P('gz', 'gy', None, 'gx'), may hold values 0 or 1
- load: float32 [3, 4, 32, 96, 256], P(None, 'gz', 'gy', None, 'gx'), may hold values from -6 to 6
Outputs:
- density_new: float32 [4, 32, 96, 256], P('gz', 'gy', None, 'gx')
- displacement: float32 [3, 4, 32, 96, 256], P(None, 'gz', 'gy', None, 'gx')
The draws below stay inside these ranges and needn't reach their ends.
All inputs are finite; a program needn't handle non-finite values. No bound on the sum of `bone` or of `fixed` on one device may be relied on, other than what follows from the above.
Results may differ from the reference program's by a relative error of at most 0.00024.
Values sent between devices are 32-bit elements; how exact they have to be, the bound alone decides.
No kernel may reach another device: no remote copies, remote signals or barrier semaphores. Data moves between devices by JAX's collectives and lax.ppermute only.
A program may use at most 64 MiB of HBM per device.

```python
import math
import jax
import jax.numpy as jnp
import numpy as np
from jax import lax

ZB = 32
RAD = 24
ITERS = 2
NX = 256
NY = 96
NZ = 128
N_GZ = 4


def draw_load(key, part):
    noise = jax.random.normal(key, (3, N_GZ, ZB, NY, NX), jnp.float32)
    traction = jnp.array([1.0, 0.0, 0.0], jnp.float32)
    return jnp.clip(noise + traction[:, None, None, None, None], -6.0, 6.0)


def plant(entries, own_key, smallest, top_value):
    extent = entries.shape
    spot = [jax.random.randint(jax.random.fold_in(own_key, axis), (), 0, extent[axis]) for axis in range(len(extent))]
    entries = entries.at[tuple(spot)].set(smallest)
    longest = extent.index(max(extent))
    spot[longest] = (spot[longest] + 1) % extent[longest]
    return entries.at[tuple(spot)].set(top_value)


def block_scale(rng, dims, split, least, high):
    gain, own = 1.0, jax.random.fold_in(rng, 6)
    for position, shards_of in split:
        heights = jnp.exp(jax.random.uniform(jax.random.fold_in(own, position), (shards_of,), jnp.float32, least / len(split), high / len(split)))
        gain = gain * jnp.repeat(heights, dims[position] // shards_of).reshape([-1 if axis == position else 1 for axis in range(len(dims))])
    return gain


def setup_inputs(seed: int = 0) -> dict:
    seeds = jax.random.split(jax.random.key(seed), 5)
    density = jnp.clip(0.2 + 0.8 * jax.random.uniform(seeds[0], (N_GZ, ZB, NY, NX), jnp.float32) ** block_scale(seeds[0], (N_GZ, ZB, NY, NX), ((0, 4), (1, 4), (3, 2)), -0.2, 0.2), 0.2, 1.0)
    bone = plant((jax.random.randint(seeds[1], (N_GZ, ZB, NY, NX), 0, 5) < 3).astype(jnp.int32), jax.random.fold_in(seeds[1], 1), 0, 1)
    fixed = plant((jax.random.randint(seeds[2], (N_GZ, ZB, NY, NX), 0, 16) < 1).astype(jnp.int32), jax.random.fold_in(seeds[2], 1), 0, 1)
    load = draw_load(jax.random.fold_in(seeds[4], 71), 0)
    return {"density": density, "bone": bone, "fixed": fixed, "load": load}


MARROW = 0.1
REMODEL = 0.25
FLOOR = 0.2
CEILING = 1.0
EPSILON = 1e-06

def element_stiffness():
    poisson = 0.3
    lame = poisson / ((1.0 + poisson) * (1.0 - 2.0 * poisson))
    shear = 0.5 / (1.0 + poisson)
    elastic = np.zeros((6, 6))
    elastic[:3, :3] = lame
    for index in range(3):
        elastic[index, index] += 2.0 * shear
        elastic[index + 3, index + 3] = shear
    points = [0.5 - 0.5 / math.sqrt(3.0), 0.5 + 0.5 / math.sqrt(3.0)]
    matrix = np.zeros((24, 24))
    for point_z in points:
        for point_y in points:
            for point_x in points:
                strain = np.zeros((6, 24))
                for corner_z in range(2):
                    for corner_y in range(2):
                        for corner_x in range(2):
                            node = 4 * corner_z + 2 * corner_y + corner_x
                            shape_x = point_x if corner_x else 1.0 - point_x
                            shape_y = point_y if corner_y else 1.0 - point_y
                            shape_z = point_z if corner_z else 1.0 - point_z
                            slope_x = 1.0 if corner_x else -1.0
                            slope_y = 1.0 if corner_y else -1.0
                            slope_z = 1.0 if corner_z else -1.0
                            along_x = slope_x * shape_y * shape_z
                            along_y = shape_x * slope_y * shape_z
                            along_z = shape_x * shape_y * slope_z
                            strain[0, node] = along_x
                            strain[1, 8 + node] = along_y
                            strain[2, 16 + node] = along_z
                            strain[3, node] = along_y
                            strain[3, 8 + node] = along_x
                            strain[4, 8 + node] = along_z
                            strain[4, 16 + node] = along_y
                            strain[5, node] = along_z
                            strain[5, 16 + node] = along_x
                matrix = matrix + strain.T @ elastic @ strain / 8.0
    return matrix

def corners():
    return [(corner_z, corner_y, corner_x) for corner_z in range(2) for corner_y in range(2) for corner_x in range(2)]

def gathered_forces(nodes, moduli, stiffness):
    depth, rows, width = moduli.shape
    height = rows - 1
    columns = jnp.stack([nodes[:, cz:cz + depth, cy:cy + rows, cx:cx + width] for cz, cy, cx in corners()], axis=1)
    product = jnp.dot(stiffness, columns.reshape(24, -1), precision=lax.Precision.HIGHEST)
    product = product.reshape(3, 8, depth, rows, width) * moduli
    product = jnp.pad(product, ((0, 0), (0, 0), (1, 1), (0, 0), (1, 1)))
    total = jnp.zeros((3, depth + 1, height, width + 1), jnp.float32)
    for node, (cz, cy, cx) in enumerate(corners()):
        total = total + product[:, node, 1 - cz:2 - cz + depth, 1 - cy:1 - cy + height, 1 - cx:2 - cx + width]
    return total

def element_energy(nodes, moduli, stiffness):
    depth, height, width = moduli.shape
    columns = jnp.stack([nodes[:, cz:cz + depth, cy:cy + height, cx:cx + width] for cz, cy, cx in corners()], axis=1)
    columns = columns.reshape(24, -1)
    product = jnp.dot(stiffness, columns, precision=lax.Precision.HIGHEST)
    return 0.5 * moduli * lax.optimization_barrier(jnp.sum(columns * product, axis=0)).reshape(depth, height, width)

def stiffness_diagonal(moduli_ext, stiffness, depth, height, width):
    main = jnp.diagonal(stiffness).reshape(3, 8)
    total = jnp.zeros((3, depth, height, width), jnp.float32)
    for node, (cz, cy, cx) in enumerate(corners()):
        piece = moduli_ext[1 - cz:1 - cz + depth, 1 - cy:1 - cy + height, 1 - cx:1 - cx + width]
        total = total + main[:, node][:, None, None, None] * piece[None]
    return total

def taps(radius):
    offsets = jnp.arange(2 * radius + 1).astype(jnp.float32) - radius
    raw = jnp.exp(-jnp.abs(offsets) / (0.5 * radius))
    return raw / jnp.sum(raw)

def smooth_reference(values, axis):
    weights = taps(RAD)
    length = values.shape[axis]
    widths = [(0, 0), (0, 0), (0, 0)]
    widths[axis] = (RAD, RAD)
    padded = jnp.pad(values, widths)
    total = jnp.zeros(values.shape, jnp.float32)
    for index in range(2 * RAD + 1):
        total = total + weights[index] * lax.slice_in_dim(padded, index, index + length, axis=axis)
    return total

def reference(density, bone, fixed, load):
    stiffness = jnp.asarray(element_stiffness(), jnp.float32)
    grid_density = density.reshape(NZ, NY, NX)
    bone_share = bone.reshape(NZ, NY, NX).astype(jnp.float32)
    free_nodes = 1.0 - fixed.reshape(NZ, NY, NX).astype(jnp.float32)
    modulus = bone_share * grid_density * grid_density + (1.0 - bone_share) * MARROW
    moduli_padded = jnp.pad(modulus, ((0, 0), (1, 0), (0, 0)))
    diagonal_full = stiffness_diagonal(jnp.pad(modulus, ((1, 0), (1, 0), (1, 0))), stiffness, NZ, NY, NX)
    precondition = free_nodes / diagonal_full
    starts = jnp.arange(N_GZ).astype(jnp.int32) * ZB

    def operate(field):
        nodes = jnp.pad(free_nodes * field, ((0, 0), (0, 1), (1, 1), (0, 1)))

        def one_block(start):
            block_nodes = lax.dynamic_slice_in_dim(nodes, start, ZB + 1, 1)
            block_moduli = lax.dynamic_slice_in_dim(moduli_padded, start, ZB, 0)
            return gathered_forces(block_nodes, block_moduli, stiffness)
        blocks = lax.map(one_block, starts)
        own = blocks[:, :, :ZB, :, :NX]
        tops = blocks[:, :, ZB:, :, :NX]
        carried = jnp.concatenate([jnp.zeros_like(tops[:1]), tops[:-1]], axis=0)
        own = jnp.concatenate([own[:, :, :1] + carried, own[:, :, 1:]], axis=2)
        return free_nodes * jnp.moveaxis(own, 0, 1).reshape(3, NZ, NY, NX)
    residual = free_nodes * load.reshape(3, NZ, NY, NX)
    solution = jnp.zeros_like(residual)
    search = precondition * residual
    gamma = jnp.sum(residual * search)
    for count in range(ITERS):
        image = operate(search)
        alpha = gamma / jnp.sum(search * image)
        solution = solution + alpha * search
        residual = residual - alpha * image
        scaled = precondition * residual
        gamma_next = jnp.sum(residual * scaled)
        search = scaled + gamma_next / gamma * search
        gamma = gamma_next
    nodes = jnp.pad(solution, ((0, 0), (0, 1), (0, 1), (0, 1)))

    def energy_block(start):
        block_nodes = lax.dynamic_slice_in_dim(nodes, start, ZB + 1, 1)
        block_moduli = lax.dynamic_slice_in_dim(modulus, start, ZB, 0)
        return element_energy(block_nodes, block_moduli, stiffness)
    energy = lax.map(energy_block, starts).reshape(NZ, NY, NX)
    specific = energy / grid_density
    stimulus = smooth_reference(smooth_reference(smooth_reference(specific, 2), 1), 0)
    mean = jnp.sum(stimulus) / (NX * NY * NZ)
    updated = grid_density + REMODEL * bone_share * (stimulus / (mean + EPSILON) - 1.0)
    updated = jnp.clip(updated, FLOOR, CEILING)
    return (updated.reshape(N_GZ, ZB, NY, NX), solution.reshape(3, N_GZ, ZB, NY, NX))
```

```python
import math

import jax
import jax.numpy as jnp
import numpy as np
from jax import lax
from jax.sharding import PartitionSpec as P

RAD = 24
ITERS = 2


MARROW = 0.1
REMODEL = 0.25
FLOOR = 0.2
CEILING = 1.0
EPSILON = 1e-06


def shifted(value, axis, steps):
    count = lax.axis_size(axis)
    initial, last = (max(0, -steps), min(count, count - steps))
    return lax.ppermute(value, axis, [(source, source + steps) for source in range(initial, last)])


def from_behind(block, axis, distance):
    devices = range(lax.axis_size(axis))
    route = [((i - distance) % len(devices), i) for i in devices]
    return lax.ppermute(block, axis, route)


def extended(block, sides, width):
    for axis, dim in sides:
        count = lax.axis_size(axis)
        forward = [(i, i + 1) for i in range(count - 1)]
        backward = [(target, source) for source, target in forward]
        low = lax.ppermute(
            lax.slice_in_dim(block, block.shape[dim] - width, None, axis=dim), axis, forward
        )
        high = lax.ppermute(lax.slice_in_dim(block, 0, width, axis=dim), axis, backward)
        block = jnp.concatenate([low, block, high], axis=dim)
    return block


def element_stiffness():
    poisson = 0.3
    lame = poisson / ((1.0 + poisson) * (1.0 - 2.0 * poisson))
    shear = 0.5 / (1.0 + poisson)
    elastic = np.zeros((6, 6))
    elastic[:3, :3] = lame
    for index in range(3):
        elastic[index, index] += 2.0 * shear
        elastic[index + 3, index + 3] = shear
    points = [0.5 - 0.5 / math.sqrt(3.0), 0.5 + 0.5 / math.sqrt(3.0)]
    matrix = np.zeros((24, 24))
    for point_z in points:
        for point_y in points:
            for point_x in points:
                strain = np.zeros((6, 24))
                for corner_z in range(2):
                    for corner_y in range(2):
                        for corner_x in range(2):
                            node = 4 * corner_z + 2 * corner_y + corner_x
                            shape_x = point_x if corner_x else 1.0 - point_x
                            shape_y = point_y if corner_y else 1.0 - point_y
                            shape_z = point_z if corner_z else 1.0 - point_z
                            slope_x = 1.0 if corner_x else -1.0
                            slope_y = 1.0 if corner_y else -1.0
                            slope_z = 1.0 if corner_z else -1.0
                            along_x = slope_x * shape_y * shape_z
                            along_y = shape_x * slope_y * shape_z
                            along_z = shape_x * shape_y * slope_z
                            strain[0, node] = along_x
                            strain[1, 8 + node] = along_y
                            strain[2, 16 + node] = along_z
                            strain[3, node] = along_y
                            strain[3, 8 + node] = along_x
                            strain[4, 8 + node] = along_z
                            strain[4, 16 + node] = along_y
                            strain[5, node] = along_z
                            strain[5, 16 + node] = along_x
                matrix = matrix + strain.T @ elastic @ strain / 8.0
    return matrix


def corners():
    return [
        (corner_z, corner_y, corner_x)
        for corner_z in range(2)
        for corner_y in range(2)
        for corner_x in range(2)
    ]


def corner_values(nodes, depth, height, width):
    values = []
    for component in range(3):
        for cz, cy, cx in corners():
            values.append(nodes[component, cz : cz + depth, cy : cy + height, cx : cx + width])
    return values


def element_rows(values, table):
    products = []
    for row in range(24):
        total = values[0] * float(table[row, 0])
        for column in range(1, 24):
            total = total + values[column] * float(table[row, column])
        products.append(total)
    return products


def lean_forces(nodes, moduli, table):
    depth, height, width = moduli.shape
    products = element_rows(corner_values(nodes, depth, height, width), table)
    components = []
    for component in range(3):
        total = jnp.zeros((depth + 1, height + 1, width + 1), jnp.float32)
        for node, (cz, cy, cx) in enumerate(corners()):
            term = moduli * products[component * 8 + node]
            total = total + jnp.pad(term, ((cz, 1 - cz), (cy, 1 - cy), (cx, 1 - cx)))
        components.append(total)
    return jnp.stack(components, axis=0)


def lean_energy(nodes, moduli, table):
    depth, height, width = moduli.shape
    values = corner_values(nodes, depth, height, width)
    products = element_rows(values, table)
    total = values[0] * products[0]
    for row in range(1, 24):
        total = total + values[row] * products[row]
    return 0.5 * moduli * total


def stiffness_diagonal(moduli_ext, stiffness, depth, height, width):
    main = jnp.diagonal(stiffness).reshape(3, 8)
    total = jnp.zeros((3, depth, height, width), jnp.float32)
    for node, (cz, cy, cx) in enumerate(corners()):
        piece = moduli_ext[
            1 - cz : 1 - cz + depth, 1 - cy : 1 - cy + height, 1 - cx : 1 - cx + width
        ]
        total = total + main[:, node][:, None, None, None] * piece[None]
    return total


def banded(length_in, length_out, radius):
    offsets = jnp.arange(2 * radius + 1).astype(jnp.float32) - radius
    normal = jnp.sum(jnp.exp(-jnp.abs(offsets) / (0.5 * radius)))
    inputs = jnp.arange(length_in)[:, None]
    outputs = jnp.arange(length_out)[None, :]
    distance = (inputs - (length_in - length_out) // 2 - outputs).astype(jnp.float32)
    weight = jnp.exp(-jnp.abs(distance) / (0.5 * radius)) / normal
    return jnp.where(jnp.abs(distance) <= radius, weight, 0.0)


def smooth(values, axis, length_out):
    matrix = banded(values.shape[axis], length_out, RAD)
    if axis == 2:
        return jnp.einsum("zyi,io->zyo", values, matrix, precision=lax.Precision.HIGHEST)
    if axis == 1:
        return jnp.einsum("zix,io->zox", values, matrix, precision=lax.Precision.HIGHEST)
    return jnp.einsum("iyx,io->oyx", values, matrix, precision=lax.Precision.HIGHEST)


def upper_nodes(field):
    column = shifted(field[:, :, :, :1], "gx", -1)
    wide = jnp.concatenate([field, column], axis=3)
    inner = from_behind(wide[:, :1], "gy", -1)
    outer = shifted(inner, "gz", -1)
    position = lax.axis_index("gy")
    upper = jnp.where(position == lax.axis_size("gy") - 1, outer, inner)
    return jnp.concatenate([wide, upper], axis=1)


def fold_upper(values):
    depth = values.shape[1] - 1
    width = values.shape[3] - 1
    inner = from_behind(values[:, depth:], "gy", 1)
    outer = shifted(inner, "gz", 1)
    position = lax.axis_index("gy")
    carried = jnp.where(position == 0, outer, inner)
    values = jnp.concatenate([values[:, :1] + carried, values[:, 1:depth]], axis=1)
    column = shifted(values[:, :, :, width:], "gx", 1)
    return jnp.concatenate([values[:, :, :, :1] + column, values[:, :, :, 1:width]], axis=3)


def node_forces(field, modulus, table):
    height = field.shape[2]
    nodes = jnp.pad(upper_nodes(field), ((0, 0), (0, 0), (0, 1), (0, 0)))
    forces = lean_forces(nodes, modulus, table)
    return fold_upper(forces[:, :, :height])


def local_energy(solution, modulus, table):
    nodes = jnp.pad(upper_nodes(solution), ((0, 0), (0, 0), (0, 1), (0, 0)))
    return lean_energy(nodes, modulus, table)


def total_over_mesh(value):
    for axis in ("gx", "gy", "gz"):
        count = lax.axis_size(axis)
        if count & (count - 1):
            value = lax.psum(value, axis)
            continue
        step = 1
        while step < count:
            other = lax.ppermute(value, axis, [(i, i ^ step) for i in range(count)])
            value = value + other
            step *= 2
    return value


def inner_sum(values):
    return total_over_mesh(jnp.full((8, 128), jnp.sum(values)))[0, 0]


def to_bricks(values):
    return lax.all_to_all(values, "gy", split_axis=2, concat_axis=1, tiled=True)


def to_slabs(values):
    return lax.all_to_all(values, "gy", split_axis=1, concat_axis=2, tiled=True)


def on_device(density, bone, fixed, load):
    table = element_stiffness()
    stiffness = jnp.asarray(table, jnp.float32)
    local_density = density[0]
    bone_share = bone[0].astype(jnp.float32)
    free_nodes = 1.0 - fixed[0].astype(jnp.float32)
    modulus = bone_share * local_density * local_density + (1.0 - bone_share) * MARROW
    depth, height, width = local_density.shape
    moduli_ext = jnp.pad(modulus, ((1, 1), (1, 0), (1, 1)))
    diagonal_part = stiffness_diagonal(moduli_ext, stiffness, depth + 1, height, width + 1)
    precondition = free_nodes / fold_upper(diagonal_part)
    residual = free_nodes * load[:, 0]
    solution = jnp.zeros_like(residual)
    search = precondition * residual
    gamma = inner_sum(residual * search)
    for count in range(ITERS):
        image = free_nodes * node_forces(free_nodes * search, modulus, table)
        alpha = gamma / inner_sum(search * image)
        solution = solution + alpha * search
        if count + 1 < ITERS:
            residual = residual - alpha * image
            scaled = precondition * residual
            gamma_next = inner_sum(residual * scaled)
            search = scaled + gamma_next / gamma * search
            gamma = gamma_next
    energy = local_energy(solution, modulus, table)
    specific = energy / local_density
    sideways = extended(specific, (("gx", 2),), RAD)
    planar = smooth(smooth(sideways, 2, width), 1, height)
    brick = to_bricks(planar[None])[0]
    deep = extended(brick, (("gz", 0),), RAD)
    stimulus = smooth(deep, 0, brick.shape[0])
    total = inner_sum(stimulus)
    cells = stimulus.size * lax.axis_size("gx") * lax.axis_size("gy") * lax.axis_size("gz")
    mean = total / cells
    returned = to_slabs(stimulus[None])[0]
    updated = local_density + REMODEL * bone_share * (returned / (mean + EPSILON) - 1.0)
    updated = jnp.clip(updated, FLOOR, CEILING)
    return (updated[None], solution[:, None])


def solution(mesh):
    placed = (
        P("gz", "gy", None, "gx"),
        P("gz", "gy", None, "gx"),
        P("gz", "gy", None, "gx"),
        P(None, "gz", "gy", None, "gx"),
    )
    return jax.shard_map(
        on_device,
        mesh=mesh,
        in_specs=placed,
        out_specs=(P("gz", "gy", None, "gx"), P(None, "gz", "gy", None, "gx")),
        check_vma=False,
    )
```

```python
import functools
import math

import jax
import jax.numpy as jnp
import numpy as np
from jax import lax
from jax.experimental import pallas as pl
from jax.experimental.pallas import tpu as pltpu
from jax.sharding import PartitionSpec as P

RAD = 24
ITERS = 2

MARROW = 0.1
REMODEL = 0.25
FLOOR = 0.2
CEILING = 1.0
EPSILON = 1e-06

LANES = 128
PAD = 8
GUARD = 0.01


def element_stiffness():
    poisson = 0.3
    lame = poisson / ((1.0 + poisson) * (1.0 - 2.0 * poisson))
    shear = 0.5 / (1.0 + poisson)
    elastic = np.zeros((6, 6))
    elastic[:3, :3] = lame
    for index in range(3):
        elastic[index, index] += 2.0 * shear
        elastic[index + 3, index + 3] = shear
    points = [0.5 - 0.5 / math.sqrt(3.0), 0.5 + 0.5 / math.sqrt(3.0)]
    matrix = np.zeros((24, 24))
    for point_z in points:
        for point_y in points:
            for point_x in points:
                strain = np.zeros((6, 24))
                for corner_z in range(2):
                    for corner_y in range(2):
                        for corner_x in range(2):
                            node = 4 * corner_z + 2 * corner_y + corner_x
                            shape_x = point_x if corner_x else 1.0 - point_x
                            shape_y = point_y if corner_y else 1.0 - point_y
                            shape_z = point_z if corner_z else 1.0 - point_z
                            slope_x = 1.0 if corner_x else -1.0
                            slope_y = 1.0 if corner_y else -1.0
                            slope_z = 1.0 if corner_z else -1.0
                            along_x = slope_x * shape_y * shape_z
                            along_y = shape_x * slope_y * shape_z
                            along_z = shape_x * shape_y * slope_z
                            strain[0, node] = along_x
                            strain[1, 8 + node] = along_y
                            strain[2, 16 + node] = along_z
                            strain[3, node] = along_y
                            strain[3, 8 + node] = along_x
                            strain[4, 8 + node] = along_z
                            strain[4, 16 + node] = along_y
                            strain[5, node] = along_z
                            strain[5, 16 + node] = along_x
                matrix = matrix + strain.T @ elastic @ strain / 8.0
    return matrix


X, Y, Z, XY, XZ, YZ, XYZ = 1, 2, 4, 3, 5, 6, 7
U, V, W = 0, 1, 2
REDUCED = [
    [(U, X)], [(V, Y)], [(W, Z)],
    [(U, Y), (V, X)], [(U, Z), (W, X)], [(V, Z), (W, Y)],
    [(V, XY)], [(W, XZ)], [(U, XY)], [(W, YZ)], [(U, XZ)], [(V, YZ)],
    [(U, YZ)], [(V, XZ)], [(W, XY)],
    [(U, XYZ)], [(V, XYZ)], [(W, XYZ)],
]


def mode_constants(table):
    one = np.array([[1.0, 1.0], [-1.0, 1.0]])
    sums = np.kron(one, np.kron(one, one))
    change = np.kron(np.eye(3), sums)
    modes = change @ table @ change.T / 64.0
    at = lambda a, b: float(modes[a[0] * 8 + a[1], b[0] * 8 + b[1]])
    k = dict(
        cross=at((U, X), (V, Y)),
        shear=at((U, Y), (U, Y)),
        pair=at((V, XY), (W, XZ)),
        group=at((U, YZ), (V, XZ)),
        triple=at((U, XYZ), (U, XYZ)),
    )
    k["normal"] = at((U, X), (U, X)) - k["cross"]
    k["single"] = at((V, XY), (V, XY)) - k["pair"]
    reduce = np.zeros((18, 24))
    for row, members in enumerate(REDUCED):
        for component, bits in members:
            reduce[row, component * 8 + bits] = 1.0
    small = np.stack([np.array(stresses(list(unit), k)) for unit in np.eye(18)], axis=1)
    assert np.allclose(reduce.T @ small @ reduce, modes, atol=1e-12)
    assert np.allclose(np.diagonal(table), table[0, 0], atol=1e-12)
    return k


def stresses(m, k):
    trace = k["cross"] * (m[0] + m[1] + m[2])
    out = [trace + k["normal"] * m[i] for i in range(3)]
    out += [k["shear"] * m[i] for i in range(3, 6)]
    for i in (6, 8, 10):
        both = k["pair"] * (m[i] + m[i + 1])
        out += [both + k["single"] * m[i], both + k["single"] * m[i + 1]]
    total = m[12] + m[13] + m[14]
    out += [k["group"] * (total + m[i]) for i in range(12, 15)]
    out += [k["triple"] * m[i] for i in range(15, 18)]
    return out


def dotted(a, b):
    terms = [p * q for p, q in zip(a, b)]
    while len(terms) > 1:
        terms = [terms[i] + terms[i + 1] if i + 1 < len(terms) else terms[i] for i in range(0, len(terms), 2)]
    return terms[0]


def layer_modes(ref, index, row):
    found = []
    for component in range(3):
        low = ref[component, index, pl.ds(row, 8), :]
        high = ref[component, index, pl.ds(row + 1, 8), :]
        both, slope = low + high, high - low
        both_up, slope_up = (pltpu.roll(v, LANES - 1, 1) for v in (both, slope))
        found.append((both + both_up, slope + slope_up, both_up - both, slope_up - slope))
    return found


def voxel_modes(below, above):
    modes = {}
    for component in range(3):
        low, high = below[component], above[component]
        for bits in (X, Y, XY):
            modes[component, bits] = low[bits] + high[bits]
        for bits in (0, X, Y, XY):
            modes[component, bits + Z] = high[bits] - low[bits]
    reduced = []
    for members in REDUCED:
        value = modes[members[0]]
        for extra in members[1:]:
            value = value + modes[extra]
        reduced.append(value)
    return reduced


SLOT = {mode: row for row, members in enumerate(REDUCED) for mode in members}


def prepare_kernel(density, bone, fixed, load, fields, up, down):
    depth, height, width = density.shape
    zeros = jnp.zeros((LANES - height, width), jnp.float32)

    def layer(z, carry):
        thick = density[z]
        share = bone[z].astype(jnp.float32)
        free = 1.0 - fixed[z].astype(jnp.float32)
        modulus = share * thick * thick + (1.0 - share) * MARROW
        values = [modulus] + [free * load[c, z] for c in range(3)] + [free, thick]
        for slot, value in enumerate(values):
            square = jnp.concatenate([value, zeros], axis=0)
            fields[slot, z] = jnp.transpose(square)
        return carry

    lax.fori_loop(0, depth, layer, 0)

    def one(z):
        thick = density[z]
        share = bone[z].astype(jnp.float32)
        free = 1.0 - fixed[z].astype(jnp.float32)
        modulus = share * thick * thick + (1.0 - share) * MARROW
        return modulus, [free * load[c, z] for c in range(3)], free

    up[0] = one(depth - 2)[0]
    modulus, force, _ = one(depth - 1)
    up[1] = modulus
    for c in range(3):
        up[2 + c] = force[c]
    for z in range(2):
        modulus, force, free = one(z)
        down[z] = modulus
        for c in range(3):
            down[2 + 3 * z + c] = force[c]
        if z == 0:
            down[8] = free


def krylov_kernel(
    k, kappa,
    fields, up, down, left, right, left_up, right_up, left_down, right_down, weights, planes,
    out_p, out_w, out_g, out_stats,
    mod, force, free, search, inverse, lower, upper, image, stress, accumulate,
):
    depth, width = fields.shape[1], fields.shape[2]
    height = up.shape[1]
    first, last = PAD, PAD + width
    chunks = width // 8
    blank = jnp.zeros((LANES - height, width), jnp.float32)

    def turned(value):
        return jnp.transpose(jnp.concatenate([value, blank], axis=0))

    empty = jnp.zeros((PAD, LANES), jnp.float32)
    for ref in (mod, force, search):
        lead = ref.shape[:-2]
        for spot in np.ndindex(*lead):
            ref[spot + (pl.ds(0, PAD),)] = empty
            ref[spot + (pl.ds(last, PAD),)] = empty
            ref[spot + (pl.ds(last + PAD, PAD),)] = empty
    for z in range(depth + 1):
        free[z, pl.ds(last, PAD)] = empty

    def local(z, carry):
        for c in range(chunks):
            rows, into = pl.ds(8 * c, 8), pl.ds(first + 8 * c, 8)
            mod[z + 2, into] = fields[0, z, rows]
            for i in range(3):
                force[i, z + 1, into] = fields[1 + i, z, rows]
            free[z, into] = fields[4, z, rows]
        mod[z + 2, pl.ds(first - 2, 2)] = left[0, z]
        mod[z + 2, pl.ds(last, 2)] = right[0, z]
        for i in range(3):
            force[i, z + 1, pl.ds(first - 2, 2)] = left[1 + i, z]
            force[i, z + 1, pl.ds(last, 2)] = right[1 + i, z]
        free[z, pl.ds(last, 2)] = right[4, z]
        return carry

    lax.fori_loop(0, depth, local, 0)
    body = pl.ds(first, width)
    for z in range(2):
        mod[z, body] = turned(up[z])
        mod[depth + 2 + z, body] = turned(down[z])
        for side, low, high in ((first - 2, left_up, left_down), (last, right_up, right_down)):
            mod[z, pl.ds(side, 2)] = low[0, z]
            mod[depth + 2 + z, pl.ds(side, 2)] = high[0, z]
    for i in range(3):
        force[i, 0, body] = turned(up[2 + i])
        for side, low, high in ((first - 2, left_up, left_down), (last, right_up, right_down)):
            force[i, 0, pl.ds(side, 2)] = low[1 + i, 1]
            for z in range(2):
                force[i, depth + 1 + z, pl.ds(side, 2)] = high[1 + i, z]
        for z in range(2):
            force[i, depth + 1 + z, body] = turned(down[2 + 3 * z + i])
    free[depth, body] = turned(down[8])
    free[depth, pl.ds(last, 2)] = right_down[4, 0]

    def divide(chunk, carry):
        row = pl.multiple_of(chunk * 8, 8)
        previous = None
        for z in range(depth + 4):
            here = mod[z, pl.ds(row + PAD, 8)] + mod[z, pl.ds(row + PAD - 1, 8)]
            here = here + pltpu.roll(here, 1, 1)
            if z >= 1 and z <= depth + 3:
                total = kappa * (here + previous)
                share = jnp.where(total > 0.0, 1.0 / jnp.where(total > 0.0, total, 1.0), 0.0)
                node = z - 1
                for i in range(3):
                    search[i, node, pl.ds(row + PAD, 8)] = force[i, node, pl.ds(row + PAD, 8)] * share
                if 1 <= node <= depth + 1:
                    inverse[node - 1, pl.ds(row + PAD, 8)] = free[node - 1, pl.ds(row + PAD, 8)] * share
            previous = here
        return carry

    lax.fori_loop(0, chunks + 1, divide, 0)
    for z in range(depth + 3):
        side = mod[z, pl.ds(0, 8)]
        if z + 1 < depth + 4:
            total = side + mod[z + 1, pl.ds(0, 8)]
            total = total + pltpu.roll(total, 1, 0)
            total = kappa * (total + pltpu.roll(total, 1, 1))
            share = jnp.where(total > 0.0, 1.0 / jnp.where(total > 0.0, total, 1.0), 0.0)
            for i in range(3):
                search[i, z, pl.ds(0, 8)] = force[i, z, pl.ds(0, 8)] * share

    for s in range(accumulate.shape[0]):
        accumulate[s] = jnp.zeros((8, LANES), jnp.float32)

    def elements(row, inner):
        below = layer_modes(search, 0, row)
        carried = None
        for node in range(1, depth + 3):
            above = layer_modes(search, node, row)
            modes = voxel_modes(below, above)
            strain = stresses(modes, k)
            scale = mod[node, pl.ds(row, 8)]
            voxel = node - 2
            if inner is not None and 0 <= voxel < depth:
                rows = pl.ds(row - PAD, 8)
                work = (0.5 * scale) * dotted(modes, strain)
                out_g[0, voxel, rows] = work
                for s in range(18):
                    stress[s, voxel, rows] = strain[s]
            strain = [scale * s for s in strain]
            carry = []
            for component in range(3):
                value = lambda bits: strain[SLOT[component, bits]]
                totals, tops = [], []
                for bits in (0, X, Y, XY):
                    slope = value(bits + Z)
                    low, high = (-slope, slope) if bits == 0 else (value(bits) - slope, value(bits) + slope)
                    tops.append(high)
                    if carried is not None:
                        totals.append(low + carried[component][len(totals)])
                carry.append(tops)
                if carried is not None:
                    plain = (totals[0] - totals[2]) + pltpu.roll(totals[0] + totals[2], 1, 1)
                    tilted = (totals[1] - totals[3]) + pltpu.roll(totals[1] + totals[3], 1, 1)
                    lower[component, voxel, pl.ds(row, 8)] = plain - tilted
                    upper[component, voxel, pl.ds(row, 8)] = plain + tilted
            carried = carry
            below = above

    def middle(chunk, carry):
        elements(pl.multiple_of(PAD + chunk * 8, 8), True)
        return carry

    elements(0, None)
    lax.fori_loop(0, chunks, middle, 0)
    elements(last, None)

    def gather(chunk, carry):
        row = pl.multiple_of(PAD + chunk * 8, 8)
        rows = pl.ds(row, 8)
        gamma, second = jnp.zeros((8, LANES), jnp.float32), jnp.zeros((8, LANES), jnp.float32)
        for node in range(depth + 1):
            share = inverse[node, rows]
            for i in range(3):
                pulled = lower[i, node, rows] + upper[i, node, pl.ds(row - 1, 8)]
                scaled = share * pulled
                image[i, node, rows] = scaled
                if node < depth:
                    second = second + scaled * pulled
                    gamma = gamma + force[i, node + 1, rows] * search[i, node + 1, rows]
        accumulate[0] = accumulate[0] + jnp.where(chunk < chunks, gamma, 0.0)
        accumulate[2] = accumulate[2] + jnp.where(chunk < chunks, second, 0.0)
        return carry

    lax.fori_loop(0, chunks + 1, gather, 0)

    def energies(chunk, carry):
        row = pl.multiple_of(PAD + chunk * 8, 8)
        rows = pl.ds(pl.multiple_of(chunk * 8, 8), 8)
        weight = weights[rows]
        sums = [jnp.zeros((8, LANES), jnp.float32) for _ in range(5)]
        below = layer_modes(image, 0, row)
        for voxel in range(depth):
            above = layer_modes(image, voxel + 1, row)
            modes = voxel_modes(below, above)
            half = 0.5 * mod[voxel + 2, pl.ds(row, 8)]
            first_work = out_g[0, voxel, rows]
            mixed = half * dotted(modes, [stress[s, voxel, rows] for s in range(18)])
            second_work = half * dotted(modes, stresses(modes, k))
            thick = fields[5, voxel, rows]
            flip = jnp.where(thick > 0.0, 1.0 / jnp.where(thick > 0.0, thick, 1.0), 0.0)
            spread = weight * planes[voxel]
            sums[0] = sums[0] + first_work
            sums[1] = sums[1] + second_work
            for i, work in enumerate((first_work, mixed, second_work)):
                value = work * flip
                out_g[i, voxel, rows] = value
                sums[2 + i] = sums[2 + i] + spread * value
            below = above
            for i in range(3):
                out_p[i, voxel, rows] = search[i, voxel + 1, pl.ds(row, 8)]
                out_w[i, voxel, rows] = image[i, voxel, pl.ds(row, 8)]
        for slot, value in zip((1, 3, 4, 5, 6), sums):
            accumulate[slot] = accumulate[slot] + value
        return carry

    lax.fori_loop(0, chunks, energies, 0)
    for s in range(8):
        out_stats[pl.ds(s, 1)] = jnp.sum(accumulate[s], axis=0, keepdims=True)


def run_prepare(density, bone, fixed, load):
    depth, height, width = density.shape
    shapes = ((6, depth, width, LANES), (5, height, width), (9, height, width))
    return pl.pallas_call(
        prepare_kernel,
        out_shape=[jax.ShapeDtypeStruct(s, jnp.float32) for s in shapes],
        name="prepare",
    )(density, bone, fixed, load)


def run_krylov(table, fields, halos, weights, planes):
    depth, width = fields.shape[1], fields.shape[2]
    rows = width + 3 * PAD
    shapes = [(3, depth, width, LANES)] * 3 + [(8, LANES)]
    layers = [(depth + 4,), (3, depth + 3), (depth + 1,), (3, depth + 3), (depth + 1,)]
    layers += [(3, depth + 1)] * 3
    scratch = [pltpu.VMEM(lead + (rows, LANES), jnp.float32) for lead in layers]
    scratch += [
        pltpu.VMEM((18, depth, width, LANES), jnp.float32),
        pltpu.VMEM((8, 8, LANES), jnp.float32),
    ]
    return pl.pallas_call(
        functools.partial(krylov_kernel, mode_constants(table), float(table[0, 0])),
        out_shape=[jax.ShapeDtypeStruct(s, jnp.float32) for s in shapes],
        scratch_shapes=scratch,
        compiler_params=pltpu.CompilerParams(vmem_limit_bytes=56 * 1024 * 1024),
        name="krylov",
    )(fields, *halos, weights, planes)


def slab_route(steps, sideways=0):
    nx, ny, nz = (lax.axis_size(a) for a in ("gx", "gy", "gz"))
    pairs = []
    for x in range(nx):
        for slab in range(ny * nz):
            to, tx = slab + steps, x + sideways
            if 0 <= to < ny * nz and 0 <= tx < nx:
                spot = lambda i, s: (i * ny + s % ny) * nz + s // ny
                pairs.append((spot(x, slab), spot(tx, to)))
    return pairs


def to_slab(value, steps, sideways=0):
    return lax.ppermute(value, ("gx", "gy", "gz"), slab_route(steps, sideways))


def edges_swapped(low_edge, high_edge, steps):
    if lax.axis_size("gx") == 2:
        first = lax.axis_index("gx") == 0
        sent = jnp.where(first, high_edge, low_edge)
        spots = slab_route(steps, 1) + slab_route(steps, -1)
        got = lax.ppermute(sent, ("gx", "gy", "gz"), spots)
        none = jnp.zeros_like(got)
        return jnp.where(first, none, got), jnp.where(first, got, none)
    return to_slab(high_edge, steps, 1), to_slab(low_edge, steps, -1)


def total_over_mesh(value):
    for axis in ("gx", "gy", "gz"):
        count = lax.axis_size(axis)
        if count & (count - 1):
            value = lax.psum(value, axis)
            continue
        step = 1
        while step < count:
            other = lax.ppermute(value, axis, [(i, i ^ step) for i in range(count)])
            value = value + other
            step *= 2
    return value


def inner_sum(values):
    return total_over_mesh(jnp.full((8, LANES), jnp.sum(values)))[0, 0]


def tap_table():
    offsets = np.abs(np.arange(2 * RAD + 1) - RAD)
    raw = np.exp(-offsets / (0.5 * RAD))
    return raw / raw.sum()


def banded(length_in, length_out, shift):
    taps = tap_table()
    matrix = np.zeros((length_in, length_out))
    for i in range(length_in):
        for o in range(length_out):
            distance = i - shift - o
            if abs(distance) <= RAD:
                matrix[i, o] = taps[distance + RAD]
    return matrix.astype(np.float32)


def coverage(position, length):
    taps = tap_table()
    ends = jnp.asarray(np.concatenate([[0.0], np.cumsum(taps)]).astype(np.float32))
    low = jnp.maximum(-RAD, -position) + RAD
    high = jnp.minimum(RAD, length - 1 - position) + RAD + 1
    return ends[high] - ends[low]


def smooth_plane(fields, height):
    width = fields.shape[2]
    fields = fields[..., :height]
    from_left, from_right = edges_swapped(fields[:, :, :RAD], fields[:, :, width - RAD :], 0)
    wide = jnp.concatenate([from_left, fields, from_right], axis=2)
    along_x = jnp.asarray(banded(width + 2 * RAD, width, RAD))
    along_y = jnp.asarray(banded(height, height, 0))
    half = jnp.einsum("fzxy,xo->fzoy", wide, along_x, precision=lax.Precision.HIGHEST)
    return jnp.einsum("fzxy,yo->fzox", half, along_y, precision=lax.Precision.HIGHEST)


def smooth_depth(planar):
    depth = planar.shape[0]
    taps = tap_table()
    ratio = math.exp(-1.0 / (0.5 * RAD))
    pieces, blocks = [planar], [banded(depth, depth, 0)]
    decay = (ratio ** np.arange(depth)).astype(np.float64)
    low_plane = jnp.tensordot(jnp.asarray(decay.astype(np.float32)), planar, 1, precision=lax.Precision.HIGHEST)
    high_plane = jnp.tensordot(jnp.asarray(decay[::-1].astype(np.float32)), planar, 1, precision=lax.Precision.HIGHEST)
    steps = 1
    while (steps - 1) * depth + 1 <= RAD:
        if steps * depth + depth - 1 <= RAD:
            pieces.append(to_slab(high_plane, steps)[None])
            near = taps[RAD] * ratio ** (steps * depth - (depth - 1) + np.arange(depth))
            blocks.append(near[None])
            pieces.append(to_slab(low_plane, -steps)[None])
            near = taps[RAD] * ratio ** (steps * depth - np.arange(depth))
            blocks.append(near[None])
        else:
            pieces.append(to_slab(planar, steps))
            blocks.append(banded(depth, depth, steps * depth))
            pieces.append(to_slab(planar, -steps))
            blocks.append(banded(depth, depth, -steps * depth))
        steps += 1
    stacked = jnp.concatenate(pieces, axis=0)
    matrix = jnp.asarray(np.concatenate(blocks, axis=0).astype(np.float32))
    return jnp.einsum("iyx,io->oyx", stacked, matrix, precision=lax.Precision.HIGHEST)


def corners():
    return [(cz, cy, cx) for cz in range(2) for cy in range(2) for cx in range(2)]


def upper_nodes(field):
    column = lax.ppermute(field[:, :, :, :1], ("gx", "gy", "gz"), slab_route(0, -1))
    wide = jnp.concatenate([field, column], axis=3)
    wide = jnp.concatenate([wide, to_slab(wide[:, :1], -1)], axis=1)
    return jnp.pad(wide, ((0, 0), (0, 0), (0, 1), (0, 0)))


def fold_upper(values):
    depth, width = values.shape[1] - 1, values.shape[3] - 1
    carried = to_slab(values[:, depth:], 1)
    values = jnp.concatenate([values[:, :1] + carried, values[:, 1:depth]], axis=1)
    column = lax.ppermute(values[:, :, :, width:], ("gx", "gy", "gz"), slab_route(0, 1))
    return jnp.concatenate([values[:, :, :, :1] + column, values[:, :, :, 1:width]], axis=3)


def corner_columns(nodes, shape):
    depth, height, width = shape
    return jnp.stack(
        [
            nodes[c, cz : cz + depth, cy : cy + height, cx : cx + width]
            for c in range(3)
            for cz, cy, cx in corners()
        ]
    )


def element_products(columns, table):
    return jnp.einsum(
        "rc,czyx->rzyx", jnp.asarray(table, jnp.float32), columns, precision=lax.Precision.HIGHEST
    )


def plain_forces(field, modulus, table):
    depth, height, width = modulus.shape
    columns = corner_columns(upper_nodes(field), modulus.shape)
    products = element_products(columns, table) * modulus
    total = jnp.zeros((3, depth + 1, height + 1, width + 1), jnp.float32)
    for node, (cz, cy, cx) in enumerate(corners()):
        total = total.at[:, cz : cz + depth, cy : cy + height, cx : cx + width].add(products[node::8])
    return fold_upper(total[:, :, :height])


def plain_path(table, density, bone, fixed, load):
    depth, height, width = density.shape
    share = bone.astype(jnp.float32)
    free = 1.0 - fixed.astype(jnp.float32)
    modulus = share * density * density + (1.0 - share) * MARROW
    spread = jnp.zeros((1, depth + 1, height + 1, width + 1), jnp.float32)
    for cz, cy, cx in corners():
        spread = spread.at[0, cz : cz + depth, cy : cy + height, cx : cx + width].add(modulus)
    precondition = free / (float(table[0, 0]) * fold_upper(spread[:, :, :height]))
    residual = free * load
    solution = jnp.zeros_like(residual)
    search = precondition * residual
    gamma = inner_sum(residual * search)
    for count in range(ITERS):
        image = free * plain_forces(free * search, modulus, table)
        alpha = gamma / inner_sum(search * image)
        solution = solution + alpha * search
        if count + 1 < ITERS:
            residual = residual - alpha * image
            scaled = precondition * residual
            gamma_next = inner_sum(residual * scaled)
            search = scaled + gamma_next / gamma * search
            gamma = gamma_next
    columns = corner_columns(upper_nodes(solution), modulus.shape)
    energy = 0.5 * modulus * jnp.sum(columns * element_products(columns, table), axis=0)
    specific = jnp.swapaxes(energy / density, 1, 2)
    return smooth_plane(specific[None], height)[0], solution, specific


def on_device(density, bone, fixed, load):
    table = element_stiffness()
    density, bone, fixed, load = density[0], bone[0], fixed[0], load[:, 0]
    depth, height, width = density.shape
    slabs = lax.axis_size("gy") * lax.axis_size("gz")
    slab = lax.axis_index("gz") * lax.axis_size("gy") + lax.axis_index("gy")
    across = lax.axis_size("gx") * width
    cover_x = coverage(lax.axis_index("gx") * width + jnp.arange(width), across)
    cover_y = coverage(jnp.arange(height), height)
    cover_z = coverage(slab * depth + jnp.arange(depth), slabs * depth)
    weights = jnp.pad(cover_x[:, None] * cover_y[None], ((0, 0), (0, LANES - height)))
    planes = jnp.broadcast_to(cover_z[:, None, None], (depth, 8, LANES))

    fields, up, down = run_prepare(density, bone, fixed, load)
    got_up, got_down = to_slab(up, 1), to_slab(down, -1)
    low, high = fields[:5, :, :2], fields[:5, :, width - 2 :]
    left, right = edges_swapped(low, high, 0)
    left_up, right_up = edges_swapped(low[:, depth - 2 :], high[:, depth - 2 :], 1)
    left_down, right_down = edges_swapped(low[:, :2], high[:, :2], -1)
    halos = (got_up, got_down, left, right, left_up, right_up, left_down, right_down)
    first, second, basis, stats = run_krylov(table, fields, halos, weights, planes)

    sums = jnp.sum(total_over_mesh(stats), axis=1)
    gamma, curve, mixed, curve_second = sums[0], 2.0 * sums[1], sums[2], 2.0 * sums[3]
    smoothed = smooth_plane(basis, height)
    alpha = gamma / curve
    grown = alpha * mixed / curve
    beta = grown - 1.0
    bent = alpha * (alpha * (alpha * curve_second / gamma))
    rest = bent - grown * grown
    alpha_next = alpha * beta / rest
    by_first = alpha + alpha_next * grown
    by_second = -alpha_next * alpha
    squares = (by_first * by_first, 2.0 * by_first * by_second, by_second * by_second)
    parts = [f * s for f, s in zip(squares, (sums[4], sums[5], sums[6]))]
    total = parts[0] + parts[1] + parts[2]
    size = jnp.abs(parts[0]) + jnp.abs(parts[1]) + jnp.abs(parts[2])
    sound = (beta > GUARD * grown) & (rest > GUARD * bent) & (total > GUARD * size)

    def combined():
        planar = sum(f * s for f, s in zip(squares, smoothed))
        moved = by_first * first[..., :height] + by_second * second[..., :height]
        return planar, jnp.swapaxes(moved, 2, 3), total

    def repeated():
        planar, moved, specific = plain_path(table, density, bone, fixed, load)
        cover = weights[None, :, :height] * cover_z[:, None, None]
        return planar, moved, inner_sum(specific * cover)

    planar, solution, total = lax.cond(sound, combined, repeated)
    stimulus = smooth_depth(planar)
    mean = total / (density.size * lax.axis_size("gx") * slabs)
    share = bone.astype(jnp.float32)
    updated = density + REMODEL * share * (stimulus / (mean + EPSILON) - 1.0)
    updated = jnp.clip(updated, FLOOR, CEILING)
    return updated[None], solution[:, None]


def solution(mesh):
    placed = (
        P("gz", "gy", None, "gx"),
        P("gz", "gy", None, "gx"),
        P("gz", "gy", None, "gx"),
        P(None, "gz", "gy", None, "gx"),
    )
    return jax.shard_map(
        on_device,
        mesh=mesh,
        in_specs=placed,
        out_specs=(P("gz", "gy", None, "gx"), P(None, "gz", "gy", None, "gx")),
        check_vma=False,
    )
```

```python
import functools
import math

import jax
import jax.numpy as jnp
import numpy as np
from jax import lax
from jax.experimental import pallas as pl
from jax.experimental.pallas import tpu as pltpu
from jax.sharding import PartitionSpec as P


RAD = 24
ITERS = 2

MARROW = 0.1
REMODEL = 0.25
FLOOR = 0.2
CEILING = 1.0
EPSILON = 1e-06

LANES = 128
PAD = 8
GUARD = 0.01


def element_stiffness():
    poisson = 0.3
    lame = poisson / ((1.0 + poisson) * (1.0 - 2.0 * poisson))
    shear = 0.5 / (1.0 + poisson)
    elastic = np.zeros((6, 6))
    elastic[:3, :3] = lame
    for index in range(3):
        elastic[index, index] += 2.0 * shear
        elastic[index + 3, index + 3] = shear
    points = [0.5 - 0.5 / math.sqrt(3.0), 0.5 + 0.5 / math.sqrt(3.0)]
    matrix = np.zeros((24, 24))
    for point_z in points:
        for point_y in points:
            for point_x in points:
                strain = np.zeros((6, 24))
                for corner_z in range(2):
                    for corner_y in range(2):
                        for corner_x in range(2):
                            node = 4 * corner_z + 2 * corner_y + corner_x
                            shape_x = point_x if corner_x else 1.0 - point_x
                            shape_y = point_y if corner_y else 1.0 - point_y
                            shape_z = point_z if corner_z else 1.0 - point_z
                            slope_x = 1.0 if corner_x else -1.0
                            slope_y = 1.0 if corner_y else -1.0
                            slope_z = 1.0 if corner_z else -1.0
                            along_x = slope_x * shape_y * shape_z
                            along_y = shape_x * slope_y * shape_z
                            along_z = shape_x * shape_y * slope_z
                            strain[0, node] = along_x
                            strain[1, 8 + node] = along_y
                            strain[2, 16 + node] = along_z
                            strain[3, node] = along_y
                            strain[3, 8 + node] = along_x
                            strain[4, 8 + node] = along_z
                            strain[4, 16 + node] = along_y
                            strain[5, node] = along_z
                            strain[5, 16 + node] = along_x
                matrix = matrix + strain.T @ elastic @ strain / 8.0
    return matrix


X, Y, Z, XY, XZ, YZ, XYZ = 1, 2, 4, 3, 5, 6, 7
U, V, W = 0, 1, 2
REDUCED = [
    [(U, X)], [(V, Y)], [(W, Z)],
    [(U, Y), (V, X)], [(U, Z), (W, X)], [(V, Z), (W, Y)],
    [(V, XY)], [(W, XZ)], [(U, XY)], [(W, YZ)], [(U, XZ)], [(V, YZ)],
    [(U, YZ)], [(V, XZ)], [(W, XY)],
    [(U, XYZ)], [(V, XYZ)], [(W, XYZ)],
]


def mode_constants(table):
    one = np.array([[1.0, 1.0], [-1.0, 1.0]])
    sums = np.kron(one, np.kron(one, one))
    change = np.kron(np.eye(3), sums)
    modes = change @ table @ change.T / 64.0
    at = lambda a, b: float(modes[a[0] * 8 + a[1], b[0] * 8 + b[1]])
    k = dict(
        cross=at((U, X), (V, Y)),
        shear=at((U, Y), (U, Y)),
        pair=at((V, XY), (W, XZ)),
        group=at((U, YZ), (V, XZ)),
        triple=at((U, XYZ), (U, XYZ)),
    )
    k["normal"] = at((U, X), (U, X)) - k["cross"]
    k["single"] = at((V, XY), (V, XY)) - k["pair"]
    reduce = np.zeros((18, 24))
    for row, members in enumerate(REDUCED):
        for component, bits in members:
            reduce[row, component * 8 + bits] = 1.0
    small = np.stack([np.array(stresses(list(unit), k)) for unit in np.eye(18)], axis=1)
    assert np.allclose(reduce.T @ small @ reduce, modes, atol=1e-12)
    assert np.allclose(np.diagonal(table), table[0, 0], atol=1e-12)
    return k


def stresses(m, k):
    trace = k["cross"] * (m[0] + m[1] + m[2])
    out = [trace + k["normal"] * m[i] for i in range(3)]
    out += [k["shear"] * m[i] for i in range(3, 6)]
    for i in (6, 8, 10):
        both = k["pair"] * (m[i] + m[i + 1])
        out += [both + k["single"] * m[i], both + k["single"] * m[i + 1]]
    total = m[12] + m[13] + m[14]
    out += [k["group"] * (total + m[i]) for i in range(12, 15)]
    out += [k["triple"] * m[i] for i in range(15, 18)]
    return out


def dotted(a, b):
    terms = [p * q for p, q in zip(a, b)]
    while len(terms) > 1:
        terms = [terms[i] + terms[i + 1] if i + 1 < len(terms) else terms[i] for i in range(0, len(terms), 2)]
    return terms[0]


def layer_modes(ref, index, row):
    found = []
    for component in range(3):
        low = ref[component, index, pl.ds(row, 8), :]
        high = ref[component, index, pl.ds(row + 1, 8), :]
        both, slope = low + high, high - low
        both_up, slope_up = (pltpu.roll(v, LANES - 1, 1) for v in (both, slope))
        found.append((both + both_up, slope + slope_up, both_up - both, slope_up - slope))
    return found


def voxel_modes(below, above):
    modes = {}
    for component in range(3):
        low, high = below[component], above[component]
        for bits in (X, Y, XY):
            modes[component, bits] = low[bits] + high[bits]
        for bits in (0, X, Y, XY):
            modes[component, bits + Z] = high[bits] - low[bits]
    reduced = []
    for members in REDUCED:
        value = modes[members[0]]
        for extra in members[1:]:
            value = value + modes[extra]
        reduced.append(value)
    return reduced


SLOT = {mode: row for row, members in enumerate(REDUCED) for mode in members}


def raw_layer(density, bone, fixed, load, z):
    thick = density[z]
    share = bone[z].astype(jnp.float32)
    free = 1.0 - fixed[z].astype(jnp.float32)
    modulus = share * thick * thick + (1.0 - share) * MARROW
    return modulus, [free * load[c, z] for c in range(3)], free, thick


def message_kernel(density, bone, fixed, load, up, down):
    depth = density.shape[0]
    raw = (density, bone, fixed, load)
    up[0] = raw_layer(*raw, depth - 2)[0]
    modulus, force, _, _ = raw_layer(*raw, depth - 1)
    up[1] = modulus
    for c in range(3):
        up[2 + c] = force[c]
    for z in range(2):
        modulus, force, free, _ = raw_layer(*raw, z)
        down[z] = modulus
        for c in range(3):
            down[2 + 3 * z + c] = force[c]
        if z == 0:
            down[8] = free


def prepare_kernel(density, bone, fixed, load, fields):
    depth, height, width = density.shape
    zeros = jnp.zeros((LANES - height, width), jnp.float32)

    def layer(z, carry):
        modulus, force, free, thick = raw_layer(density, bone, fixed, load, z)
        for slot, value in enumerate([modulus] + force + [free, thick]):
            square = jnp.concatenate([value, zeros], axis=0)
            fields[slot, z] = jnp.transpose(square)
        return carry

    lax.fori_loop(0, depth, layer, 0)


def krylov_kernel(
    k, kappa,
    fields, up, down, left, right, left_up, right_up, left_down, right_down, weights, planes,
    out_p, out_w, out_g, out_stats,
    mod, force, free, search, inverse, lower, upper, image, stress, accumulate,
):
    depth, width = fields.shape[1], fields.shape[2]
    height = up.shape[1]
    first, last = PAD, PAD + width
    chunks = width // 8
    blank = jnp.zeros((LANES - height, width), jnp.float32)

    def turned(value):
        return jnp.transpose(jnp.concatenate([value, blank], axis=0))

    empty = jnp.zeros((PAD, LANES), jnp.float32)
    for ref in (mod, force, search):
        lead = ref.shape[:-2]
        for spot in np.ndindex(*lead):
            ref[spot + (pl.ds(0, PAD),)] = empty
            ref[spot + (pl.ds(last, PAD),)] = empty
            ref[spot + (pl.ds(last + PAD, PAD),)] = empty
    for z in range(depth + 1):
        free[z, pl.ds(last, PAD)] = empty

    def local(z, carry):
        for c in range(chunks):
            rows, into = pl.ds(8 * c, 8), pl.ds(first + 8 * c, 8)
            mod[z + 2, into] = fields[0, z, rows]
            for i in range(3):
                force[i, z + 1, into] = fields[1 + i, z, rows]
            free[z, into] = fields[4, z, rows]
        mod[z + 2, pl.ds(first - 2, 2)] = left[0, z]
        mod[z + 2, pl.ds(last, 2)] = right[0, z]
        for i in range(3):
            force[i, z + 1, pl.ds(first - 2, 2)] = left[1 + i, z]
            force[i, z + 1, pl.ds(last, 2)] = right[1 + i, z]
        free[z, pl.ds(last, 2)] = right[4, z]
        return carry

    lax.fori_loop(0, depth, local, 0)
    body = pl.ds(first, width)
    for z in range(2):
        mod[z, body] = turned(up[z])
        mod[depth + 2 + z, body] = turned(down[z])
        for side, low, high in ((first - 2, left_up, left_down), (last, right_up, right_down)):
            mod[z, pl.ds(side, 2)] = low[0, z]
            mod[depth + 2 + z, pl.ds(side, 2)] = high[0, z]
    for i in range(3):
        force[i, 0, body] = turned(up[2 + i])
        for side, low, high in ((first - 2, left_up, left_down), (last, right_up, right_down)):
            force[i, 0, pl.ds(side, 2)] = low[1 + i, 1]
            for z in range(2):
                force[i, depth + 1 + z, pl.ds(side, 2)] = high[1 + i, z]
        for z in range(2):
            force[i, depth + 1 + z, body] = turned(down[2 + 3 * z + i])
    free[depth, body] = turned(down[8])
    free[depth, pl.ds(last, 2)] = right_down[4, 0]

    def divide(chunk, carry):
        row = pl.multiple_of(chunk * 8, 8)
        previous = None
        for z in range(depth + 4):
            here = mod[z, pl.ds(row + PAD, 8)] + mod[z, pl.ds(row + PAD - 1, 8)]
            here = here + pltpu.roll(here, 1, 1)
            if z >= 1 and z <= depth + 3:
                total = kappa * (here + previous)
                share = jnp.where(total > 0.0, 1.0 / jnp.where(total > 0.0, total, 1.0), 0.0)
                node = z - 1
                for i in range(3):
                    search[i, node, pl.ds(row + PAD, 8)] = force[i, node, pl.ds(row + PAD, 8)] * share
                if 1 <= node <= depth + 1:
                    inverse[node - 1, pl.ds(row + PAD, 8)] = free[node - 1, pl.ds(row + PAD, 8)] * share
            previous = here
        return carry

    lax.fori_loop(0, chunks + 1, divide, 0)
    for z in range(depth + 3):
        side = mod[z, pl.ds(0, 8)]
        if z + 1 < depth + 4:
            total = side + mod[z + 1, pl.ds(0, 8)]
            total = total + pltpu.roll(total, 1, 0)
            total = kappa * (total + pltpu.roll(total, 1, 1))
            share = jnp.where(total > 0.0, 1.0 / jnp.where(total > 0.0, total, 1.0), 0.0)
            for i in range(3):
                search[i, z, pl.ds(0, 8)] = force[i, z, pl.ds(0, 8)] * share

    for s in range(accumulate.shape[0]):
        accumulate[s] = jnp.zeros((8, LANES), jnp.float32)

    def elements(row, inner):
        below = layer_modes(search, 0, row)
        carried = None
        for node in range(1, depth + 3):
            above = layer_modes(search, node, row)
            modes = voxel_modes(below, above)
            strain = stresses(modes, k)
            scale = mod[node, pl.ds(row, 8)]
            voxel = node - 2
            if inner is not None and 0 <= voxel < depth:
                rows = pl.ds(row - PAD, 8)
                work = (0.5 * scale) * dotted(modes, strain)
                out_g[0, voxel, rows] = work
                for s in range(18):
                    stress[s, voxel, rows] = strain[s]
            strain = [scale * s for s in strain]
            carry = []
            for component in range(3):
                value = lambda bits: strain[SLOT[component, bits]]
                totals, tops = [], []
                for bits in (0, X, Y, XY):
                    slope = value(bits + Z)
                    low, high = (-slope, slope) if bits == 0 else (value(bits) - slope, value(bits) + slope)
                    tops.append(high)
                    if carried is not None:
                        totals.append(low + carried[component][len(totals)])
                carry.append(tops)
                if carried is not None:
                    plain = (totals[0] - totals[2]) + pltpu.roll(totals[0] + totals[2], 1, 1)
                    tilted = (totals[1] - totals[3]) + pltpu.roll(totals[1] + totals[3], 1, 1)
                    lower[component, voxel, pl.ds(row, 8)] = plain - tilted
                    upper[component, voxel, pl.ds(row, 8)] = plain + tilted
            carried = carry
            below = above

    def middle(chunk, carry):
        elements(pl.multiple_of(PAD + chunk * 8, 8), True)
        return carry

    elements(0, None)
    lax.fori_loop(0, chunks, middle, 0)
    elements(last, None)

    def gather(chunk, carry):
        row = pl.multiple_of(PAD + chunk * 8, 8)
        rows = pl.ds(row, 8)
        gamma, second = jnp.zeros((8, LANES), jnp.float32), jnp.zeros((8, LANES), jnp.float32)
        for node in range(depth + 1):
            share = inverse[node, rows]
            for i in range(3):
                pulled = lower[i, node, rows] + upper[i, node, pl.ds(row - 1, 8)]
                scaled = share * pulled
                image[i, node, rows] = scaled
                if node < depth:
                    second = second + scaled * pulled
                    gamma = gamma + force[i, node + 1, rows] * search[i, node + 1, rows]
        accumulate[0] = accumulate[0] + jnp.where(chunk < chunks, gamma, 0.0)
        accumulate[2] = accumulate[2] + jnp.where(chunk < chunks, second, 0.0)
        return carry

    lax.fori_loop(0, chunks + 1, gather, 0)

    def energies(chunk, carry):
        row = pl.multiple_of(PAD + chunk * 8, 8)
        rows = pl.ds(pl.multiple_of(chunk * 8, 8), 8)
        weight = weights[rows]
        sums = [jnp.zeros((8, LANES), jnp.float32) for _ in range(5)]
        below = layer_modes(image, 0, row)
        for voxel in range(depth):
            above = layer_modes(image, voxel + 1, row)
            modes = voxel_modes(below, above)
            half = 0.5 * mod[voxel + 2, pl.ds(row, 8)]
            first_work = out_g[0, voxel, rows]
            mixed = half * dotted(modes, [stress[s, voxel, rows] for s in range(18)])
            second_work = half * dotted(modes, stresses(modes, k))
            thick = fields[5, voxel, rows]
            flip = jnp.where(thick > 0.0, 1.0 / jnp.where(thick > 0.0, thick, 1.0), 0.0)
            spread = weight * planes[voxel]
            sums[0] = sums[0] + first_work
            sums[1] = sums[1] + second_work
            for i, work in enumerate((first_work, mixed, second_work)):
                value = work * flip
                out_g[i, voxel, rows] = value
                sums[2 + i] = sums[2 + i] + spread * value
            below = above
            for i in range(3):
                out_p[i, voxel, rows] = search[i, voxel + 1, pl.ds(row, 8)]
                out_w[i, voxel, rows] = image[i, voxel, pl.ds(row, 8)]
        for slot, value in zip((1, 3, 4, 5, 6), sums):
            accumulate[slot] = accumulate[slot] + value
        return carry

    lax.fori_loop(0, chunks, energies, 0)
    for s in range(8):
        out_stats[pl.ds(s, 1)] = jnp.sum(accumulate[s], axis=0, keepdims=True)


def run_messages(density, bone, fixed, load):
    _, height, width = density.shape
    return pl.pallas_call(
        message_kernel,
        out_shape=[jax.ShapeDtypeStruct((n, height, width), jnp.float32) for n in (5, 9)],
        name="messages",
    )(density, bone, fixed, load)


def run_prepare(density, bone, fixed, load):
    depth, _, width = density.shape
    return pl.pallas_call(
        prepare_kernel,
        out_shape=jax.ShapeDtypeStruct((6, depth, width, LANES), jnp.float32),
        name="prepare",
    )(density, bone, fixed, load)


def run_krylov(table, fields, halos, weights, planes):
    depth, width = fields.shape[1], fields.shape[2]
    rows = width + 3 * PAD
    shapes = [(3, depth, width, LANES)] * 3 + [(8, LANES)]
    layers = [(depth + 4,), (3, depth + 3), (depth + 1,), (3, depth + 3), (depth + 1,)]
    layers += [(3, depth + 1)] * 3
    scratch = [pltpu.VMEM(lead + (rows, LANES), jnp.float32) for lead in layers]
    scratch += [
        pltpu.VMEM((18, depth, width, LANES), jnp.float32),
        pltpu.VMEM((8, 8, LANES), jnp.float32),
    ]
    return pl.pallas_call(
        functools.partial(krylov_kernel, mode_constants(table), float(table[0, 0])),
        out_shape=[jax.ShapeDtypeStruct(s, jnp.float32) for s in shapes],
        scratch_shapes=scratch,
        compiler_params=pltpu.CompilerParams(vmem_limit_bytes=56 * 1024 * 1024),
        name="krylov",
    )(fields, *halos, weights, planes)


def slab_route(steps, sideways=0):
    nx, ny, nz = (lax.axis_size(a) for a in ("gx", "gy", "gz"))
    pairs = []
    for x in range(nx):
        for slab in range(ny * nz):
            to, tx = slab + steps, x + sideways
            if 0 <= to < ny * nz and 0 <= tx < nx:
                spot = lambda i, s: (i * ny + s % ny) * nz + s // ny
                pairs.append((spot(x, slab), spot(tx, to)))
    return pairs


def to_slab(value, steps, sideways=0):
    return lax.ppermute(value, ("gx", "gy", "gz"), slab_route(steps, sideways))


def edges_swapped(low_edge, high_edge, steps):
    if lax.axis_size("gx") == 2:
        first = lax.axis_index("gx") == 0
        sent = jnp.where(first, high_edge, low_edge)
        spots = slab_route(steps, 1) + slab_route(steps, -1)
        got = lax.ppermute(sent, ("gx", "gy", "gz"), spots)
        none = jnp.zeros_like(got)
        return jnp.where(first, none, got), jnp.where(first, got, none)
    return to_slab(high_edge, steps, 1), to_slab(low_edge, steps, -1)


def total_over_mesh(value):
    for axis in ("gx", "gy", "gz"):
        count = lax.axis_size(axis)
        if count & (count - 1):
            value = lax.psum(value, axis)
            continue
        step = 1
        while step < count:
            other = lax.ppermute(value, axis, [(i, i ^ step) for i in range(count)])
            value = value + other
            step *= 2
    return value


def inner_sum(values):
    return total_over_mesh(jnp.full((8, LANES), jnp.sum(values)))[0, 0]


def tap_table():
    offsets = np.abs(np.arange(2 * RAD + 1) - RAD)
    raw = np.exp(-offsets / (0.5 * RAD))
    return raw / raw.sum()


def banded(length_in, length_out, shift):
    taps = tap_table()
    matrix = np.zeros((length_in, length_out))
    for i in range(length_in):
        for o in range(length_out):
            distance = i - shift - o
            if abs(distance) <= RAD:
                matrix[i, o] = taps[distance + RAD]
    return matrix.astype(np.float32)


def coverage(length):
    ends = np.concatenate([[0.0], np.cumsum(tap_table())])
    position = np.arange(length)
    low = np.maximum(-RAD, -position) + RAD
    high = np.minimum(RAD, length - 1 - position) + RAD + 1
    return (ends[high] - ends[low]).astype(np.float32)


def depth_pieces(planar, low_plane, high_plane):
    depth = planar.shape[0]
    taps = tap_table()
    ratio = math.exp(-1.0 / (0.5 * RAD))
    pieces, blocks = [planar], [banded(depth, depth, 0)]
    near, far = [], []
    steps = 1
    while (steps - 1) * depth + 1 <= RAD:
        if steps * depth + depth - 1 <= RAD:
            away = steps * depth + np.arange(depth)
            near.append((high_plane, steps, taps[RAD] * ratio ** (away - (depth - 1))))
            away = steps * depth - np.arange(depth)
            near.append((low_plane, -steps, taps[RAD] * ratio ** away))
        else:
            far.append((steps, banded(depth, depth, steps * depth)))
            far.append((-steps, banded(depth, depth, -steps * depth)))
        steps += 1
    for move, block in far:
        pieces.append(to_slab(planar, move))
        blocks.append(block)
    for plane, move, weight in near:
        pieces.append(to_slab(plane, move)[None])
        blocks.append(weight[None].astype(np.float32))
    return pieces, blocks


def depth_decay(depth):
    return (math.exp(-1.0 / (0.5 * RAD)) ** np.arange(depth)).astype(np.float32)


def krylov_coefficients(sums):
    gamma, curve, mixed, curve_second = sums[0], 2.0 * sums[1], sums[2], 2.0 * sums[3]
    alpha = gamma / curve
    grown = alpha * mixed / curve
    beta = grown - 1.0
    bent = alpha * (alpha * (alpha * curve_second / gamma))
    rest = bent - grown * grown
    alpha_next = alpha * beta / rest
    by_first = alpha + alpha_next * grown
    by_second = -alpha_next * alpha
    squares = [by_first * by_first, 2.0 * by_first * by_second, by_second * by_second]
    parts = [f * s for f, s in zip(squares, sums[4:7])]
    total = parts[0] + parts[1] + parts[2]
    size = jnp.abs(parts[0]) + jnp.abs(parts[1]) + jnp.abs(parts[2])
    sound = (beta > GUARD * grown) & (rest > GUARD * bent) & (total > GUARD * size)
    return by_first, by_second, squares, total, jnp.where(sound, 1.0, 0.0)


def smooth_kernel(plain, cells, stats, basis, left, right, along_x, along_y, planar, low, high, factors):
    depth = basis.shape[1]
    decay = depth_decay(depth)
    exact = dict(precision=lax.Precision.HIGHEST, preferred_element_type=jnp.float32)
    tile = stats[...]
    sums = [jnp.sum(tile[i : i + 1], axis=1, keepdims=True) for i in range(8)]
    if plain:
        one = jnp.ones((1, 1), jnp.float32)
        by_first, by_second, squares, total, sound = one, one, [one], sums[4], one
    else:
        by_first, by_second, squares, total, sound = krylov_coefficients(sums)
    scale = 1.0 / (total / cells + EPSILON)
    for i, value in enumerate((by_first, by_second, scale, sound)):
        factors[pl.ds(i, 1)] = jnp.broadcast_to(value, (1, LANES))
    factors[pl.ds(4, 4)] = jnp.zeros((4, LANES), jnp.float32)
    for z in range(depth):
        wide = jnp.concatenate(
            [sum(f * v[i, z] for i, f in enumerate(squares)) for v in (left, basis, right)], axis=0
        )
        half = lax.dot_general(along_x[...], wide, (((1,), (0,)), ((), ())), **exact)
        plane = lax.dot_general(along_y[...], half, (((1,), (1,)), ((), ())), **exact)
        planar[z] = plane
        for ref, weight in ((low, decay[z]), (high, decay[depth - 1 - z])):
            share = plane * float(weight)
            ref[...] = share if z == 0 else ref[...] + share


def run_smooth(plain, cells, stats, basis, sides, height):
    depth, width = basis.shape[1:3]
    along_x = banded(width + 2 * RAD, width, RAD).T
    along_y = np.zeros((height, LANES), np.float32)
    along_y[:, :height] = banded(height, height, 0).T
    shapes = ((depth, height, width), (height, width), (height, width), (8, LANES))
    return pl.pallas_call(
        functools.partial(smooth_kernel, plain, float(cells)),
        out_shape=[jax.ShapeDtypeStruct(s, jnp.float32) for s in shapes],
        name="smooth",
    )(stats, basis, *sides, jnp.asarray(along_x), jnp.asarray(along_y))


def finish_kernel(blocks, factors, density, bone, *rest):
    pieces, out = rest[:-1], rest[-1]
    depth, height, _ = density.shape

    scale = factors[pl.ds(2, 1)]

    def chunk(index, carry):
        rows = pl.ds(pl.multiple_of(index * 8, 8), 8)
        totals = [None] * depth
        for piece, block in zip(pieces, blocks):
            for i in range(block.shape[0]):
                value = piece[i, rows]
                for o in range(depth):
                    if block[i, o] != 0.0:
                        term = value * float(block[i, o])
                        totals[o] = term if totals[o] is None else totals[o] + term
        for o in range(depth):
            share = REMODEL * bone[o, rows].astype(jnp.float32)
            moved = density[o, rows] + share * (totals[o] * scale - 1.0)
            out[o, rows] = jnp.clip(moved, FLOOR, CEILING)
        return carry

    lax.fori_loop(0, height // 8, chunk, 0)


def run_finish(factors, density, bone, pieces, blocks):
    return pl.pallas_call(
        functools.partial(finish_kernel, blocks),
        out_shape=jax.ShapeDtypeStruct(density.shape, jnp.float32),
        name="finish",
    )(factors, density, bone, *pieces)


def displacement_kernel(height, factors, first, second, out):
    by_first, by_second = factors[pl.ds(0, 1)], factors[pl.ds(1, 1)]

    def layer(z, carry):
        for i in range(3):
            moved = by_first * first[i, z] + by_second * second[i, z]
            out[i, z] = jnp.transpose(moved)[:height]
        return carry

    lax.fori_loop(0, first.shape[1], layer, 0)


def run_displacement(factors, first, second, height):
    depth, width = first.shape[1:3]
    return pl.pallas_call(
        functools.partial(displacement_kernel, height),
        out_shape=jax.ShapeDtypeStruct((3, depth, height, width), jnp.float32),
        name="displacement",
    )(factors, first, second)


def corners():
    return [(cz, cy, cx) for cz in range(2) for cy in range(2) for cx in range(2)]


def upper_nodes(field):
    column = lax.ppermute(field[:, :, :, :1], ("gx", "gy", "gz"), slab_route(0, -1))
    wide = jnp.concatenate([field, column], axis=3)
    wide = jnp.concatenate([wide, to_slab(wide[:, :1], -1)], axis=1)
    return jnp.pad(wide, ((0, 0), (0, 0), (0, 1), (0, 0)))


def fold_upper(values):
    depth, width = values.shape[1] - 1, values.shape[3] - 1
    carried = to_slab(values[:, depth:], 1)
    values = jnp.concatenate([values[:, :1] + carried, values[:, 1:depth]], axis=1)
    column = lax.ppermute(values[:, :, :, width:], ("gx", "gy", "gz"), slab_route(0, 1))
    return jnp.concatenate([values[:, :, :, :1] + column, values[:, :, :, 1:width]], axis=3)


def corner_columns(nodes, shape):
    depth, height, width = shape
    return jnp.stack(
        [
            nodes[c, cz : cz + depth, cy : cy + height, cx : cx + width]
            for c in range(3)
            for cz, cy, cx in corners()
        ]
    )


def element_products(columns, table):
    return jnp.einsum(
        "rc,czyx->rzyx", jnp.asarray(table, jnp.float32), columns, precision=lax.Precision.HIGHEST
    )


def spread_corner(values, corner):
    return jnp.pad(values, ((0, 0),) + tuple((c, 1 - c) for c in corner))


def plain_forces(field, modulus, table):
    _, height, _ = modulus.shape
    columns = corner_columns(upper_nodes(field), modulus.shape)
    products = element_products(columns, table) * modulus
    products = products.reshape((3, 8) + modulus.shape)
    total = sum(spread_corner(products[:, node], corner) for node, corner in enumerate(corners()))
    return fold_upper(total[:, :, :height])


def plain_path(table, density, bone, fixed, load):
    _, height, _ = density.shape
    share = bone.astype(jnp.float32)
    free = 1.0 - fixed.astype(jnp.float32)
    modulus = share * density * density + (1.0 - share) * MARROW
    spread = sum(spread_corner(modulus[None], corner) for corner in corners())
    precondition = free / (float(table[0, 0]) * fold_upper(spread[:, :, :height]))
    residual = free * load
    search = precondition * residual
    start = (jnp.zeros_like(residual), residual, search, inner_sum(residual * search))

    def iterate(_, state):
        moved, residual, search, gamma = state
        image = free * plain_forces(free * search, modulus, table)
        alpha = gamma / inner_sum(search * image)
        moved = moved + alpha * search
        residual = residual - alpha * image
        scaled = precondition * residual
        gamma_next = inner_sum(residual * scaled)
        return moved, residual, scaled + gamma_next / gamma * search, gamma_next

    moved = lax.fori_loop(0, ITERS, iterate, start)[0]
    columns = corner_columns(upper_nodes(moved), modulus.shape)
    energy = 0.5 * modulus * jnp.sum(columns * element_products(columns, table), axis=0)
    specific = jnp.swapaxes(energy / density, 1, 2)
    return jnp.pad(specific, ((0, 0), (0, 0), (0, LANES - height))), moved


def side_halos(basis):
    width = basis.shape[2]
    return edges_swapped(basis[:, :, :RAD], basis[:, :, width - RAD :], 0)


def remodelled(plain, cells, density, bone, stats, basis, sides):
    planar, low, high, factors = run_smooth(plain, cells, stats, basis, sides, density.shape[1])
    pieces, blocks = depth_pieces(planar, low, high)
    return run_finish(factors, density, bone, pieces, blocks), factors


def on_device(density, bone, fixed, load):
    table = element_stiffness()
    density, bone, fixed, load = density[0], bone[0], fixed[0], load[:, 0]
    depth, height, width = density.shape
    slabs = lax.axis_size("gy") * lax.axis_size("gz")
    slab = lax.axis_index("gz") * lax.axis_size("gy") + lax.axis_index("gy")
    across = lax.axis_size("gx") * width
    cells = density.size * lax.axis_size("gx") * slabs
    cover_x = lax.dynamic_slice(jnp.asarray(coverage(across)), (lax.axis_index("gx") * width,), (width,))
    cover_y = jnp.asarray(np.pad(coverage(height), (0, LANES - height)))
    cover_z = lax.dynamic_slice(jnp.asarray(coverage(slabs * depth)), (slab * depth,), (depth,))
    weights = cover_x[:, None] * cover_y[None]
    planes = jnp.broadcast_to(cover_z[:, None, None], (depth, 8, LANES))

    up, down = run_messages(density, bone, fixed, load)
    got_up = to_slab(up, 1)
    got_down = to_slab(down, -1)
    fields = run_prepare(density, bone, fixed, load)
    low, high = fields[:5, :, :2], fields[:5, :, width - 2 :]
    left, right = edges_swapped(low, high, 0)
    left_up, right_up = edges_swapped(low[:, depth - 2 :], high[:, depth - 2 :], 1)
    left_down, right_down = edges_swapped(low[:, :2], high[:, :2], -1)
    halos = (got_up, got_down, left, right, left_up, right_up, left_down, right_down)
    first, second, basis, stats = run_krylov(table, fields, halos, weights, planes)
    sides = side_halos(basis)
    stats = total_over_mesh(stats)
    updated, factors = remodelled(False, cells, density, bone, stats, basis, sides)
    moved = run_displacement(factors, first, second, height)

    def repeated(state):
        specific, moved = plain_path(table, density, bone, fixed, load)
        total = inner_sum(specific * weights[None] * cover_z[:, None, None])
        row, lane = (lax.broadcasted_iota(jnp.int32, (8, LANES), i) for i in range(2))
        tile = jnp.where((row == 4) & (lane == 0), total, 0.0)
        again = specific[None]
        updated = remodelled(True, cells, density, bone, tile, again, side_halos(again))[0]
        return True, updated, moved.reshape(-1, width)

    sound = factors[3, 0] > 0.5
    _, updated, moved = lax.while_loop(lambda state: ~state[0], repeated, (sound, updated, moved.reshape(-1, width)))
    return updated[None], moved.reshape(3, 1, depth, height, width)


def solution(mesh):
    placed = (
        P("gz", "gy", None, "gx"),
        P("gz", "gy", None, "gx"),
        P("gz", "gy", None, "gx"),
        P(None, "gz", "gy", None, "gx"),
    )
    return jax.shard_map(
        on_device,
        mesh=mesh,
        in_specs=placed,
        out_specs=(P("gz", "gy", None, "gx"), P(None, "gz", "gy", None, "gx")),
        check_vma=False,
    )
```

```python
import functools
import math

import jax
import jax.numpy as jnp
import numpy as np
from jax import lax
from jax.experimental import pallas as pl
from jax.experimental.pallas import tpu as pltpu
from jax.sharding import PartitionSpec as P


RAD = 24
ITERS = 2

MARROW = 0.1
REMODEL = 0.25
FLOOR = 0.2
CEILING = 1.0
EPSILON = 1e-06

LANES = 128
PAD = 8
GUARD = 0.01


def element_stiffness():
    poisson = 0.3
    lame = poisson / ((1.0 + poisson) * (1.0 - 2.0 * poisson))
    shear = 0.5 / (1.0 + poisson)
    elastic = np.zeros((6, 6))
    elastic[:3, :3] = lame
    for index in range(3):
        elastic[index, index] += 2.0 * shear
        elastic[index + 3, index + 3] = shear
    points = [0.5 - 0.5 / math.sqrt(3.0), 0.5 + 0.5 / math.sqrt(3.0)]
    matrix = np.zeros((24, 24))
    for point_z in points:
        for point_y in points:
            for point_x in points:
                strain = np.zeros((6, 24))
                for corner_z in range(2):
                    for corner_y in range(2):
                        for corner_x in range(2):
                            node = 4 * corner_z + 2 * corner_y + corner_x
                            shape_x = point_x if corner_x else 1.0 - point_x
                            shape_y = point_y if corner_y else 1.0 - point_y
                            shape_z = point_z if corner_z else 1.0 - point_z
                            slope_x = 1.0 if corner_x else -1.0
                            slope_y = 1.0 if corner_y else -1.0
                            slope_z = 1.0 if corner_z else -1.0
                            along_x = slope_x * shape_y * shape_z
                            along_y = shape_x * slope_y * shape_z
                            along_z = shape_x * shape_y * slope_z
                            strain[0, node] = along_x
                            strain[1, 8 + node] = along_y
                            strain[2, 16 + node] = along_z
                            strain[3, node] = along_y
                            strain[3, 8 + node] = along_x
                            strain[4, 8 + node] = along_z
                            strain[4, 16 + node] = along_y
                            strain[5, node] = along_z
                            strain[5, 16 + node] = along_x
                matrix = matrix + strain.T @ elastic @ strain / 8.0
    return matrix


X, Y, Z, XY, XZ, YZ, XYZ = 1, 2, 4, 3, 5, 6, 7
U, V, W = 0, 1, 2
REDUCED = [
    [(U, X)], [(V, Y)], [(W, Z)],
    [(U, Y), (V, X)], [(U, Z), (W, X)], [(V, Z), (W, Y)],
    [(V, XY)], [(W, XZ)], [(U, XY)], [(W, YZ)], [(U, XZ)], [(V, YZ)],
    [(U, YZ)], [(V, XZ)], [(W, XY)],
    [(U, XYZ)], [(V, XYZ)], [(W, XYZ)],
]


def mode_constants(table):
    one = np.array([[1.0, 1.0], [-1.0, 1.0]])
    sums = np.kron(one, np.kron(one, one))
    change = np.kron(np.eye(3), sums)
    modes = change @ table @ change.T / 64.0
    at = lambda a, b: float(modes[a[0] * 8 + a[1], b[0] * 8 + b[1]])
    k = dict(
        cross=at((U, X), (V, Y)),
        shear=at((U, Y), (U, Y)),
        pair=at((V, XY), (W, XZ)),
        group=at((U, YZ), (V, XZ)),
        triple=at((U, XYZ), (U, XYZ)),
    )
    k["normal"] = at((U, X), (U, X)) - k["cross"]
    k["single"] = at((V, XY), (V, XY)) - k["pair"]
    reduce = np.zeros((18, 24))
    for row, members in enumerate(REDUCED):
        for component, bits in members:
            reduce[row, component * 8 + bits] = 1.0
    small = np.stack([np.array(stresses(list(unit), k)) for unit in np.eye(18)], axis=1)
    assert np.allclose(reduce.T @ small @ reduce, modes, atol=1e-12)
    assert np.allclose(np.diagonal(table), table[0, 0], atol=1e-12)
    return k


def stresses(m, k):
    trace = k["cross"] * (m[0] + m[1] + m[2])
    out = [trace + k["normal"] * m[i] for i in range(3)]
    out += [k["shear"] * m[i] for i in range(3, 6)]
    for i in (6, 8, 10):
        both = k["pair"] * (m[i] + m[i + 1])
        out += [both + k["single"] * m[i], both + k["single"] * m[i + 1]]
    total = m[12] + m[13] + m[14]
    out += [k["group"] * (total + m[i]) for i in range(12, 15)]
    out += [k["triple"] * m[i] for i in range(15, 18)]
    return out


def dotted(a, b):
    terms = [p * q for p, q in zip(a, b)]
    while len(terms) > 1:
        terms = [terms[i] + terms[i + 1] if i + 1 < len(terms) else terms[i] for i in range(0, len(terms), 2)]
    return terms[0]


def layer_modes(ref, index, row):
    found = []
    for component in range(3):
        low = ref[component, index, pl.ds(row, 8), :]
        high = ref[component, index, pl.ds(row + 1, 8), :]
        both, slope = low + high, high - low
        both_up, slope_up = (pltpu.roll(v, LANES - 1, 1) for v in (both, slope))
        found.append((both + both_up, slope + slope_up, both_up - both, slope_up - slope))
    return found


def voxel_modes(below, above):
    modes = {}
    for component in range(3):
        low, high = below[component], above[component]
        for bits in (X, Y, XY):
            modes[component, bits] = low[bits] + high[bits]
        for bits in (0, X, Y, XY):
            modes[component, bits + Z] = high[bits] - low[bits]
    reduced = []
    for members in REDUCED:
        value = modes[members[0]]
        for extra in members[1:]:
            value = value + modes[extra]
        reduced.append(value)
    return reduced


SLOT = {mode: row for row, members in enumerate(REDUCED) for mode in members}


def raw_layer(density, bone, fixed, load, z):
    thick = density[z]
    share = bone[z].astype(jnp.float32)
    free = 1.0 - fixed[z].astype(jnp.float32)
    modulus = share * thick * thick + (1.0 - share) * MARROW
    return modulus, [free * load[c, z] for c in range(3)], free, thick


def message_kernel(*refs):
    lowest, highest, (up, down) = refs[:8:2], refs[1:8:2], refs[8:]
    up[0] = raw_layer(*highest, 0)[0]
    modulus, force, _, _ = raw_layer(*highest, 1)
    up[1] = modulus
    for c in range(3):
        up[2 + c] = force[c]
    for z in range(2):
        modulus, force, free, _ = raw_layer(*lowest, z)
        down[z] = modulus
        for c in range(3):
            down[2 + 3 * z + c] = force[c]
        if z == 0:
            down[8] = free


def prepare_kernel(swap, place, density, bone, fixed, load, fields, *edges):
    depth, height, width = density.shape
    zeros = jnp.zeros((LANES - height, width), jnp.float32)
    first = place[0] == 0
    kinds = len(edges) // 3
    for z in range(depth):
        modulus, force, free, thick = raw_layer(density, bone, fixed, load, z)
        for slot, value in enumerate([modulus] + force + [free, thick]):
            turned = jnp.transpose(jnp.concatenate([value, zeros], axis=0))
            fields[slot, z] = turned
            if slot == 5:
                continue
            low, high = turned[:2], turned[width - 2 :]
            sent = (jnp.where(first, high, low),) if swap else (low, high)
            for kind in range(kinds):
                edges[kind][slot, z] = sent[kind]
                if z >= depth - 2:
                    edges[kinds + kind][slot, z - (depth - 2)] = sent[kind]
                if z < 2:
                    edges[2 * kinds + kind][slot, z] = sent[kind]


def krylov_kernel(
    k, kappa, across,
    place, cover_z, fields, up, down, left, right, left_up, right_up, left_down, right_down,
    cover_x, cover_y,
    *rest,
):
    out_p, out_w, out_g, out_stats = rest[:4]
    out_edges, rest = rest[4:-10], rest[-10:]
    mod, force, free, search, inverse, lower, upper, image, stress, accumulate = rest
    on_left = jnp.where(place[0] > 0, 1.0, 0.0)
    on_right = jnp.where(place[0] < across - 1, 1.0, 0.0)
    depth, width = fields.shape[1], fields.shape[2]
    height = up.shape[1]
    first, last = PAD, PAD + width
    chunks = width // 8
    blank = jnp.zeros((LANES - height, width), jnp.float32)

    def turned(value):
        return jnp.transpose(jnp.concatenate([value, blank], axis=0))

    empty = jnp.zeros((PAD, LANES), jnp.float32)
    for ref in (mod, force, search):
        lead = ref.shape[:-2]
        for spot in np.ndindex(*lead):
            ref[spot + (pl.ds(0, PAD),)] = empty
            ref[spot + (pl.ds(last, PAD),)] = empty
            ref[spot + (pl.ds(last + PAD, PAD),)] = empty
    for z in range(depth + 1):
        free[z, pl.ds(last, PAD)] = empty

    def local(z, carry):
        for c in range(chunks):
            rows, into = pl.ds(8 * c, 8), pl.ds(first + 8 * c, 8)
            mod[z + 2, into] = fields[0, z, rows]
            for i in range(3):
                force[i, z + 1, into] = fields[1 + i, z, rows]
            free[z, into] = fields[4, z, rows]
        mod[z + 2, pl.ds(first - 2, 2)] = left[0, z] * on_left
        mod[z + 2, pl.ds(last, 2)] = right[0, z] * on_right
        for i in range(3):
            force[i, z + 1, pl.ds(first - 2, 2)] = left[1 + i, z] * on_left
            force[i, z + 1, pl.ds(last, 2)] = right[1 + i, z] * on_right
        free[z, pl.ds(last, 2)] = right[4, z] * on_right
        return carry

    lax.fori_loop(0, depth, local, 0)
    body = pl.ds(first, width)
    for z in range(2):
        mod[z, body] = turned(up[z])
        mod[depth + 2 + z, body] = turned(down[z])
        for side, low, high, there in (
            (first - 2, left_up, left_down, on_left),
            (last, right_up, right_down, on_right),
        ):
            mod[z, pl.ds(side, 2)] = low[0, z] * there
            mod[depth + 2 + z, pl.ds(side, 2)] = high[0, z] * there
    for i in range(3):
        force[i, 0, body] = turned(up[2 + i])
        for side, low, high, there in (
            (first - 2, left_up, left_down, on_left),
            (last, right_up, right_down, on_right),
        ):
            force[i, 0, pl.ds(side, 2)] = low[1 + i, 1] * there
            for z in range(2):
                force[i, depth + 1 + z, pl.ds(side, 2)] = high[1 + i, z] * there
        for z in range(2):
            force[i, depth + 1 + z, body] = turned(down[2 + 3 * z + i])
    free[depth, body] = turned(down[8])
    free[depth, pl.ds(last, 2)] = right_down[4, 0] * on_right

    def divide(chunk, carry):
        row = pl.multiple_of(chunk * 8, 8)
        previous = None
        for z in range(depth + 4):
            here = mod[z, pl.ds(row + PAD, 8)] + mod[z, pl.ds(row + PAD - 1, 8)]
            here = here + pltpu.roll(here, 1, 1)
            if z >= 1 and z <= depth + 3:
                total = kappa * (here + previous)
                share = jnp.where(total > 0.0, 1.0 / jnp.where(total > 0.0, total, 1.0), 0.0)
                node = z - 1
                for i in range(3):
                    search[i, node, pl.ds(row + PAD, 8)] = force[i, node, pl.ds(row + PAD, 8)] * share
                if 1 <= node <= depth + 1:
                    inverse[node - 1, pl.ds(row + PAD, 8)] = free[node - 1, pl.ds(row + PAD, 8)] * share
            previous = here
        return carry

    lax.fori_loop(0, chunks + 1, divide, 0)
    for z in range(depth + 3):
        side = mod[z, pl.ds(0, 8)]
        if z + 1 < depth + 4:
            total = side + mod[z + 1, pl.ds(0, 8)]
            total = total + pltpu.roll(total, 1, 0)
            total = kappa * (total + pltpu.roll(total, 1, 1))
            share = jnp.where(total > 0.0, 1.0 / jnp.where(total > 0.0, total, 1.0), 0.0)
            for i in range(3):
                search[i, z, pl.ds(0, 8)] = force[i, z, pl.ds(0, 8)] * share

    for s in range(accumulate.shape[0]):
        accumulate[s] = jnp.zeros((8, LANES), jnp.float32)

    def elements(row, inner):
        below = layer_modes(search, 0, row)
        carried = None
        for node in range(1, depth + 3):
            above = layer_modes(search, node, row)
            modes = voxel_modes(below, above)
            strain = stresses(modes, k)
            scale = mod[node, pl.ds(row, 8)]
            voxel = node - 2
            if inner is not None and 0 <= voxel < depth:
                rows = pl.ds(row - PAD, 8)
                work = (0.5 * scale) * dotted(modes, strain)
                out_g[0, voxel, rows] = work
                for s in range(18):
                    stress[s, voxel, rows] = strain[s]
            strain = [scale * s for s in strain]
            carry = []
            for component in range(3):
                value = lambda bits: strain[SLOT[component, bits]]
                totals, tops = [], []
                for bits in (0, X, Y, XY):
                    slope = value(bits + Z)
                    low, high = (-slope, slope) if bits == 0 else (value(bits) - slope, value(bits) + slope)
                    tops.append(high)
                    if carried is not None:
                        totals.append(low + carried[component][len(totals)])
                carry.append(tops)
                if carried is not None:
                    plain = (totals[0] - totals[2]) + pltpu.roll(totals[0] + totals[2], 1, 1)
                    tilted = (totals[1] - totals[3]) + pltpu.roll(totals[1] + totals[3], 1, 1)
                    lower[component, voxel, pl.ds(row, 8)] = plain - tilted
                    upper[component, voxel, pl.ds(row, 8)] = plain + tilted
            carried = carry
            below = above

    def middle(chunk, carry):
        elements(pl.multiple_of(PAD + chunk * 8, 8), True)
        return carry

    elements(0, None)
    lax.fori_loop(0, chunks, middle, 0)
    elements(last, None)

    def gather(chunk, carry):
        row = pl.multiple_of(PAD + chunk * 8, 8)
        rows = pl.ds(row, 8)
        gamma, second = jnp.zeros((8, LANES), jnp.float32), jnp.zeros((8, LANES), jnp.float32)
        for node in range(depth + 1):
            share = inverse[node, rows]
            for i in range(3):
                pulled = lower[i, node, rows] + upper[i, node, pl.ds(row - 1, 8)]
                scaled = share * pulled
                image[i, node, rows] = scaled
                if node < depth:
                    second = second + scaled * pulled
                    gamma = gamma + force[i, node + 1, rows] * search[i, node + 1, rows]
        accumulate[0] = accumulate[0] + jnp.where(chunk < chunks, gamma, 0.0)
        accumulate[2] = accumulate[2] + jnp.where(chunk < chunks, second, 0.0)
        return carry

    lax.fori_loop(0, chunks + 1, gather, 0)

    def energies(chunk, carry):
        row = pl.multiple_of(PAD + chunk * 8, 8)
        rows = pl.ds(pl.multiple_of(chunk * 8, 8), 8)
        across_rows = pl.ds(pl.multiple_of(place[0] * width + chunk * 8, 8), 8)
        weight = cover_x[across_rows] * cover_y[...]
        sums = [jnp.zeros((8, LANES), jnp.float32) for _ in range(5)]
        below = layer_modes(image, 0, row)
        for voxel in range(depth):
            above = layer_modes(image, voxel + 1, row)
            modes = voxel_modes(below, above)
            half = 0.5 * mod[voxel + 2, pl.ds(row, 8)]
            first_work = out_g[0, voxel, rows]
            mixed = half * dotted(modes, [stress[s, voxel, rows] for s in range(18)])
            second_work = half * dotted(modes, stresses(modes, k))
            thick = fields[5, voxel, rows]
            flip = jnp.where(thick > 0.0, 1.0 / jnp.where(thick > 0.0, thick, 1.0), 0.0)
            spread = weight * cover_z[place[1] * depth + voxel]
            sums[0] = sums[0] + first_work
            sums[1] = sums[1] + second_work
            for i, work in enumerate((first_work, mixed, second_work)):
                value = work * flip
                out_g[i, voxel, rows] = value
                sums[2 + i] = sums[2 + i] + spread * value
            below = above
            for i in range(3):
                out_p[i, voxel, rows] = search[i, voxel + 1, pl.ds(row, 8)]
                out_w[i, voxel, rows] = image[i, voxel, pl.ds(row, 8)]
        for slot, value in zip((1, 3, 4, 5, 6), sums):
            accumulate[slot] = accumulate[slot] + value
        return carry

    lax.fori_loop(0, chunks, energies, 0)
    for i in range(3):
        for z in range(depth):
            low, high = out_g[i, z, pl.ds(0, RAD)], out_g[i, z, pl.ds(width - RAD, RAD)]
            sent = (jnp.where(place[0] == 0, high, low),) if len(out_edges) == 1 else (low, high)
            for ref, value in zip(out_edges, sent):
                ref[i, z] = value
    for s in range(8):
        out_stats[pl.ds(s, 1)] = jnp.sum(accumulate[s], axis=0, keepdims=True)


def run_messages(density, bone, fixed, load):
    depth, height, width = density.shape
    specs, arrays = [], []
    for array in (density, bone, fixed, load):
        lead = array.shape[:-3]
        for block in (0, depth // 2 - 1):
            spot = lambda _, block=block, lead=lead: (0,) * len(lead) + (block, 0, 0)
            specs.append(pl.BlockSpec(lead + (2, height, width), spot))
            arrays.append(array)
    return pl.pallas_call(
        message_kernel,
        grid=(1,),
        in_specs=specs,
        out_specs=[pl.BlockSpec((n, height, width), lambda _: (0, 0, 0)) for n in (5, 9)],
        out_shape=[jax.ShapeDtypeStruct((n, height, width), jnp.float32) for n in (5, 9)],
        name="messages",
    )(*arrays)


SCALAR = pl.BlockSpec(memory_space=pltpu.SMEM)
VECTOR = pl.BlockSpec(memory_space=pltpu.VMEM)


def run_prepare(place, density, bone, fixed, load):
    depth, _, width = density.shape
    swap = lax.axis_size("gx") == 2
    shapes = [(6, depth, width, LANES)]
    for layers in (depth, 2, 2):
        shapes += [(5, layers, 2, LANES)] * (1 if swap else 2)
    fields, *edges = pl.pallas_call(
        functools.partial(prepare_kernel, swap),
        in_specs=[SCALAR] + [VECTOR] * 4,
        out_specs=[VECTOR] * len(shapes),
        out_shape=[jax.ShapeDtypeStruct(s, jnp.float32) for s in shapes],
        name="prepare",
    )(place, density, bone, fixed, load)
    kinds = len(edges) // 3
    return fields, [edges[i * kinds : (i + 1) * kinds] for i in range(3)]


def run_krylov(table, place, fields, halos):
    depth, width = fields.shape[1], fields.shape[2]
    height = halos[0].shape[1]
    nx = lax.axis_size("gx")
    slabs = lax.axis_size("gy") * lax.axis_size("gz")
    rows = width + 3 * PAD
    shapes = [(3, depth, width, LANES)] * 3 + [(8, LANES)]
    shapes += [(3, depth, RAD, LANES)] * (1 if nx == 2 else 2)
    layers = [(depth + 4,), (3, depth + 3), (depth + 1,), (3, depth + 3), (depth + 1,)]
    layers += [(3, depth + 1)] * 3
    scratch = [pltpu.VMEM(lead + (rows, LANES), jnp.float32) for lead in layers]
    scratch += [
        pltpu.VMEM((18, depth, width, LANES), jnp.float32),
        pltpu.VMEM((8, 8, LANES), jnp.float32),
    ]
    cover_x = coverage(nx * width)[:, None]
    cover_y = np.pad(coverage(height), (0, LANES - height))[None]
    return pl.pallas_call(
        functools.partial(krylov_kernel, mode_constants(table), float(table[0, 0]), nx),
        in_specs=[SCALAR] * 2 + [VECTOR] * (len(halos) + 3),
        out_specs=[VECTOR] * len(shapes),
        out_shape=[jax.ShapeDtypeStruct(s, jnp.float32) for s in shapes],
        scratch_shapes=scratch,
        compiler_params=pltpu.CompilerParams(vmem_limit_bytes=56 * 1024 * 1024),
        name="krylov",
    )(place, jnp.asarray(coverage(slabs * depth)), fields, *halos, jnp.asarray(cover_x), jnp.asarray(cover_y))


def slab_route(steps, sideways=0):
    nx, ny, nz = (lax.axis_size(a) for a in ("gx", "gy", "gz"))
    pairs = []
    for x in range(nx):
        for slab in range(ny * nz):
            to, tx = slab + steps, x + sideways
            if 0 <= to < ny * nz and 0 <= tx < nx:
                spot = lambda i, s: (i * ny + s % ny) * nz + s // ny
                pairs.append((spot(x, slab), spot(tx, to)))
    return pairs


def to_slab(value, steps, sideways=0):
    return lax.ppermute(value, ("gx", "gy", "gz"), slab_route(steps, sideways))


def edges_swapped(low_edge, high_edge, steps):
    if lax.axis_size("gx") == 2:
        first = lax.axis_index("gx") == 0
        sent = jnp.where(first, high_edge, low_edge)
        spots = slab_route(steps, 1) + slab_route(steps, -1)
        got = lax.ppermute(sent, ("gx", "gy", "gz"), spots)
        none = jnp.zeros_like(got)
        return jnp.where(first, none, got), jnp.where(first, got, none)
    return to_slab(high_edge, steps, 1), to_slab(low_edge, steps, -1)


def edges_moved(sent, steps):
    if len(sent) == 1:
        spots = slab_route(steps, 1) + slab_route(steps, -1)
        got = lax.ppermute(sent[0], ("gx", "gy", "gz"), spots)
        return got, got
    return to_slab(sent[1], steps, 1), to_slab(sent[0], steps, -1)


def total_over_mesh(value):
    for axis in ("gx", "gy", "gz"):
        count = lax.axis_size(axis)
        if count & (count - 1):
            value = lax.psum(value, axis)
            continue
        step = 1
        while step < count:
            other = lax.ppermute(value, axis, [(i, i ^ step) for i in range(count)])
            value = value + other
            step *= 2
    return value


def inner_sum(values):
    return total_over_mesh(jnp.full((8, LANES), jnp.sum(values)))[0, 0]


def tap_table():
    offsets = np.abs(np.arange(2 * RAD + 1) - RAD)
    raw = np.exp(-offsets / (0.5 * RAD))
    return raw / raw.sum()


def banded(length_in, length_out, shift):
    taps = tap_table()
    matrix = np.zeros((length_in, length_out))
    for i in range(length_in):
        for o in range(length_out):
            distance = i - shift - o
            if abs(distance) <= RAD:
                matrix[i, o] = taps[distance + RAD]
    return matrix.astype(np.float32)


def coverage(length):
    ends = np.concatenate([[0.0], np.cumsum(tap_table())])
    position = np.arange(length)
    low = np.maximum(-RAD, -position) + RAD
    high = np.minimum(RAD, length - 1 - position) + RAD + 1
    return (ends[high] - ends[low]).astype(np.float32)


def depth_pieces(planar, low_plane, high_plane):
    depth = planar.shape[0]
    taps = tap_table()
    ratio = math.exp(-1.0 / (0.5 * RAD))
    pieces, blocks = [planar], [banded(depth, depth, 0)]
    near, far = [], []
    steps = 1
    while (steps - 1) * depth + 1 <= RAD:
        if steps * depth + depth - 1 <= RAD:
            away = steps * depth + np.arange(depth)
            near.append((high_plane, steps, taps[RAD] * ratio ** (away - (depth - 1))))
            away = steps * depth - np.arange(depth)
            near.append((low_plane, -steps, taps[RAD] * ratio ** away))
        else:
            far.append((steps, banded(depth, depth, steps * depth)))
            far.append((-steps, banded(depth, depth, -steps * depth)))
        steps += 1
    for move, block in far:
        pieces.append(to_slab(planar, move))
        blocks.append(block)
    for plane, move, weight in near:
        pieces.append(to_slab(plane, move)[None])
        blocks.append(weight[None].astype(np.float32))
    return pieces, blocks


def depth_decay(depth):
    return (math.exp(-1.0 / (0.5 * RAD)) ** np.arange(depth)).astype(np.float32)


def krylov_coefficients(sums):
    gamma, curve, mixed, curve_second = sums[0], 2.0 * sums[1], sums[2], 2.0 * sums[3]
    alpha = gamma / curve
    grown = alpha * mixed / curve
    beta = grown - 1.0
    bent = alpha * (alpha * (alpha * curve_second / gamma))
    rest = bent - grown * grown
    alpha_next = alpha * beta / rest
    by_first = alpha + alpha_next * grown
    by_second = -alpha_next * alpha
    squares = [by_first * by_first, 2.0 * by_first * by_second, by_second * by_second]
    parts = [f * s for f, s in zip(squares, sums[4:7])]
    total = parts[0] + parts[1] + parts[2]
    size = jnp.abs(parts[0]) + jnp.abs(parts[1]) + jnp.abs(parts[2])
    sound = (beta > GUARD * grown) & (rest > GUARD * bent) & (total > GUARD * size)
    return by_first, by_second, squares, total, jnp.where(sound, 1.0, 0.0)


def smooth_kernel(
    plain, cells, nx, place, stats, basis, left, right, along_x, along_y, planar, low, high, factors
):
    on_left = jnp.where(place[0] > 0, 1.0, 0.0)
    on_right = jnp.where(place[0] < nx - 1, 1.0, 0.0)
    depth = basis.shape[1]
    decay = depth_decay(depth)
    exact = dict(precision=lax.Precision.HIGHEST, preferred_element_type=jnp.float32)
    tile = stats[...]
    sums = [jnp.sum(tile[i : i + 1], axis=1, keepdims=True) for i in range(8)]
    if plain:
        one = jnp.ones((1, 1), jnp.float32)
        by_first, by_second, squares, total, sound = one, one, [one], sums[4], one
    else:
        by_first, by_second, squares, total, sound = krylov_coefficients(sums)
    scale = 1.0 / (total / cells + EPSILON)
    for i, value in enumerate((by_first, by_second, scale, sound)):
        factors[pl.ds(i, 1)] = jnp.broadcast_to(value, (1, LANES))
    factors[pl.ds(4, 4)] = jnp.zeros((4, LANES), jnp.float32)
    for z in range(depth):
        wide = jnp.concatenate(
            [
                there * sum(f * v[i, z] for i, f in enumerate(squares))
                for v, there in ((left, on_left), (basis, 1.0), (right, on_right))
            ],
            axis=0,
        )
        half = lax.dot_general(along_x[...], wide, (((1,), (0,)), ((), ())), **exact)
        plane = lax.dot_general(along_y[...], half, (((1,), (1,)), ((), ())), **exact)
        planar[z] = plane
        for ref, weight in ((low, decay[z]), (high, decay[depth - 1 - z])):
            share = plane * float(weight)
            ref[...] = share if z == 0 else ref[...] + share


def run_smooth(plain, cells, place, stats, basis, sides, height):
    depth, width = basis.shape[1:3]
    along_x = banded(width + 2 * RAD, width, RAD).T
    along_y = np.zeros((height, LANES), np.float32)
    along_y[:, :height] = banded(height, height, 0).T
    shapes = ((depth, height, width), (height, width), (height, width), (8, LANES))
    return pl.pallas_call(
        functools.partial(smooth_kernel, plain, float(cells), lax.axis_size("gx")),
        in_specs=[SCALAR] + [VECTOR] * 6,
        out_specs=[VECTOR] * 4,
        out_shape=[jax.ShapeDtypeStruct(s, jnp.float32) for s in shapes],
        name="smooth",
    )(place, stats, basis, *sides, jnp.asarray(along_x), jnp.asarray(along_y))


def finish_kernel(blocks, factors, density, bone, *rest):
    pieces, out = rest[:-1], rest[-1]
    depth, height, _ = density.shape

    scale = factors[pl.ds(2, 1)]

    def chunk(index, carry):
        rows = pl.ds(pl.multiple_of(index * 8, 8), 8)
        totals = [None] * depth
        for piece, block in zip(pieces, blocks):
            for i in range(block.shape[0]):
                value = piece[i, rows]
                for o in range(depth):
                    if block[i, o] != 0.0:
                        term = value * float(block[i, o])
                        totals[o] = term if totals[o] is None else totals[o] + term
        for o in range(depth):
            share = REMODEL * bone[o, rows].astype(jnp.float32)
            moved = density[o, rows] + share * (totals[o] * scale - 1.0)
            out[o, rows] = jnp.clip(moved, FLOOR, CEILING)
        return carry

    lax.fori_loop(0, height // 8, chunk, 0)


def run_finish(factors, density, bone, pieces, blocks):
    return pl.pallas_call(
        functools.partial(finish_kernel, blocks),
        out_shape=jax.ShapeDtypeStruct(density.shape, jnp.float32),
        name="finish",
    )(factors, density, bone, *pieces)


def displacement_kernel(height, factors, first, second, out):
    by_first, by_second = factors[pl.ds(0, 1)], factors[pl.ds(1, 1)]

    def layer(z, carry):
        for i in range(3):
            moved = by_first * first[i, z] + by_second * second[i, z]
            out[i, z] = jnp.transpose(moved)[:height]
        return carry

    lax.fori_loop(0, first.shape[1], layer, 0)


def run_displacement(factors, first, second, height):
    depth, width = first.shape[1:3]
    return pl.pallas_call(
        functools.partial(displacement_kernel, height),
        out_shape=jax.ShapeDtypeStruct((3, depth, height, width), jnp.float32),
        name="displacement",
    )(factors, first, second)


def corners():
    return [(cz, cy, cx) for cz in range(2) for cy in range(2) for cx in range(2)]


def upper_nodes(field):
    column = lax.ppermute(field[:, :, :, :1], ("gx", "gy", "gz"), slab_route(0, -1))
    wide = jnp.concatenate([field, column], axis=3)
    wide = jnp.concatenate([wide, to_slab(wide[:, :1], -1)], axis=1)
    return jnp.pad(wide, ((0, 0), (0, 0), (0, 1), (0, 0)))


def fold_upper(values):
    depth, width = values.shape[1] - 1, values.shape[3] - 1
    carried = to_slab(values[:, depth:], 1)
    values = jnp.concatenate([values[:, :1] + carried, values[:, 1:depth]], axis=1)
    column = lax.ppermute(values[:, :, :, width:], ("gx", "gy", "gz"), slab_route(0, 1))
    return jnp.concatenate([values[:, :, :, :1] + column, values[:, :, :, 1:width]], axis=3)


def corner_columns(nodes, shape):
    depth, height, width = shape
    return jnp.stack(
        [
            nodes[c, cz : cz + depth, cy : cy + height, cx : cx + width]
            for c in range(3)
            for cz, cy, cx in corners()
        ]
    )


def element_products(columns, table):
    return jnp.einsum(
        "rc,czyx->rzyx", jnp.asarray(table, jnp.float32), columns, precision=lax.Precision.HIGHEST
    )


def spread_corner(values, corner):
    return jnp.pad(values, ((0, 0),) + tuple((c, 1 - c) for c in corner))


def plain_forces(field, modulus, table):
    _, height, _ = modulus.shape
    columns = corner_columns(upper_nodes(field), modulus.shape)
    products = element_products(columns, table) * modulus
    products = products.reshape((3, 8) + modulus.shape)
    total = sum(spread_corner(products[:, node], corner) for node, corner in enumerate(corners()))
    return fold_upper(total[:, :, :height])


def plain_path(table, density, bone, fixed, load):
    _, height, _ = density.shape
    share = bone.astype(jnp.float32)
    free = 1.0 - fixed.astype(jnp.float32)
    modulus = share * density * density + (1.0 - share) * MARROW
    spread = sum(spread_corner(modulus[None], corner) for corner in corners())
    precondition = free / (float(table[0, 0]) * fold_upper(spread[:, :, :height]))
    residual = free * load
    search = precondition * residual
    start = (jnp.zeros_like(residual), residual, search, inner_sum(residual * search))

    def iterate(_, state):
        moved, residual, search, gamma = state
        image = free * plain_forces(free * search, modulus, table)
        alpha = gamma / inner_sum(search * image)
        moved = moved + alpha * search
        residual = residual - alpha * image
        scaled = precondition * residual
        gamma_next = inner_sum(residual * scaled)
        return moved, residual, scaled + gamma_next / gamma * search, gamma_next

    moved = lax.fori_loop(0, ITERS, iterate, start)[0]
    columns = corner_columns(upper_nodes(moved), modulus.shape)
    energy = 0.5 * modulus * jnp.sum(columns * element_products(columns, table), axis=0)
    specific = jnp.swapaxes(energy / density, 1, 2)
    return jnp.pad(specific, ((0, 0), (0, 0), (0, LANES - height))), moved


def side_halos(basis):
    width = basis.shape[2]
    return edges_swapped(basis[:, :, :RAD], basis[:, :, width - RAD :], 0)


def remodelled(plain, cells, place, density, bone, stats, basis, sides):
    planar, low, high, factors = run_smooth(plain, cells, place, stats, basis, sides, density.shape[1])
    pieces, blocks = depth_pieces(planar, low, high)
    return run_finish(factors, density, bone, pieces, blocks), factors


def on_device(density, bone, fixed, load):
    table = element_stiffness()
    density, bone, fixed, load = density[0], bone[0], fixed[0], load[:, 0]
    depth, height, width = density.shape
    slabs = lax.axis_size("gy") * lax.axis_size("gz")
    slab = lax.axis_index("gz") * lax.axis_size("gy") + lax.axis_index("gy")
    nx = lax.axis_size("gx")
    cells = density.size * nx * slabs
    place = jnp.stack([lax.axis_index("gx"), slab]).astype(jnp.int32)

    up, down = run_messages(density, bone, fixed, load)
    got_up = to_slab(up, 1)
    got_down = to_slab(down, -1)
    fields, edges = run_prepare(place, density, bone, fixed, load)
    around = [side for sent, steps in zip(edges, (0, 1, -1)) for side in edges_moved(sent, steps)]
    first, second, basis, stats, *ends = run_krylov(
        table, place, fields, (got_up, got_down, *around)
    )
    sides = edges_moved(ends, 0)
    stats = total_over_mesh(stats)
    updated, factors = remodelled(False, cells, place, density, bone, stats, basis, sides)
    moved = run_displacement(factors, first, second, height)

    def repeated(state):
        specific, moved = plain_path(table, density, bone, fixed, load)
        cover = lambda length, start, count: lax.dynamic_slice(
            jnp.asarray(coverage(length)), (start,), (count,)
        )
        cover_x = cover(nx * width, place[0] * width, width)
        cover_z = cover(slabs * depth, place[1] * depth, depth)
        spread = cover_z[:, None, None] * cover_x[:, None] * jnp.asarray(coverage(height))
        total = inner_sum(specific[..., :height] * spread)
        row, lane = (lax.broadcasted_iota(jnp.int32, (8, LANES), i) for i in range(2))
        tile = jnp.where((row == 4) & (lane == 0), total, 0.0)
        again = specific[None]
        updated = remodelled(True, cells, place, density, bone, tile, again, side_halos(again))[0]
        return True, updated, moved.reshape(-1, width)

    sound = factors[3, 0] > 0.5
    _, updated, moved = lax.while_loop(lambda state: ~state[0], repeated, (sound, updated, moved.reshape(-1, width)))
    return updated[None], moved.reshape(3, 1, depth, height, width)


def solution(mesh):
    placed = (
        P("gz", "gy", None, "gx"),
        P("gz", "gy", None, "gx"),
        P("gz", "gy", None, "gx"),
        P(None, "gz", "gy", None, "gx"),
    )
    return jax.shard_map(
        on_device,
        mesh=mesh,
        in_specs=placed,
        out_specs=(P("gz", "gy", None, "gx"), P(None, "gz", "gy", None, "gx")),
        check_vma=False,
    )
```

```python
import functools
import math

import jax
import jax.numpy as jnp
import numpy as np
from jax import lax
from jax.experimental import pallas as pl
from jax.experimental.pallas import tpu as pltpu
from jax.sharding import PartitionSpec as P


RAD = 24
ITERS = 2

MARROW = 0.1
REMODEL = 0.25
FLOOR = 0.2
CEILING = 1.0
EPSILON = 1e-06

LANES = 128
PAD = 8
GUARD = 0.01


def element_stiffness():
    poisson = 0.3
    lame = poisson / ((1.0 + poisson) * (1.0 - 2.0 * poisson))
    shear = 0.5 / (1.0 + poisson)
    elastic = np.zeros((6, 6))
    elastic[:3, :3] = lame
    for index in range(3):
        elastic[index, index] += 2.0 * shear
        elastic[index + 3, index + 3] = shear
    points = [0.5 - 0.5 / math.sqrt(3.0), 0.5 + 0.5 / math.sqrt(3.0)]
    matrix = np.zeros((24, 24))
    for point_z in points:
        for point_y in points:
            for point_x in points:
                strain = np.zeros((6, 24))
                for corner_z in range(2):
                    for corner_y in range(2):
                        for corner_x in range(2):
                            node = 4 * corner_z + 2 * corner_y + corner_x
                            shape_x = point_x if corner_x else 1.0 - point_x
                            shape_y = point_y if corner_y else 1.0 - point_y
                            shape_z = point_z if corner_z else 1.0 - point_z
                            slope_x = 1.0 if corner_x else -1.0
                            slope_y = 1.0 if corner_y else -1.0
                            slope_z = 1.0 if corner_z else -1.0
                            along_x = slope_x * shape_y * shape_z
                            along_y = shape_x * slope_y * shape_z
                            along_z = shape_x * shape_y * slope_z
                            strain[0, node] = along_x
                            strain[1, 8 + node] = along_y
                            strain[2, 16 + node] = along_z
                            strain[3, node] = along_y
                            strain[3, 8 + node] = along_x
                            strain[4, 8 + node] = along_z
                            strain[4, 16 + node] = along_y
                            strain[5, node] = along_z
                            strain[5, 16 + node] = along_x
                matrix = matrix + strain.T @ elastic @ strain / 8.0
    return matrix


X, Y, Z, XY, XZ, YZ, XYZ = 1, 2, 4, 3, 5, 6, 7
U, V, W = 0, 1, 2
REDUCED = [
    [(U, X)], [(V, Y)], [(W, Z)],
    [(U, Y), (V, X)], [(U, Z), (W, X)], [(V, Z), (W, Y)],
    [(V, XY)], [(W, XZ)], [(U, XY)], [(W, YZ)], [(U, XZ)], [(V, YZ)],
    [(U, YZ)], [(V, XZ)], [(W, XY)],
    [(U, XYZ)], [(V, XYZ)], [(W, XYZ)],
]


def mode_constants(table):
    one = np.array([[1.0, 1.0], [-1.0, 1.0]])
    sums = np.kron(one, np.kron(one, one))
    change = np.kron(np.eye(3), sums)
    modes = change @ table @ change.T / 64.0
    at = lambda a, b: float(modes[a[0] * 8 + a[1], b[0] * 8 + b[1]])
    k = dict(
        cross=at((U, X), (V, Y)),
        shear=at((U, Y), (U, Y)),
        pair=at((V, XY), (W, XZ)),
        group=at((U, YZ), (V, XZ)),
        triple=at((U, XYZ), (U, XYZ)),
    )
    k["normal"] = at((U, X), (U, X)) - k["cross"]
    k["single"] = at((V, XY), (V, XY)) - k["pair"]
    reduce = np.zeros((18, 24))
    for row, members in enumerate(REDUCED):
        for component, bits in members:
            reduce[row, component * 8 + bits] = 1.0
    small = np.stack([np.array(stresses(list(unit), k)) for unit in np.eye(18)], axis=1)
    assert np.allclose(reduce.T @ small @ reduce, modes, atol=1e-12)
    assert np.allclose(np.diagonal(table), table[0, 0], atol=1e-12)
    return k


def stresses(m, k):
    trace = k["cross"] * (m[0] + m[1] + m[2])
    out = [trace + k["normal"] * m[i] for i in range(3)]
    out += [k["shear"] * m[i] for i in range(3, 6)]
    for i in (6, 8, 10):
        both = k["pair"] * (m[i] + m[i + 1])
        out += [both + k["single"] * m[i], both + k["single"] * m[i + 1]]
    total = m[12] + m[13] + m[14]
    out += [k["group"] * (total + m[i]) for i in range(12, 15)]
    out += [k["triple"] * m[i] for i in range(15, 18)]
    return out


def dotted(a, b):
    terms = [p * q for p, q in zip(a, b)]
    while len(terms) > 1:
        terms = [terms[i] + terms[i + 1] if i + 1 < len(terms) else terms[i] for i in range(0, len(terms), 2)]
    return terms[0]


def layer_modes(ref, index, row):
    found = []
    for component in range(3):
        low = ref[component, index, pl.ds(row, 8), :]
        high = ref[component, index, pl.ds(row + 1, 8), :]
        both, slope = low + high, high - low
        both_up, slope_up = (pltpu.roll(v, LANES - 1, 1) for v in (both, slope))
        found.append((both + both_up, slope + slope_up, both_up - both, slope_up - slope))
    return found


def voxel_modes(below, above):
    modes = {}
    for component in range(3):
        low, high = below[component], above[component]
        for bits in (X, Y, XY):
            modes[component, bits] = low[bits] + high[bits]
        for bits in (0, X, Y, XY):
            modes[component, bits + Z] = high[bits] - low[bits]
    reduced = []
    for members in REDUCED:
        value = modes[members[0]]
        for extra in members[1:]:
            value = value + modes[extra]
        reduced.append(value)
    return reduced


SLOT = {mode: row for row, members in enumerate(REDUCED) for mode in members}


def raw_layer(density, bone, fixed, load, z):
    thick = density[z]
    share = bone[z].astype(jnp.float32)
    free = 1.0 - fixed[z].astype(jnp.float32)
    modulus = share * thick * thick + (1.0 - share) * MARROW
    return modulus, [free * load[c, z] for c in range(3)], free, thick


def message_kernel(*refs):
    lowest, highest, (up, down) = refs[:8:2], refs[1:8:2], refs[8:]
    up[0] = raw_layer(*highest, 0)[0]
    modulus, force, _, _ = raw_layer(*highest, 1)
    up[1] = modulus
    for c in range(3):
        up[2 + c] = force[c]
    for z in range(2):
        modulus, force, free, _ = raw_layer(*lowest, z)
        down[z] = modulus
        for c in range(3):
            down[2 + 3 * z + c] = force[c]
        if z == 0:
            down[8] = free


def prepare_kernel(swap, place, density, bone, fixed, load, fields, *edges):
    depth, height, width = density.shape
    zeros = jnp.zeros((LANES - height, width), jnp.float32)
    first = place[0] == 0
    kinds = len(edges) // 3
    for z in range(depth):
        modulus, force, free, thick = raw_layer(density, bone, fixed, load, z)
        for slot, value in enumerate([modulus] + force + [free, thick]):
            turned = jnp.transpose(jnp.concatenate([value, zeros], axis=0))
            fields[slot, z] = turned
            if slot == 5:
                continue
            low, high = turned[:2], turned[width - 2 :]
            sent = (jnp.where(first, high, low),) if swap else (low, high)
            for kind in range(kinds):
                edges[kind][slot, z] = sent[kind]
                if z >= depth - 2:
                    edges[kinds + kind][slot, z - (depth - 2)] = sent[kind]
                if z < 2:
                    edges[2 * kinds + kind][slot, z] = sent[kind]


def krylov_kernel(
    k, kappa, across,
    place, cover_z, fields, up, down, left, right, left_up, right_up, left_down, right_down,
    cover_x, cover_y,
    *rest,
):
    out_p, out_w, out_g, out_stats = rest[:4]
    out_edges, rest = rest[4:-10], rest[-10:]
    mod, force, free, search, inverse, lower, upper, image, stress, accumulate = rest
    on_left = jnp.where(place[0] > 0, 1.0, 0.0)
    on_right = jnp.where(place[0] < across - 1, 1.0, 0.0)
    depth, width = fields.shape[1], fields.shape[2]
    height = up.shape[1]
    first, last = PAD, PAD + width
    chunks = width // 8
    blank = jnp.zeros((LANES - height, width), jnp.float32)

    def turned(value):
        return jnp.transpose(jnp.concatenate([value, blank], axis=0))

    empty = jnp.zeros((PAD, LANES), jnp.float32)
    for ref in (mod, force, search):
        lead = ref.shape[:-2]
        for spot in np.ndindex(*lead):
            ref[spot + (pl.ds(0, PAD),)] = empty
            ref[spot + (pl.ds(last, PAD),)] = empty
            ref[spot + (pl.ds(last + PAD, PAD),)] = empty
    for z in range(depth + 1):
        free[z, pl.ds(last, PAD)] = empty

    def local(z, carry):
        for c in range(chunks):
            rows, into = pl.ds(8 * c, 8), pl.ds(first + 8 * c, 8)
            mod[z + 2, into] = fields[0, z, rows]
            for i in range(3):
                force[i, z + 1, into] = fields[1 + i, z, rows]
            free[z, into] = fields[4, z, rows]
        mod[z + 2, pl.ds(first - 2, 2)] = left[0, z] * on_left
        mod[z + 2, pl.ds(last, 2)] = right[0, z] * on_right
        for i in range(3):
            force[i, z + 1, pl.ds(first - 2, 2)] = left[1 + i, z] * on_left
            force[i, z + 1, pl.ds(last, 2)] = right[1 + i, z] * on_right
        free[z, pl.ds(last, 2)] = right[4, z] * on_right
        return carry

    lax.fori_loop(0, depth, local, 0)
    body = pl.ds(first, width)
    for z in range(2):
        mod[z, body] = turned(up[z])
        mod[depth + 2 + z, body] = turned(down[z])
        for side, low, high, there in (
            (first - 2, left_up, left_down, on_left),
            (last, right_up, right_down, on_right),
        ):
            mod[z, pl.ds(side, 2)] = low[0, z] * there
            mod[depth + 2 + z, pl.ds(side, 2)] = high[0, z] * there
    for i in range(3):
        force[i, 0, body] = turned(up[2 + i])
        for side, low, high, there in (
            (first - 2, left_up, left_down, on_left),
            (last, right_up, right_down, on_right),
        ):
            force[i, 0, pl.ds(side, 2)] = low[1 + i, 1] * there
            for z in range(2):
                force[i, depth + 1 + z, pl.ds(side, 2)] = high[1 + i, z] * there
        for z in range(2):
            force[i, depth + 1 + z, body] = turned(down[2 + 3 * z + i])
    free[depth, body] = turned(down[8])
    free[depth, pl.ds(last, 2)] = right_down[4, 0] * on_right

    def divide(chunk, carry):
        row = pl.multiple_of(chunk * 8, 8)
        previous = None
        for z in range(depth + 4):
            here = mod[z, pl.ds(row + PAD, 8)] + mod[z, pl.ds(row + PAD - 1, 8)]
            here = here + pltpu.roll(here, 1, 1)
            if z >= 1 and z <= depth + 3:
                total = kappa * (here + previous)
                share = jnp.where(total > 0.0, 1.0 / jnp.where(total > 0.0, total, 1.0), 0.0)
                node = z - 1
                for i in range(3):
                    search[i, node, pl.ds(row + PAD, 8)] = force[i, node, pl.ds(row + PAD, 8)] * share
                if 1 <= node <= depth + 1:
                    inverse[node - 1, pl.ds(row + PAD, 8)] = free[node - 1, pl.ds(row + PAD, 8)] * share
            previous = here
        return carry

    lax.fori_loop(0, chunks + 1, divide, 0)
    for z in range(depth + 3):
        side = mod[z, pl.ds(0, 8)]
        if z + 1 < depth + 4:
            total = side + mod[z + 1, pl.ds(0, 8)]
            total = total + pltpu.roll(total, 1, 0)
            total = kappa * (total + pltpu.roll(total, 1, 1))
            share = jnp.where(total > 0.0, 1.0 / jnp.where(total > 0.0, total, 1.0), 0.0)
            for i in range(3):
                search[i, z, pl.ds(0, 8)] = force[i, z, pl.ds(0, 8)] * share

    for s in range(accumulate.shape[0]):
        accumulate[s] = jnp.zeros((8, LANES), jnp.float32)

    def elements(row, inner):
        below = layer_modes(search, 0, row)
        carried = None
        for node in range(1, depth + 3):
            above = layer_modes(search, node, row)
            modes = voxel_modes(below, above)
            strain = stresses(modes, k)
            scale = mod[node, pl.ds(row, 8)]
            voxel = node - 2
            if inner is not None and 0 <= voxel < depth:
                rows = pl.ds(row - PAD, 8)
                work = (0.5 * scale) * dotted(modes, strain)
                out_g[0, voxel, rows] = work
                for s in range(18):
                    stress[s, voxel, rows] = strain[s]
            strain = [scale * s for s in strain]
            carry = []
            for component in range(3):
                value = lambda bits: strain[SLOT[component, bits]]
                totals, tops = [], []
                for bits in (0, X, Y, XY):
                    slope = value(bits + Z)
                    low, high = (-slope, slope) if bits == 0 else (value(bits) - slope, value(bits) + slope)
                    tops.append(high)
                    if carried is not None:
                        totals.append(low + carried[component][len(totals)])
                carry.append(tops)
                if carried is not None:
                    plain = (totals[0] - totals[2]) + pltpu.roll(totals[0] + totals[2], 1, 1)
                    tilted = (totals[1] - totals[3]) + pltpu.roll(totals[1] + totals[3], 1, 1)
                    lower[component, voxel, pl.ds(row, 8)] = plain - tilted
                    upper[component, voxel, pl.ds(row, 8)] = plain + tilted
            carried = carry
            below = above

    def middle(chunk, carry):
        elements(pl.multiple_of(PAD + chunk * 8, 8), True)
        return carry

    elements(0, None)
    lax.fori_loop(0, chunks, middle, 0)
    elements(last, None)

    def gather(chunk, carry):
        row = pl.multiple_of(PAD + chunk * 8, 8)
        rows = pl.ds(row, 8)
        gamma, second = jnp.zeros((8, LANES), jnp.float32), jnp.zeros((8, LANES), jnp.float32)
        for node in range(depth + 1):
            share = inverse[node, rows]
            for i in range(3):
                pulled = lower[i, node, rows] + upper[i, node, pl.ds(row - 1, 8)]
                scaled = share * pulled
                image[i, node, rows] = scaled
                if node < depth:
                    second = second + scaled * pulled
                    gamma = gamma + force[i, node + 1, rows] * search[i, node + 1, rows]
        accumulate[0] = accumulate[0] + jnp.where(chunk < chunks, gamma, 0.0)
        accumulate[2] = accumulate[2] + jnp.where(chunk < chunks, second, 0.0)
        return carry

    lax.fori_loop(0, chunks + 1, gather, 0)

    def energies(chunk, carry):
        row = pl.multiple_of(PAD + chunk * 8, 8)
        rows = pl.ds(pl.multiple_of(chunk * 8, 8), 8)
        across_rows = pl.ds(pl.multiple_of(place[0] * width + chunk * 8, 8), 8)
        weight = cover_x[across_rows] * cover_y[...]
        sums = [jnp.zeros((8, LANES), jnp.float32) for _ in range(5)]
        below = layer_modes(image, 0, row)
        for voxel in range(depth):
            above = layer_modes(image, voxel + 1, row)
            modes = voxel_modes(below, above)
            half = 0.5 * mod[voxel + 2, pl.ds(row, 8)]
            first_work = out_g[0, voxel, rows]
            mixed = half * dotted(modes, [stress[s, voxel, rows] for s in range(18)])
            second_work = half * dotted(modes, stresses(modes, k))
            thick = fields[5, voxel, rows]
            flip = jnp.where(thick > 0.0, 1.0 / jnp.where(thick > 0.0, thick, 1.0), 0.0)
            spread = weight * cover_z[place[1] * depth + voxel]
            sums[0] = sums[0] + first_work
            sums[1] = sums[1] + second_work
            for i, work in enumerate((first_work, mixed, second_work)):
                value = work * flip
                out_g[i, voxel, rows] = value
                sums[2 + i] = sums[2 + i] + spread * value
            below = above
            for i in range(3):
                out_p[i, voxel, rows] = search[i, voxel + 1, pl.ds(row, 8)]
                out_w[i, voxel, rows] = image[i, voxel, pl.ds(row, 8)]
        for slot, value in zip((1, 3, 4, 5, 6), sums):
            accumulate[slot] = accumulate[slot] + value
        return carry

    lax.fori_loop(0, chunks, energies, 0)
    for i in range(3):
        for z in range(depth):
            low, high = out_g[i, z, pl.ds(0, RAD)], out_g[i, z, pl.ds(width - RAD, RAD)]
            sent = (jnp.where(place[0] == 0, high, low),) if len(out_edges) == 1 else (low, high)
            for ref, value in zip(out_edges, sent):
                ref[i, z] = value
    for s in range(8):
        out_stats[pl.ds(s, 1)] = jnp.sum(accumulate[s], axis=0, keepdims=True)


def run_messages(density, bone, fixed, load):
    depth, height, width = density.shape
    specs, arrays = [], []
    for array in (density, bone, fixed, load):
        lead = array.shape[:-3]
        for block in (0, depth // 2 - 1):
            spot = lambda _, block=block, lead=lead: (0,) * len(lead) + (block, 0, 0)
            specs.append(pl.BlockSpec(lead + (2, height, width), spot))
            arrays.append(array)
    return pl.pallas_call(
        message_kernel,
        grid=(1,),
        in_specs=specs,
        out_specs=[pl.BlockSpec((n, height, width), lambda _: (0, 0, 0)) for n in (5, 9)],
        out_shape=[jax.ShapeDtypeStruct((n, height, width), jnp.float32) for n in (5, 9)],
        name="messages",
    )(*arrays)


SCALAR = pl.BlockSpec(memory_space=pltpu.SMEM)
VECTOR = pl.BlockSpec(memory_space=pltpu.VMEM)


def run_prepare(place, density, bone, fixed, load):
    depth, _, width = density.shape
    swap = lax.axis_size("gx") == 2
    shapes = [(6, depth, width, LANES)]
    for layers in (depth, 2, 2):
        shapes += [(5, layers, 2, LANES)] * (1 if swap else 2)
    fields, *edges = pl.pallas_call(
        functools.partial(prepare_kernel, swap),
        in_specs=[SCALAR] + [VECTOR] * 4,
        out_specs=[VECTOR] * len(shapes),
        out_shape=[jax.ShapeDtypeStruct(s, jnp.float32) for s in shapes],
        name="prepare",
    )(place, density, bone, fixed, load)
    kinds = len(edges) // 3
    return fields, [edges[i * kinds : (i + 1) * kinds] for i in range(3)]


def run_krylov(table, place, fields, halos):
    depth, width = fields.shape[1], fields.shape[2]
    height = halos[0].shape[1]
    nx = lax.axis_size("gx")
    slabs = lax.axis_size("gy") * lax.axis_size("gz")
    rows = width + 3 * PAD
    shapes = [(3, depth, width, LANES)] * 3 + [(8, LANES)]
    shapes += [(3, depth, RAD, LANES)] * (1 if nx == 2 else 2)
    layers = [(depth + 4,), (3, depth + 3), (depth + 1,), (3, depth + 3), (depth + 1,)]
    layers += [(3, depth + 1)] * 3
    scratch = [pltpu.VMEM(lead + (rows, LANES), jnp.float32) for lead in layers]
    scratch += [
        pltpu.VMEM((18, depth, width, LANES), jnp.float32),
        pltpu.VMEM((8, 8, LANES), jnp.float32),
    ]
    cover_x = coverage(nx * width)[:, None]
    cover_y = np.pad(coverage(height), (0, LANES - height))[None]
    return pl.pallas_call(
        functools.partial(krylov_kernel, mode_constants(table), float(table[0, 0]), nx),
        in_specs=[SCALAR] * 2 + [VECTOR] * (len(halos) + 3),
        out_specs=[VECTOR] * len(shapes),
        out_shape=[jax.ShapeDtypeStruct(s, jnp.float32) for s in shapes],
        scratch_shapes=scratch,
        compiler_params=pltpu.CompilerParams(vmem_limit_bytes=56 * 1024 * 1024),
        name="krylov",
    )(place, jnp.asarray(coverage(slabs * depth)), fields, *halos, jnp.asarray(cover_x), jnp.asarray(cover_y))


def slab_route(steps, sideways=0):
    nx, ny, nz = (lax.axis_size(a) for a in ("gx", "gy", "gz"))
    pairs = []
    for x in range(nx):
        for slab in range(ny * nz):
            to, tx = slab + steps, x + sideways
            if 0 <= to < ny * nz and 0 <= tx < nx:
                spot = lambda i, s: (i * ny + s % ny) * nz + s // ny
                pairs.append((spot(x, slab), spot(tx, to)))
    return pairs


def to_slab(value, steps, sideways=0):
    return lax.ppermute(value, ("gx", "gy", "gz"), slab_route(steps, sideways))


def edges_swapped(low_edge, high_edge, steps):
    if lax.axis_size("gx") == 2:
        first = lax.axis_index("gx") == 0
        sent = jnp.where(first, high_edge, low_edge)
        spots = slab_route(steps, 1) + slab_route(steps, -1)
        got = lax.ppermute(sent, ("gx", "gy", "gz"), spots)
        none = jnp.zeros_like(got)
        return jnp.where(first, none, got), jnp.where(first, got, none)
    return to_slab(high_edge, steps, 1), to_slab(low_edge, steps, -1)


def edges_moved(sent, steps):
    if len(sent) == 1:
        spots = slab_route(steps, 1) + slab_route(steps, -1)
        got = lax.ppermute(sent[0], ("gx", "gy", "gz"), spots)
        return got, got
    return to_slab(sent[1], steps, 1), to_slab(sent[0], steps, -1)


def total_over_mesh(value):
    for axis in ("gz", "gy", "gx"):
        count = lax.axis_size(axis)
        if count & (count - 1):
            value = lax.psum(value, axis)
            continue
        step = 1
        while step < count:
            other = lax.ppermute(value, axis, [(i, i ^ step) for i in range(count)])
            value = value + other
            step *= 2
    return value


def inner_sum(values):
    return total_over_mesh(jnp.full((8, LANES), jnp.sum(values)))[0, 0]


def tap_table():
    offsets = np.abs(np.arange(2 * RAD + 1) - RAD)
    raw = np.exp(-offsets / (0.5 * RAD))
    return raw / raw.sum()


def banded(length_in, length_out, shift):
    taps = tap_table()
    matrix = np.zeros((length_in, length_out))
    for i in range(length_in):
        for o in range(length_out):
            distance = i - shift - o
            if abs(distance) <= RAD:
                matrix[i, o] = taps[distance + RAD]
    return matrix.astype(np.float32)


def coverage(length):
    ends = np.concatenate([[0.0], np.cumsum(tap_table())])
    position = np.arange(length)
    low = np.maximum(-RAD, -position) + RAD
    high = np.minimum(RAD, length - 1 - position) + RAD + 1
    return (ends[high] - ends[low]).astype(np.float32)


def depth_pieces(planar, low_plane, high_plane):
    depth = planar.shape[0]
    taps = tap_table()
    ratio = math.exp(-1.0 / (0.5 * RAD))
    pieces, blocks = [planar], [banded(depth, depth, 0)]
    near, far = [], []
    steps = 1
    while (steps - 1) * depth + 1 <= RAD:
        if steps * depth + depth - 1 <= RAD:
            away = steps * depth + np.arange(depth)
            near.append((high_plane, steps, taps[RAD] * ratio ** (away - (depth - 1))))
            away = steps * depth - np.arange(depth)
            near.append((low_plane, -steps, taps[RAD] * ratio ** away))
        else:
            far.append((steps, banded(depth, depth, steps * depth)))
            far.append((-steps, banded(depth, depth, -steps * depth)))
        steps += 1
    for move, block in far:
        pieces.append(to_slab(planar, move))
        blocks.append(block)
    for plane, move, weight in near:
        pieces.append(to_slab(plane, move)[None])
        blocks.append(weight[None].astype(np.float32))
    return pieces, blocks


def depth_decay(depth):
    return (math.exp(-1.0 / (0.5 * RAD)) ** np.arange(depth)).astype(np.float32)


def krylov_coefficients(sums):
    gamma, curve, mixed, curve_second = sums[0], 2.0 * sums[1], sums[2], 2.0 * sums[3]
    alpha = gamma / curve
    grown = alpha * mixed / curve
    beta = grown - 1.0
    bent = alpha * (alpha * (alpha * curve_second / gamma))
    rest = bent - grown * grown
    alpha_next = alpha * beta / rest
    by_first = alpha + alpha_next * grown
    by_second = -alpha_next * alpha
    squares = [by_first * by_first, 2.0 * by_first * by_second, by_second * by_second]
    parts = [f * s for f, s in zip(squares, sums[4:7])]
    total = parts[0] + parts[1] + parts[2]
    size = jnp.abs(parts[0]) + jnp.abs(parts[1]) + jnp.abs(parts[2])
    sound = (beta > GUARD * grown) & (rest > GUARD * bent) & (total > GUARD * size)
    return by_first, by_second, squares, total, jnp.where(sound, 1.0, 0.0)


def smooth_kernel(
    plain, cells, nx, place, stats, basis, left, right, along_x, along_y, planar, low, high, factors
):
    on_left = jnp.where(place[0] > 0, 1.0, 0.0)
    on_right = jnp.where(place[0] < nx - 1, 1.0, 0.0)
    depth = basis.shape[1]
    decay = depth_decay(depth)
    exact = dict(precision=lax.Precision.HIGHEST, preferred_element_type=jnp.float32)
    tile = stats[...]
    sums = [jnp.sum(tile[i : i + 1], axis=1, keepdims=True) for i in range(8)]
    if plain:
        one = jnp.ones((1, 1), jnp.float32)
        by_first, by_second, squares, total, sound = one, one, [one], sums[4], one
    else:
        by_first, by_second, squares, total, sound = krylov_coefficients(sums)
    scale = 1.0 / (total / cells + EPSILON)
    for i, value in enumerate((by_first, by_second, scale, sound)):
        factors[pl.ds(i, 1)] = jnp.broadcast_to(value, (1, LANES))
    factors[pl.ds(4, 4)] = jnp.zeros((4, LANES), jnp.float32)
    for z in range(depth):
        wide = jnp.concatenate(
            [
                there * sum(f * v[i, z] for i, f in enumerate(squares))
                for v, there in ((left, on_left), (basis, 1.0), (right, on_right))
            ],
            axis=0,
        )
        half = lax.dot_general(along_x[...], wide, (((1,), (0,)), ((), ())), **exact)
        plane = lax.dot_general(along_y[...], half, (((1,), (1,)), ((), ())), **exact)
        planar[z] = plane
        for ref, weight in ((low, decay[z]), (high, decay[depth - 1 - z])):
            share = plane * float(weight)
            ref[...] = share if z == 0 else ref[...] + share


def run_smooth(plain, cells, place, stats, basis, sides, height):
    depth, width = basis.shape[1:3]
    along_x = banded(width + 2 * RAD, width, RAD).T
    along_y = np.zeros((height, LANES), np.float32)
    along_y[:, :height] = banded(height, height, 0).T
    shapes = ((depth, height, width), (height, width), (height, width), (8, LANES))
    return pl.pallas_call(
        functools.partial(smooth_kernel, plain, float(cells), lax.axis_size("gx")),
        in_specs=[SCALAR] + [VECTOR] * 6,
        out_specs=[VECTOR] * 4,
        out_shape=[jax.ShapeDtypeStruct(s, jnp.float32) for s in shapes],
        name="smooth",
    )(place, stats, basis, *sides, jnp.asarray(along_x), jnp.asarray(along_y))


def finish_kernel(blocks, factors, density, bone, *rest):
    pieces, out = rest[:-1], rest[-1]
    depth, height, _ = density.shape

    scale = factors[pl.ds(2, 1)]

    def chunk(index, carry):
        rows = pl.ds(pl.multiple_of(index * 8, 8), 8)
        totals = [None] * depth
        for piece, block in zip(pieces, blocks):
            for i in range(block.shape[0]):
                value = piece[i, rows]
                for o in range(depth):
                    if block[i, o] != 0.0:
                        term = value * float(block[i, o])
                        totals[o] = term if totals[o] is None else totals[o] + term
        for o in range(depth):
            share = REMODEL * bone[o, rows].astype(jnp.float32)
            moved = density[o, rows] + share * (totals[o] * scale - 1.0)
            out[o, rows] = jnp.clip(moved, FLOOR, CEILING)
        return carry

    lax.fori_loop(0, height // 8, chunk, 0)


def run_finish(factors, density, bone, pieces, blocks):
    return pl.pallas_call(
        functools.partial(finish_kernel, blocks),
        out_shape=jax.ShapeDtypeStruct(density.shape, jnp.float32),
        name="finish",
    )(factors, density, bone, *pieces)


def displacement_kernel(height, factors, first, second, out):
    by_first, by_second = factors[pl.ds(0, 1)], factors[pl.ds(1, 1)]

    def layer(z, carry):
        for i in range(3):
            moved = by_first * first[i, z] + by_second * second[i, z]
            out[i, z] = jnp.transpose(moved)[:height]
        return carry

    lax.fori_loop(0, first.shape[1], layer, 0)


def run_displacement(factors, first, second, height):
    depth, width = first.shape[1:3]
    return pl.pallas_call(
        functools.partial(displacement_kernel, height),
        out_shape=jax.ShapeDtypeStruct((3, depth, height, width), jnp.float32),
        name="displacement",
    )(factors, first, second)


def corners():
    return [(cz, cy, cx) for cz in range(2) for cy in range(2) for cx in range(2)]


def upper_nodes(field):
    column = lax.ppermute(field[:, :, :, :1], ("gx", "gy", "gz"), slab_route(0, -1))
    wide = jnp.concatenate([field, column], axis=3)
    wide = jnp.concatenate([wide, to_slab(wide[:, :1], -1)], axis=1)
    return jnp.pad(wide, ((0, 0), (0, 0), (0, 1), (0, 0)))


def fold_upper(values):
    depth, width = values.shape[1] - 1, values.shape[3] - 1
    carried = to_slab(values[:, depth:], 1)
    values = jnp.concatenate([values[:, :1] + carried, values[:, 1:depth]], axis=1)
    column = lax.ppermute(values[:, :, :, width:], ("gx", "gy", "gz"), slab_route(0, 1))
    return jnp.concatenate([values[:, :, :, :1] + column, values[:, :, :, 1:width]], axis=3)


def corner_columns(nodes, shape):
    depth, height, width = shape
    return jnp.stack(
        [
            nodes[c, cz : cz + depth, cy : cy + height, cx : cx + width]
            for c in range(3)
            for cz, cy, cx in corners()
        ]
    )


def element_products(columns, table):
    return jnp.einsum(
        "rc,czyx->rzyx", jnp.asarray(table, jnp.float32), columns, precision=lax.Precision.HIGHEST
    )


def spread_corner(values, corner):
    return jnp.pad(values, ((0, 0),) + tuple((c, 1 - c) for c in corner))


def plain_forces(field, modulus, table):
    _, height, _ = modulus.shape
    columns = corner_columns(upper_nodes(field), modulus.shape)
    products = element_products(columns, table) * modulus
    products = products.reshape((3, 8) + modulus.shape)
    total = sum(spread_corner(products[:, node], corner) for node, corner in enumerate(corners()))
    return fold_upper(total[:, :, :height])


def plain_path(table, density, bone, fixed, load):
    _, height, _ = density.shape
    share = bone.astype(jnp.float32)
    free = 1.0 - fixed.astype(jnp.float32)
    modulus = share * density * density + (1.0 - share) * MARROW
    spread = sum(spread_corner(modulus[None], corner) for corner in corners())
    precondition = free / (float(table[0, 0]) * fold_upper(spread[:, :, :height]))
    residual = free * load
    search = precondition * residual
    start = (jnp.zeros_like(residual), residual, search, inner_sum(residual * search))

    def iterate(_, state):
        moved, residual, search, gamma = state
        image = free * plain_forces(free * search, modulus, table)
        alpha = gamma / inner_sum(search * image)
        moved = moved + alpha * search
        residual = residual - alpha * image
        scaled = precondition * residual
        gamma_next = inner_sum(residual * scaled)
        return moved, residual, scaled + gamma_next / gamma * search, gamma_next

    moved = lax.fori_loop(0, ITERS, iterate, start)[0]
    columns = corner_columns(upper_nodes(moved), modulus.shape)
    energy = 0.5 * modulus * jnp.sum(columns * element_products(columns, table), axis=0)
    specific = jnp.swapaxes(energy / density, 1, 2)
    return jnp.pad(specific, ((0, 0), (0, 0), (0, LANES - height))), moved


def side_halos(basis):
    width = basis.shape[2]
    return edges_swapped(basis[:, :, :RAD], basis[:, :, width - RAD :], 0)


def remodelled(plain, cells, place, density, bone, stats, basis, sides):
    planar, low, high, factors = run_smooth(plain, cells, place, stats, basis, sides, density.shape[1])
    pieces, blocks = depth_pieces(planar, low, high)
    return run_finish(factors, density, bone, pieces, blocks), factors


def on_device(density, bone, fixed, load):
    table = element_stiffness()
    density, bone, fixed, load = density[0], bone[0], fixed[0], load[:, 0]
    depth, height, width = density.shape
    slabs = lax.axis_size("gy") * lax.axis_size("gz")
    slab = lax.axis_index("gz") * lax.axis_size("gy") + lax.axis_index("gy")
    nx = lax.axis_size("gx")
    cells = density.size * nx * slabs
    place = jnp.stack([lax.axis_index("gx"), slab]).astype(jnp.int32)

    up, down = run_messages(density, bone, fixed, load)
    got_up = to_slab(up, 1)
    got_down = to_slab(down, -1)
    fields, edges = run_prepare(place, density, bone, fixed, load)
    around = [side for sent, steps in zip(edges, (0, 1, -1)) for side in edges_moved(sent, steps)]
    first, second, basis, stats, *ends = run_krylov(
        table, place, fields, (got_up, got_down, *around)
    )
    sides = edges_moved(ends, 0)
    stats = total_over_mesh(stats)
    updated, factors = remodelled(False, cells, place, density, bone, stats, basis, sides)
    moved = run_displacement(factors, first, second, height)

    kept = [v.reshape(-1, width) for v in (density, bone, fixed, load)]

    def repeated(state):
        again = [v.reshape((-1, depth, height, width)) for v in kept]
        specific, moved = plain_path(table, *(v[0] for v in again[:3]), again[3])
        cover = lambda length, start, count: lax.dynamic_slice(
            jnp.asarray(coverage(length)), (start,), (count,)
        )
        cover_x = cover(nx * width, place[0] * width, width)
        cover_z = cover(slabs * depth, place[1] * depth, depth)
        spread = cover_z[:, None, None] * cover_x[:, None] * jnp.asarray(coverage(height))
        total = inner_sum(specific[..., :height] * spread)
        row, lane = (lax.broadcasted_iota(jnp.int32, (8, LANES), i) for i in range(2))
        tile = jnp.where((row == 4) & (lane == 0), total, 0.0)
        again = specific[None]
        updated = remodelled(True, cells, place, density, bone, tile, again, side_halos(again))[0]
        return True, updated, moved.reshape(-1, width)

    sound = factors[3, 0] > 0.5
    _, updated, moved = lax.while_loop(lambda state: ~state[0], repeated, (sound, updated, moved.reshape(-1, width)))
    return updated[None], moved.reshape(3, 1, depth, height, width)


def solution(mesh):
    placed = (
        P("gz", "gy", None, "gx"),
        P("gz", "gy", None, "gx"),
        P("gz", "gy", None, "gx"),
        P(None, "gz", "gy", None, "gx"),
    )
    return jax.shard_map(
        on_device,
        mesh=mesh,
        in_specs=placed,
        out_specs=(P("gz", "gy", None, "gx"), P(None, "gz", "gy", None, "gx")),
        check_vma=False,
    )
```

```python
import functools
import math

import jax
import jax.numpy as jnp
import numpy as np
from jax import lax
from jax.experimental import pallas as pl
from jax.experimental.pallas import tpu as pltpu
from jax.sharding import PartitionSpec as P


RAD = 24
ITERS = 2

MARROW = 0.1
REMODEL = 0.25
FLOOR = 0.2
CEILING = 1.0
EPSILON = 1e-06

LANES = 128
PAD = 8
GUARD = 0.01


def element_stiffness():
    poisson = 0.3
    lame = poisson / ((1.0 + poisson) * (1.0 - 2.0 * poisson))
    shear = 0.5 / (1.0 + poisson)
    elastic = np.zeros((6, 6))
    elastic[:3, :3] = lame
    for index in range(3):
        elastic[index, index] += 2.0 * shear
        elastic[index + 3, index + 3] = shear
    points = [0.5 - 0.5 / math.sqrt(3.0), 0.5 + 0.5 / math.sqrt(3.0)]
    matrix = np.zeros((24, 24))
    for point_z in points:
        for point_y in points:
            for point_x in points:
                strain = np.zeros((6, 24))
                for corner_z in range(2):
                    for corner_y in range(2):
                        for corner_x in range(2):
                            node = 4 * corner_z + 2 * corner_y + corner_x
                            shape_x = point_x if corner_x else 1.0 - point_x
                            shape_y = point_y if corner_y else 1.0 - point_y
                            shape_z = point_z if corner_z else 1.0 - point_z
                            slope_x = 1.0 if corner_x else -1.0
                            slope_y = 1.0 if corner_y else -1.0
                            slope_z = 1.0 if corner_z else -1.0
                            along_x = slope_x * shape_y * shape_z
                            along_y = shape_x * slope_y * shape_z
                            along_z = shape_x * shape_y * slope_z
                            strain[0, node] = along_x
                            strain[1, 8 + node] = along_y
                            strain[2, 16 + node] = along_z
                            strain[3, node] = along_y
                            strain[3, 8 + node] = along_x
                            strain[4, 8 + node] = along_z
                            strain[4, 16 + node] = along_y
                            strain[5, node] = along_z
                            strain[5, 16 + node] = along_x
                matrix = matrix + strain.T @ elastic @ strain / 8.0
    return matrix


X, Y, Z, XY, XZ, YZ, XYZ = 1, 2, 4, 3, 5, 6, 7
U, V, W = 0, 1, 2
REDUCED = [
    [(U, X)], [(V, Y)], [(W, Z)],
    [(U, Y), (V, X)], [(U, Z), (W, X)], [(V, Z), (W, Y)],
    [(V, XY)], [(W, XZ)], [(U, XY)], [(W, YZ)], [(U, XZ)], [(V, YZ)],
    [(U, YZ)], [(V, XZ)], [(W, XY)],
    [(U, XYZ)], [(V, XYZ)], [(W, XYZ)],
]


def mode_constants(table):
    one = np.array([[1.0, 1.0], [-1.0, 1.0]])
    sums = np.kron(one, np.kron(one, one))
    change = np.kron(np.eye(3), sums)
    modes = change @ table @ change.T / 64.0
    at = lambda a, b: float(modes[a[0] * 8 + a[1], b[0] * 8 + b[1]])
    k = dict(
        cross=at((U, X), (V, Y)),
        shear=at((U, Y), (U, Y)),
        pair=at((V, XY), (W, XZ)),
        group=at((U, YZ), (V, XZ)),
        triple=at((U, XYZ), (U, XYZ)),
    )
    k["normal"] = at((U, X), (U, X)) - k["cross"]
    k["single"] = at((V, XY), (V, XY)) - k["pair"]
    reduce = np.zeros((18, 24))
    for row, members in enumerate(REDUCED):
        for component, bits in members:
            reduce[row, component * 8 + bits] = 1.0
    small = np.stack([np.array(stresses(list(unit), k)) for unit in np.eye(18)], axis=1)
    assert np.allclose(reduce.T @ small @ reduce, modes, atol=1e-12)
    assert np.allclose(np.diagonal(table), table[0, 0], atol=1e-12)
    return k


def stresses(m, k):
    trace = k["cross"] * (m[0] + m[1] + m[2])
    out = [trace + k["normal"] * m[i] for i in range(3)]
    out += [k["shear"] * m[i] for i in range(3, 6)]
    for i in (6, 8, 10):
        both = k["pair"] * (m[i] + m[i + 1])
        out += [both + k["single"] * m[i], both + k["single"] * m[i + 1]]
    total = m[12] + m[13] + m[14]
    out += [k["group"] * (total + m[i]) for i in range(12, 15)]
    out += [k["triple"] * m[i] for i in range(15, 18)]
    return out


def dotted(a, b):
    terms = [p * q for p, q in zip(a, b)]
    while len(terms) > 1:
        terms = [terms[i] + terms[i + 1] if i + 1 < len(terms) else terms[i] for i in range(0, len(terms), 2)]
    return terms[0]


def layer_modes(ref, index, row):
    found = []
    for component in range(3):
        low = ref[component, index, pl.ds(row, 8), :]
        high = ref[component, index, pl.ds(row + 1, 8), :]
        both, slope = low + high, high - low
        both_up, slope_up = (pltpu.roll(v, LANES - 1, 1) for v in (both, slope))
        found.append((both + both_up, slope + slope_up, both_up - both, slope_up - slope))
    return found


def voxel_modes(below, above):
    modes = {}
    for component in range(3):
        low, high = below[component], above[component]
        for bits in (X, Y, XY):
            modes[component, bits] = low[bits] + high[bits]
        for bits in (0, X, Y, XY):
            modes[component, bits + Z] = high[bits] - low[bits]
    reduced = []
    for members in REDUCED:
        value = modes[members[0]]
        for extra in members[1:]:
            value = value + modes[extra]
        reduced.append(value)
    return reduced


SLOT = {mode: row for row, members in enumerate(REDUCED) for mode in members}


def raw_layer(density, bone, fixed, load, z):
    thick = density[z]
    share = bone[z].astype(jnp.float32)
    free = 1.0 - fixed[z].astype(jnp.float32)
    modulus = share * thick * thick + (1.0 - share) * MARROW
    return modulus, [free * load[c, z] for c in range(3)], free, thick


def message_kernel(*refs):
    lowest, highest, (up, down) = refs[:8:2], refs[1:8:2], refs[8:]
    up[0] = raw_layer(*highest, 0)[0]
    modulus, force, _, _ = raw_layer(*highest, 1)
    up[1] = modulus
    for c in range(3):
        up[2 + c] = force[c]
    for z in range(2):
        modulus, force, free, _ = raw_layer(*lowest, z)
        down[z] = modulus
        for c in range(3):
            down[2 + 3 * z + c] = force[c]
        if z == 0:
            down[8] = free


def prepare_kernel(swap, place, density, bone, fixed, load, fields, *edges):
    depth, height, width = density.shape
    zeros = jnp.zeros((LANES - height, width), jnp.float32)
    first = place[0] == 0
    kinds = len(edges) // 3
    for z in range(depth):
        modulus, force, free, thick = raw_layer(density, bone, fixed, load, z)
        for slot, value in enumerate([modulus] + force + [free, thick]):
            turned = jnp.transpose(jnp.concatenate([value, zeros], axis=0))
            fields[slot, z] = turned
            if slot == 5:
                continue
            low, high = turned[:2], turned[width - 2 :]
            sent = (jnp.where(first, high, low),) if swap else (low, high)
            for kind in range(kinds):
                edges[kind][slot, z] = sent[kind]
                if z >= depth - 2:
                    edges[kinds + kind][slot, z - (depth - 2)] = sent[kind]
                if z < 2:
                    edges[2 * kinds + kind][slot, z] = sent[kind]


def krylov_kernel(
    k, kappa, across,
    place, cover_z, fields, up, down, left, right, left_up, right_up, left_down, right_down,
    cover_x, cover_y,
    *rest,
):
    out_p, out_w, out_g, out_stats = rest[:4]
    out_edges, rest = rest[4:-10], rest[-10:]
    mod, force, free, search, inverse, lower, upper, image, stress, accumulate = rest
    on_left = jnp.where(place[0] > 0, 1.0, 0.0)
    on_right = jnp.where(place[0] < across - 1, 1.0, 0.0)
    depth, width = fields.shape[1], fields.shape[2]
    height = up.shape[1]
    first, last = PAD, PAD + width
    chunks = width // 8
    blank = jnp.zeros((LANES - height, width), jnp.float32)

    def turned(value):
        return jnp.transpose(jnp.concatenate([value, blank], axis=0))

    empty = jnp.zeros((PAD, LANES), jnp.float32)
    for ref in (mod, force, search):
        lead = ref.shape[:-2]
        for spot in np.ndindex(*lead):
            ref[spot + (pl.ds(0, PAD),)] = empty
            ref[spot + (pl.ds(last, PAD),)] = empty
            ref[spot + (pl.ds(last + PAD, PAD),)] = empty
    for z in range(depth + 1):
        free[z, pl.ds(last, PAD)] = empty

    def local(z, carry):
        for c in range(chunks):
            rows, into = pl.ds(8 * c, 8), pl.ds(first + 8 * c, 8)
            mod[z + 2, into] = fields[0, z, rows]
            for i in range(3):
                force[i, z + 1, into] = fields[1 + i, z, rows]
            free[z, into] = fields[4, z, rows]
        mod[z + 2, pl.ds(first - 2, 2)] = left[0, z] * on_left
        mod[z + 2, pl.ds(last, 2)] = right[0, z] * on_right
        for i in range(3):
            force[i, z + 1, pl.ds(first - 2, 2)] = left[1 + i, z] * on_left
            force[i, z + 1, pl.ds(last, 2)] = right[1 + i, z] * on_right
        free[z, pl.ds(last, 2)] = right[4, z] * on_right
        return carry

    lax.fori_loop(0, depth, local, 0)
    body = pl.ds(first, width)
    for z in range(2):
        mod[z, body] = turned(up[z])
        mod[depth + 2 + z, body] = turned(down[z])
        for side, low, high, there in (
            (first - 2, left_up, left_down, on_left),
            (last, right_up, right_down, on_right),
        ):
            mod[z, pl.ds(side, 2)] = low[0, z] * there
            mod[depth + 2 + z, pl.ds(side, 2)] = high[0, z] * there
    for i in range(3):
        force[i, 0, body] = turned(up[2 + i])
        for side, low, high, there in (
            (first - 2, left_up, left_down, on_left),
            (last, right_up, right_down, on_right),
        ):
            force[i, 0, pl.ds(side, 2)] = low[1 + i, 1] * there
            for z in range(2):
                force[i, depth + 1 + z, pl.ds(side, 2)] = high[1 + i, z] * there
        for z in range(2):
            force[i, depth + 1 + z, body] = turned(down[2 + 3 * z + i])
    free[depth, body] = turned(down[8])
    free[depth, pl.ds(last, 2)] = right_down[4, 0] * on_right

    def divide(chunk, carry):
        row = pl.multiple_of(chunk * 8, 8)
        previous = None
        for z in range(depth + 4):
            here = mod[z, pl.ds(row + PAD, 8)] + mod[z, pl.ds(row + PAD - 1, 8)]
            here = here + pltpu.roll(here, 1, 1)
            if z >= 1 and z <= depth + 3:
                total = kappa * (here + previous)
                share = jnp.where(total > 0.0, 1.0 / jnp.where(total > 0.0, total, 1.0), 0.0)
                node = z - 1
                for i in range(3):
                    search[i, node, pl.ds(row + PAD, 8)] = force[i, node, pl.ds(row + PAD, 8)] * share
                if 1 <= node <= depth + 1:
                    inverse[node - 1, pl.ds(row + PAD, 8)] = free[node - 1, pl.ds(row + PAD, 8)] * share
            previous = here
        return carry

    lax.fori_loop(0, chunks + 1, divide, 0)
    for z in range(depth + 3):
        side = mod[z, pl.ds(0, 8)]
        if z + 1 < depth + 4:
            total = side + mod[z + 1, pl.ds(0, 8)]
            total = total + pltpu.roll(total, 1, 0)
            total = kappa * (total + pltpu.roll(total, 1, 1))
            share = jnp.where(total > 0.0, 1.0 / jnp.where(total > 0.0, total, 1.0), 0.0)
            for i in range(3):
                search[i, z, pl.ds(0, 8)] = force[i, z, pl.ds(0, 8)] * share

    for s in range(accumulate.shape[0]):
        accumulate[s] = jnp.zeros((8, LANES), jnp.float32)

    def elements(row, inner):
        below = layer_modes(search, 0, row)
        carried = None
        for node in range(1, depth + 3):
            above = layer_modes(search, node, row)
            modes = voxel_modes(below, above)
            strain = stresses(modes, k)
            scale = mod[node, pl.ds(row, 8)]
            voxel = node - 2
            if inner is not None and 0 <= voxel < depth:
                rows = pl.ds(row - PAD, 8)
                work = (0.5 * scale) * dotted(modes, strain)
                out_g[0, voxel, rows] = work
                for s in range(18):
                    stress[s, voxel, rows] = strain[s]
            strain = [scale * s for s in strain]
            carry = []
            for component in range(3):
                value = lambda bits: strain[SLOT[component, bits]]
                totals, tops = [], []
                for bits in (0, X, Y, XY):
                    slope = value(bits + Z)
                    low, high = (-slope, slope) if bits == 0 else (value(bits) - slope, value(bits) + slope)
                    tops.append(high)
                    if carried is not None:
                        totals.append(low + carried[component][len(totals)])
                carry.append(tops)
                if carried is not None:
                    plain = (totals[0] - totals[2]) + pltpu.roll(totals[0] + totals[2], 1, 1)
                    tilted = (totals[1] - totals[3]) + pltpu.roll(totals[1] + totals[3], 1, 1)
                    lower[component, voxel, pl.ds(row, 8)] = plain - tilted
                    upper[component, voxel, pl.ds(row, 8)] = plain + tilted
            carried = carry
            below = above

    def middle(chunk, carry):
        elements(pl.multiple_of(PAD + chunk * 8, 8), True)
        return carry

    elements(0, None)
    lax.fori_loop(0, chunks, middle, 0)
    elements(last, None)

    def gather(chunk, carry):
        row = pl.multiple_of(PAD + chunk * 8, 8)
        rows = pl.ds(row, 8)
        gamma, second = jnp.zeros((8, LANES), jnp.float32), jnp.zeros((8, LANES), jnp.float32)
        for node in range(depth + 1):
            share = inverse[node, rows]
            for i in range(3):
                pulled = lower[i, node, rows] + upper[i, node, pl.ds(row - 1, 8)]
                scaled = share * pulled
                image[i, node, rows] = scaled
                if node < depth:
                    second = second + scaled * pulled
                    gamma = gamma + force[i, node + 1, rows] * search[i, node + 1, rows]
        accumulate[0] = accumulate[0] + jnp.where(chunk < chunks, gamma, 0.0)
        accumulate[2] = accumulate[2] + jnp.where(chunk < chunks, second, 0.0)
        return carry

    lax.fori_loop(0, chunks + 1, gather, 0)

    def energies(chunk, carry):
        row = pl.multiple_of(PAD + chunk * 8, 8)
        rows = pl.ds(pl.multiple_of(chunk * 8, 8), 8)
        across_rows = pl.ds(pl.multiple_of(place[0] * width + chunk * 8, 8), 8)
        weight = cover_x[across_rows] * cover_y[...]
        sums = [jnp.zeros((8, LANES), jnp.float32) for _ in range(5)]
        below = layer_modes(image, 0, row)
        for voxel in range(depth):
            above = layer_modes(image, voxel + 1, row)
            modes = voxel_modes(below, above)
            half = 0.5 * mod[voxel + 2, pl.ds(row, 8)]
            first_work = out_g[0, voxel, rows]
            mixed = half * dotted(modes, [stress[s, voxel, rows] for s in range(18)])
            second_work = half * dotted(modes, stresses(modes, k))
            thick = fields[5, voxel, rows]
            flip = jnp.where(thick > 0.0, 1.0 / jnp.where(thick > 0.0, thick, 1.0), 0.0)
            spread = weight * cover_z[place[1] * depth + voxel]
            sums[0] = sums[0] + first_work
            sums[1] = sums[1] + second_work
            for i, work in enumerate((first_work, mixed, second_work)):
                value = work * flip
                out_g[i, voxel, rows] = value
                sums[2 + i] = sums[2 + i] + spread * value
            below = above
            for i in range(3):
                out_p[i, voxel, rows] = search[i, voxel + 1, pl.ds(row, 8)]
                out_w[i, voxel, rows] = image[i, voxel, pl.ds(row, 8)]
        for slot, value in zip((1, 3, 4, 5, 6), sums):
            accumulate[slot] = accumulate[slot] + value
        return carry

    lax.fori_loop(0, chunks, energies, 0)
    for i in range(3):
        for z in range(depth):
            low, high = out_g[i, z, pl.ds(0, RAD)], out_g[i, z, pl.ds(width - RAD, RAD)]
            sent = (jnp.where(place[0] == 0, high, low),) if len(out_edges) == 1 else (low, high)
            for ref, value in zip(out_edges, sent):
                ref[i, z] = value
    for s in range(8):
        out_stats[pl.ds(s, 1)] = jnp.sum(accumulate[s], axis=0, keepdims=True)


def run_messages(density, bone, fixed, load):
    depth, height, width = density.shape
    specs, arrays = [], []
    for array in (density, bone, fixed, load):
        lead = array.shape[:-3]
        for block in (0, depth // 2 - 1):
            spot = lambda _, block=block, lead=lead: (0,) * len(lead) + (block, 0, 0)
            specs.append(pl.BlockSpec(lead + (2, height, width), spot))
            arrays.append(array)
    return pl.pallas_call(
        message_kernel,
        grid=(1,),
        in_specs=specs,
        out_specs=[pl.BlockSpec((n, height, width), lambda _: (0, 0, 0)) for n in (5, 9)],
        out_shape=[jax.ShapeDtypeStruct((n, height, width), jnp.float32) for n in (5, 9)],
        name="messages",
    )(*arrays)


SCALAR = pl.BlockSpec(memory_space=pltpu.SMEM)
VECTOR = pl.BlockSpec(memory_space=pltpu.VMEM)


def run_prepare(place, density, bone, fixed, load):
    depth, _, width = density.shape
    swap = lax.axis_size("gx") == 2
    shapes = [(6, depth, width, LANES)]
    for layers in (depth, 2, 2):
        shapes += [(5, layers, 2, LANES)] * (1 if swap else 2)
    fields, *edges = pl.pallas_call(
        functools.partial(prepare_kernel, swap),
        in_specs=[SCALAR] + [VECTOR] * 4,
        out_specs=[VECTOR] * len(shapes),
        out_shape=[jax.ShapeDtypeStruct(s, jnp.float32) for s in shapes],
        name="prepare",
    )(place, density, bone, fixed, load)
    kinds = len(edges) // 3
    return fields, [edges[i * kinds : (i + 1) * kinds] for i in range(3)]


def run_krylov(table, place, fields, halos):
    depth, width = fields.shape[1], fields.shape[2]
    height = halos[0].shape[1]
    nx = lax.axis_size("gx")
    slabs = lax.axis_size("gy") * lax.axis_size("gz")
    rows = width + 3 * PAD
    shapes = [(3, depth, width, LANES)] * 3 + [(8, LANES)]
    shapes += [(3, depth, RAD, LANES)] * (1 if nx == 2 else 2)
    layers = [(depth + 4,), (3, depth + 3), (depth + 1,), (3, depth + 3), (depth + 1,)]
    layers += [(3, depth + 1)] * 3
    scratch = [pltpu.VMEM(lead + (rows, LANES), jnp.float32) for lead in layers]
    scratch += [
        pltpu.VMEM((18, depth, width, LANES), jnp.float32),
        pltpu.VMEM((8, 8, LANES), jnp.float32),
    ]
    cover_x = coverage(nx * width)[:, None]
    cover_y = np.pad(coverage(height), (0, LANES - height))[None]
    return pl.pallas_call(
        functools.partial(krylov_kernel, mode_constants(table), float(table[0, 0]), nx),
        in_specs=[SCALAR] * 2 + [VECTOR] * (len(halos) + 3),
        out_specs=[VECTOR] * len(shapes),
        out_shape=[jax.ShapeDtypeStruct(s, jnp.float32) for s in shapes],
        scratch_shapes=scratch,
        compiler_params=pltpu.CompilerParams(vmem_limit_bytes=56 * 1024 * 1024),
        name="krylov",
    )(place, jnp.asarray(coverage(slabs * depth)), fields, *halos, jnp.asarray(cover_x), jnp.asarray(cover_y))


def slab_route(steps, sideways=0):
    nx, ny, nz = (lax.axis_size(a) for a in ("gx", "gy", "gz"))
    pairs = []
    for x in range(nx):
        for slab in range(ny * nz):
            to, tx = slab + steps, x + sideways
            if 0 <= to < ny * nz and 0 <= tx < nx:
                spot = lambda i, s: (i * ny + s % ny) * nz + s // ny
                pairs.append((spot(x, slab), spot(tx, to)))
    return pairs


def to_slab(value, steps, sideways=0):
    return lax.ppermute(value, ("gx", "gy", "gz"), slab_route(steps, sideways))


def edges_swapped(low_edge, high_edge, steps):
    if lax.axis_size("gx") == 2:
        first = lax.axis_index("gx") == 0
        sent = jnp.where(first, high_edge, low_edge)
        spots = slab_route(steps, 1) + slab_route(steps, -1)
        got = lax.ppermute(sent, ("gx", "gy", "gz"), spots)
        none = jnp.zeros_like(got)
        return jnp.where(first, none, got), jnp.where(first, got, none)
    return to_slab(high_edge, steps, 1), to_slab(low_edge, steps, -1)


def edges_moved(sent, steps):
    if len(sent) == 1:
        spots = slab_route(steps, 1) + slab_route(steps, -1)
        got = lax.ppermute(sent[0], ("gx", "gy", "gz"), spots)
        return got, got
    return to_slab(sent[1], steps, 1), to_slab(sent[0], steps, -1)


def total_over_mesh(value):
    for axis in ("gz", "gy", "gx"):
        count = lax.axis_size(axis)
        if count & (count - 1):
            value = lax.psum(value, axis)
            continue
        step = 1
        while step < count:
            other = lax.ppermute(value, axis, [(i, i ^ step) for i in range(count)])
            value = value + other
            step *= 2
    return value


def inner_sum(values):
    return total_over_mesh(jnp.full((8, LANES), jnp.sum(values)))[0, 0]


def tap_table():
    offsets = np.abs(np.arange(2 * RAD + 1) - RAD)
    raw = np.exp(-offsets / (0.5 * RAD))
    return raw / raw.sum()


def banded(length_in, length_out, shift):
    taps = tap_table()
    matrix = np.zeros((length_in, length_out))
    for i in range(length_in):
        for o in range(length_out):
            distance = i - shift - o
            if abs(distance) <= RAD:
                matrix[i, o] = taps[distance + RAD]
    return matrix.astype(np.float32)


def coverage(length):
    ends = np.concatenate([[0.0], np.cumsum(tap_table())])
    position = np.arange(length)
    low = np.maximum(-RAD, -position) + RAD
    high = np.minimum(RAD, length - 1 - position) + RAD + 1
    return (ends[high] - ends[low]).astype(np.float32)


def depth_pieces(planar, low_plane, high_plane):
    depth = planar.shape[0]
    taps = tap_table()
    ratio = math.exp(-1.0 / (0.5 * RAD))
    pieces, blocks = [planar], [banded(depth, depth, 0)]
    near, far = [], []
    steps = 1
    while (steps - 1) * depth + 1 <= RAD:
        if steps * depth + depth - 1 <= RAD:
            away = steps * depth + np.arange(depth)
            near.append((high_plane, steps, taps[RAD] * ratio ** (away - (depth - 1))))
            away = steps * depth - np.arange(depth)
            near.append((low_plane, -steps, taps[RAD] * ratio ** away))
        else:
            far.append((steps, banded(depth, depth, steps * depth)))
            far.append((-steps, banded(depth, depth, -steps * depth)))
        steps += 1
    for move, block in far:
        pieces.append(to_slab(planar, move))
        blocks.append(block)
    for plane, move, weight in near:
        pieces.append(to_slab(plane, move)[None])
        blocks.append(weight[None].astype(np.float32))
    return pieces, blocks


def depth_decay(depth):
    return (math.exp(-1.0 / (0.5 * RAD)) ** np.arange(depth)).astype(np.float32)


def krylov_coefficients(sums):
    gamma, curve, mixed, curve_second = sums[0], 2.0 * sums[1], sums[2], 2.0 * sums[3]
    alpha = gamma / curve
    grown = alpha * mixed / curve
    beta = grown - 1.0
    bent = alpha * (alpha * (alpha * curve_second / gamma))
    rest = bent - grown * grown
    alpha_next = alpha * beta / rest
    by_first = alpha + alpha_next * grown
    by_second = -alpha_next * alpha
    squares = [by_first * by_first, 2.0 * by_first * by_second, by_second * by_second]
    parts = [f * s for f, s in zip(squares, sums[4:7])]
    total = parts[0] + parts[1] + parts[2]
    size = jnp.abs(parts[0]) + jnp.abs(parts[1]) + jnp.abs(parts[2])
    sound = (beta > GUARD * grown) & (rest > GUARD * bent) & (total > GUARD * size)
    return by_first, by_second, squares, total, jnp.where(sound, 1.0, 0.0)


def smooth_kernel(
    plain, cells, nx, place, stats, basis, left, right, along_x, along_y, planar, low, high, factors, verdict
):
    on_left = jnp.where(place[0] > 0, 1.0, 0.0)
    on_right = jnp.where(place[0] < nx - 1, 1.0, 0.0)
    depth = basis.shape[1]
    decay = depth_decay(depth)
    exact = dict(precision=lax.Precision.HIGHEST, preferred_element_type=jnp.float32)
    tile = stats[...]
    sums = [jnp.sum(tile[i : i + 1], axis=1, keepdims=True) for i in range(8)]
    if plain:
        one = jnp.ones((1, 1), jnp.float32)
        by_first, by_second, squares, total, sound = one, one, [one], sums[4], one
    else:
        by_first, by_second, squares, total, sound = krylov_coefficients(sums)
    scale = 1.0 / (total / cells + EPSILON)
    for i, value in enumerate((by_first, by_second, scale, sound)):
        factors[pl.ds(i, 1)] = jnp.broadcast_to(value, (1, LANES))
    factors[pl.ds(4, 4)] = jnp.zeros((4, LANES), jnp.float32)
    verdict[...] = sound
    for z in range(depth):
        wide = jnp.concatenate(
            [
                there * sum(f * v[i, z] for i, f in enumerate(squares))
                for v, there in ((left, on_left), (basis, 1.0), (right, on_right))
            ],
            axis=0,
        )
        half = lax.dot_general(along_x[...], wide, (((1,), (0,)), ((), ())), **exact)
        plane = lax.dot_general(along_y[...], half, (((1,), (1,)), ((), ())), **exact)
        planar[z] = plane
        for ref, weight in ((low, decay[z]), (high, decay[depth - 1 - z])):
            share = plane * float(weight)
            ref[...] = share if z == 0 else ref[...] + share


def run_smooth(plain, cells, place, stats, basis, sides, height):
    depth, width = basis.shape[1:3]
    along_x = banded(width + 2 * RAD, width, RAD).T
    along_y = np.zeros((height, LANES), np.float32)
    along_y[:, :height] = banded(height, height, 0).T
    shapes = ((depth, height, width), (height, width), (height, width), (8, LANES), (1, 1))
    return pl.pallas_call(
        functools.partial(smooth_kernel, plain, float(cells), lax.axis_size("gx")),
        in_specs=[SCALAR] + [VECTOR] * 6,
        out_specs=[VECTOR] * 5,
        out_shape=[jax.ShapeDtypeStruct(s, jnp.float32) for s in shapes],
        name="smooth",
    )(place, stats, basis, *sides, jnp.asarray(along_x), jnp.asarray(along_y))


def finish_kernel(blocks, factors, density, bone, *rest):
    pieces, out = rest[:-1], rest[-1]
    depth, height, _ = density.shape

    scale = factors[pl.ds(2, 1)]

    def chunk(index, carry):
        rows = pl.ds(pl.multiple_of(index * 8, 8), 8)
        totals = [None] * depth
        for piece, block in zip(pieces, blocks):
            for i in range(block.shape[0]):
                value = piece[i, rows]
                for o in range(depth):
                    if block[i, o] != 0.0:
                        term = value * float(block[i, o])
                        totals[o] = term if totals[o] is None else totals[o] + term
        for o in range(depth):
            share = REMODEL * bone[o, rows].astype(jnp.float32)
            moved = density[o, rows] + share * (totals[o] * scale - 1.0)
            out[o, rows] = jnp.clip(moved, FLOOR, CEILING)
        return carry

    lax.fori_loop(0, height // 8, chunk, 0)


def run_finish(factors, density, bone, pieces, blocks):
    return pl.pallas_call(
        functools.partial(finish_kernel, blocks),
        out_shape=jax.ShapeDtypeStruct(density.shape, jnp.float32),
        name="finish",
    )(factors, density, bone, *pieces)


def displacement_kernel(height, factors, first, second, out):
    by_first, by_second = factors[pl.ds(0, 1)], factors[pl.ds(1, 1)]

    def layer(z, carry):
        for i in range(3):
            moved = by_first * first[i, z] + by_second * second[i, z]
            out[i, z] = jnp.transpose(moved)[:height]
        return carry

    lax.fori_loop(0, first.shape[1], layer, 0)


def run_displacement(factors, first, second, height):
    depth, width = first.shape[1:3]
    return pl.pallas_call(
        functools.partial(displacement_kernel, height),
        out_shape=jax.ShapeDtypeStruct((3, depth, height, width), jnp.float32),
        name="displacement",
    )(factors, first, second)


def corners():
    return [(cz, cy, cx) for cz in range(2) for cy in range(2) for cx in range(2)]


def upper_nodes(field):
    column = lax.ppermute(field[:, :, :, :1], ("gx", "gy", "gz"), slab_route(0, -1))
    wide = jnp.concatenate([field, column], axis=3)
    wide = jnp.concatenate([wide, to_slab(wide[:, :1], -1)], axis=1)
    return jnp.pad(wide, ((0, 0), (0, 0), (0, 1), (0, 0)))


def fold_upper(values):
    depth, width = values.shape[1] - 1, values.shape[3] - 1
    carried = to_slab(values[:, depth:], 1)
    values = jnp.concatenate([values[:, :1] + carried, values[:, 1:depth]], axis=1)
    column = lax.ppermute(values[:, :, :, width:], ("gx", "gy", "gz"), slab_route(0, 1))
    return jnp.concatenate([values[:, :, :, :1] + column, values[:, :, :, 1:width]], axis=3)


def corner_columns(nodes, shape):
    depth, height, width = shape
    return jnp.stack(
        [
            nodes[c, cz : cz + depth, cy : cy + height, cx : cx + width]
            for c in range(3)
            for cz, cy, cx in corners()
        ]
    )


def element_products(columns, table):
    return jnp.einsum(
        "rc,czyx->rzyx", jnp.asarray(table, jnp.float32), columns, precision=lax.Precision.HIGHEST
    )


def spread_corner(values, corner):
    return jnp.pad(values, ((0, 0),) + tuple((c, 1 - c) for c in corner))


def plain_forces(field, modulus, table):
    _, height, _ = modulus.shape
    columns = corner_columns(upper_nodes(field), modulus.shape)
    products = element_products(columns, table) * modulus
    products = products.reshape((3, 8) + modulus.shape)
    total = sum(spread_corner(products[:, node], corner) for node, corner in enumerate(corners()))
    return fold_upper(total[:, :, :height])


def plain_path(table, fields, height):
    modulus, *force, free, density = jnp.swapaxes(fields[..., :height], 2, 3)
    _, height, _ = density.shape
    spread = sum(spread_corner(modulus[None], corner) for corner in corners())
    precondition = free / (float(table[0, 0]) * fold_upper(spread[:, :, :height]))
    residual = jnp.stack(force)
    search = precondition * residual
    start = (jnp.zeros_like(residual), residual, search, inner_sum(residual * search))

    def iterate(_, state):
        moved, residual, search, gamma = state
        image = free * plain_forces(free * search, modulus, table)
        alpha = gamma / inner_sum(search * image)
        moved = moved + alpha * search
        residual = residual - alpha * image
        scaled = precondition * residual
        gamma_next = inner_sum(residual * scaled)
        return moved, residual, scaled + gamma_next / gamma * search, gamma_next

    moved = lax.fori_loop(0, ITERS, iterate, start)[0]
    columns = corner_columns(upper_nodes(moved), modulus.shape)
    energy = 0.5 * modulus * jnp.sum(columns * element_products(columns, table), axis=0)
    specific = jnp.swapaxes(energy / density, 1, 2)
    return jnp.pad(specific, ((0, 0), (0, 0), (0, LANES - height))), moved


def side_halos(basis):
    width = basis.shape[2]
    return edges_swapped(basis[:, :, :RAD], basis[:, :, width - RAD :], 0)


def remodelled(plain, cells, place, density, bone, stats, basis, sides):
    planar, low, high, factors, verdict = run_smooth(plain, cells, place, stats, basis, sides, density.shape[1])
    pieces, blocks = depth_pieces(planar, low, high)
    return run_finish(factors, density, bone, pieces, blocks), factors, verdict


def on_device(density, bone, fixed, load):
    table = element_stiffness()
    density, bone, fixed, load = density[0], bone[0], fixed[0], load[:, 0]
    depth, height, width = density.shape
    slabs = lax.axis_size("gy") * lax.axis_size("gz")
    slab = lax.axis_index("gz") * lax.axis_size("gy") + lax.axis_index("gy")
    nx = lax.axis_size("gx")
    cells = density.size * nx * slabs
    place = jnp.stack([lax.axis_index("gx"), slab]).astype(jnp.int32)

    up, down = run_messages(density, bone, fixed, load)
    got_up = to_slab(up, 1)
    got_down = to_slab(down, -1)
    fields, edges = run_prepare(place, density, bone, fixed, load)
    around = [side for sent, steps in zip(edges, (0, 1, -1)) for side in edges_moved(sent, steps)]
    first, second, basis, stats, *ends = run_krylov(
        table, place, fields, (got_up, got_down, *around)
    )
    sides = edges_moved(ends, 0)
    stats = total_over_mesh(stats)
    updated, factors, verdict = remodelled(False, cells, place, density, bone, stats, basis, sides)
    moved = run_displacement(factors, first, second, height)

    shares = bone.reshape(-1, width)

    def repeated(state):
        specific, moved = plain_path(table, fields, height)
        thick = jnp.swapaxes(fields[5, ..., :height], 1, 2)
        cover = lambda length, start, count: lax.dynamic_slice(
            jnp.asarray(coverage(length)), (start,), (count,)
        )
        cover_x = cover(nx * width, place[0] * width, width)
        cover_z = cover(slabs * depth, place[1] * depth, depth)
        spread = cover_z[:, None, None] * cover_x[:, None] * jnp.asarray(coverage(height))
        total = inner_sum(specific[..., :height] * spread)
        row, lane = (lax.broadcasted_iota(jnp.int32, (8, LANES), i) for i in range(2))
        tile = jnp.where((row == 4) & (lane == 0), total, 0.0)
        again = specific[None]
        updated = remodelled(
            True, cells, place, thick, shares.reshape(bone.shape), tile, again, side_halos(again)
        )[0]
        return True, updated, moved.reshape(-1, width)

    sound = verdict.reshape(()) > 0.5
    _, updated, moved = lax.while_loop(lambda state: ~state[0], repeated, (sound, updated, moved.reshape(-1, width)))
    return updated[None], moved.reshape(3, 1, depth, height, width)


def solution(mesh):
    placed = (
        P("gz", "gy", None, "gx"),
        P("gz", "gy", None, "gx"),
        P("gz", "gy", None, "gx"),
        P(None, "gz", "gy", None, "gx"),
    )
    return jax.shard_map(
        on_device,
        mesh=mesh,
        in_specs=placed,
        out_specs=(P("gz", "gy", None, "gx"), P(None, "gz", "gy", None, "gx")),
        check_vma=False,
    )
```

```python
import functools
import math

import jax
import jax.numpy as jnp
import numpy as np
from jax import lax
from jax.experimental import pallas as pl
from jax.experimental.pallas import tpu as pltpu
from jax.sharding import PartitionSpec as P


RAD = 24
ITERS = 2

MARROW = 0.1
REMODEL = 0.25
FLOOR = 0.2
CEILING = 1.0
EPSILON = 1e-06

LANES = 128
PAD = 8
GUARD = 0.01


def element_stiffness():
    poisson = 0.3
    lame = poisson / ((1.0 + poisson) * (1.0 - 2.0 * poisson))
    shear = 0.5 / (1.0 + poisson)
    elastic = np.zeros((6, 6))
    elastic[:3, :3] = lame
    for index in range(3):
        elastic[index, index] += 2.0 * shear
        elastic[index + 3, index + 3] = shear
    points = [0.5 - 0.5 / math.sqrt(3.0), 0.5 + 0.5 / math.sqrt(3.0)]
    matrix = np.zeros((24, 24))
    for point_z in points:
        for point_y in points:
            for point_x in points:
                strain = np.zeros((6, 24))
                for corner_z in range(2):
                    for corner_y in range(2):
                        for corner_x in range(2):
                            node = 4 * corner_z + 2 * corner_y + corner_x
                            shape_x = point_x if corner_x else 1.0 - point_x
                            shape_y = point_y if corner_y else 1.0 - point_y
                            shape_z = point_z if corner_z else 1.0 - point_z
                            slope_x = 1.0 if corner_x else -1.0
                            slope_y = 1.0 if corner_y else -1.0
                            slope_z = 1.0 if corner_z else -1.0
                            along_x = slope_x * shape_y * shape_z
                            along_y = shape_x * slope_y * shape_z
                            along_z = shape_x * shape_y * slope_z
                            strain[0, node] = along_x
                            strain[1, 8 + node] = along_y
                            strain[2, 16 + node] = along_z
                            strain[3, node] = along_y
                            strain[3, 8 + node] = along_x
                            strain[4, 8 + node] = along_z
                            strain[4, 16 + node] = along_y
                            strain[5, node] = along_z
                            strain[5, 16 + node] = along_x
                matrix = matrix + strain.T @ elastic @ strain / 8.0
    return matrix


X, Y, Z, XY, XZ, YZ, XYZ = 1, 2, 4, 3, 5, 6, 7
U, V, W = 0, 1, 2
REDUCED = [
    [(U, X)], [(V, Y)], [(W, Z)],
    [(U, Y), (V, X)], [(U, Z), (W, X)], [(V, Z), (W, Y)],
    [(V, XY)], [(W, XZ)], [(U, XY)], [(W, YZ)], [(U, XZ)], [(V, YZ)],
    [(U, YZ)], [(V, XZ)], [(W, XY)],
    [(U, XYZ)], [(V, XYZ)], [(W, XYZ)],
]


def mode_constants(table):
    one = np.array([[1.0, 1.0], [-1.0, 1.0]])
    sums = np.kron(one, np.kron(one, one))
    change = np.kron(np.eye(3), sums)
    modes = change @ table @ change.T / 64.0
    at = lambda a, b: float(modes[a[0] * 8 + a[1], b[0] * 8 + b[1]])
    k = dict(
        cross=at((U, X), (V, Y)),
        shear=at((U, Y), (U, Y)),
        pair=at((V, XY), (W, XZ)),
        group=at((U, YZ), (V, XZ)),
        triple=at((U, XYZ), (U, XYZ)),
    )
    k["normal"] = at((U, X), (U, X)) - k["cross"]
    k["single"] = at((V, XY), (V, XY)) - k["pair"]
    reduce = np.zeros((18, 24))
    for row, members in enumerate(REDUCED):
        for component, bits in members:
            reduce[row, component * 8 + bits] = 1.0
    small = np.stack([np.array(stresses(list(unit), k)) for unit in np.eye(18)], axis=1)
    assert np.allclose(reduce.T @ small @ reduce, modes, atol=1e-12)
    assert np.allclose(np.diagonal(table), table[0, 0], atol=1e-12)
    return k


def stresses(m, k):
    trace = k["cross"] * (m[0] + m[1] + m[2])
    out = [trace + k["normal"] * m[i] for i in range(3)]
    out += [k["shear"] * m[i] for i in range(3, 6)]
    for i in (6, 8, 10):
        both = k["pair"] * (m[i] + m[i + 1])
        out += [both + k["single"] * m[i], both + k["single"] * m[i + 1]]
    total = m[12] + m[13] + m[14]
    out += [k["group"] * (total + m[i]) for i in range(12, 15)]
    out += [k["triple"] * m[i] for i in range(15, 18)]
    return out


def dotted(a, b):
    terms = [p * q for p, q in zip(a, b)]
    while len(terms) > 1:
        terms = [terms[i] + terms[i + 1] if i + 1 < len(terms) else terms[i] for i in range(0, len(terms), 2)]
    return terms[0]


def layer_modes(ref, index, row):
    found = []
    for component in range(3):
        low = ref[component, index, pl.ds(row, 8), :]
        high = ref[component, index, pl.ds(row + 1, 8), :]
        both, slope = low + high, high - low
        both_up, slope_up = (pltpu.roll(v, LANES - 1, 1) for v in (both, slope))
        found.append((both + both_up, slope + slope_up, both_up - both, slope_up - slope))
    return found


def voxel_modes(below, above):
    modes = {}
    for component in range(3):
        low, high = below[component], above[component]
        for bits in (X, Y, XY):
            modes[component, bits] = low[bits] + high[bits]
        for bits in (0, X, Y, XY):
            modes[component, bits + Z] = high[bits] - low[bits]
    reduced = []
    for members in REDUCED:
        value = modes[members[0]]
        for extra in members[1:]:
            value = value + modes[extra]
        reduced.append(value)
    return reduced


SLOT = {mode: row for row, members in enumerate(REDUCED) for mode in members}


def raw_layer(density, bone, fixed, load, z):
    thick = density[z]
    share = bone[z].astype(jnp.float32)
    free = 1.0 - fixed[z].astype(jnp.float32)
    modulus = share * thick * thick + (1.0 - share) * MARROW
    return modulus, [free * load[c, z] for c in range(3)], free, thick


def message_kernel(*refs):
    lowest, highest, (up, down) = refs[:8:2], refs[1:8:2], refs[8:]
    up[0] = raw_layer(*highest, 0)[0]
    modulus, force, _, _ = raw_layer(*highest, 1)
    up[1] = modulus
    for c in range(3):
        up[2 + c] = force[c]
    for z in range(2):
        modulus, force, free, _ = raw_layer(*lowest, z)
        down[z] = modulus
        for c in range(3):
            down[2 + 3 * z + c] = force[c]
        if z == 0:
            down[8] = free


def prepare_kernel(swap, place, density, bone, fixed, load, fields, *edges):
    depth, height, width = density.shape
    zeros = jnp.zeros((LANES - height, width), jnp.float32)
    first = place[0] == 0
    kinds = len(edges) // 3
    for z in range(depth):
        modulus, force, free, thick = raw_layer(density, bone, fixed, load, z)
        for slot, value in enumerate([modulus] + force + [free, thick]):
            turned = jnp.transpose(jnp.concatenate([value, zeros], axis=0))
            fields[slot, z] = turned
            if slot == 5:
                continue
            low, high = turned[:2], turned[width - 2 :]
            sent = (jnp.where(first, high, low),) if swap else (low, high)
            for kind in range(kinds):
                edges[kind][slot, z] = sent[kind]
                if z >= depth - 2:
                    edges[kinds + kind][slot, z - (depth - 2)] = sent[kind]
                if z < 2:
                    edges[2 * kinds + kind][slot, z] = sent[kind]


def krylov_kernel(
    k, kappa, across,
    place, cover_z, fields, up, down, left, right, left_up, right_up, left_down, right_down,
    cover_x, cover_y,
    *rest,
):
    out_p, out_w, out_g, out_stats = rest[:4]
    out_edges, rest = rest[4:-10], rest[-10:]
    mod, force, free, search, inverse, lower, upper, image, stress, accumulate = rest
    on_left = jnp.where(place[0] > 0, 1.0, 0.0)
    on_right = jnp.where(place[0] < across - 1, 1.0, 0.0)
    depth, width = fields.shape[1], fields.shape[2]
    height = up.shape[1]
    first, last = PAD, PAD + width
    chunks = width // 8
    blank = jnp.zeros((LANES - height, width), jnp.float32)

    def turned(value):
        return jnp.transpose(jnp.concatenate([value, blank], axis=0))

    empty = jnp.zeros((PAD, LANES), jnp.float32)
    for ref in (mod, force, search):
        lead = ref.shape[:-2]
        for spot in np.ndindex(*lead):
            ref[spot + (pl.ds(0, PAD),)] = empty
            ref[spot + (pl.ds(last, PAD),)] = empty
            ref[spot + (pl.ds(last + PAD, PAD),)] = empty
    for z in range(depth + 1):
        free[z, pl.ds(last, PAD)] = empty

    def local(z, carry):
        for c in range(chunks):
            rows, into = pl.ds(8 * c, 8), pl.ds(first + 8 * c, 8)
            mod[z + 2, into] = fields[0, z, rows]
            for i in range(3):
                force[i, z + 1, into] = fields[1 + i, z, rows]
            free[z, into] = fields[4, z, rows]
        mod[z + 2, pl.ds(first - 2, 2)] = left[0, z] * on_left
        mod[z + 2, pl.ds(last, 2)] = right[0, z] * on_right
        for i in range(3):
            force[i, z + 1, pl.ds(first - 2, 2)] = left[1 + i, z] * on_left
            force[i, z + 1, pl.ds(last, 2)] = right[1 + i, z] * on_right
        free[z, pl.ds(last, 2)] = right[4, z] * on_right
        return carry

    lax.fori_loop(0, depth, local, 0)
    body = pl.ds(first, width)
    for z in range(2):
        mod[z, body] = turned(up[z])
        mod[depth + 2 + z, body] = turned(down[z])
        for side, low, high, there in (
            (first - 2, left_up, left_down, on_left),
            (last, right_up, right_down, on_right),
        ):
            mod[z, pl.ds(side, 2)] = low[0, z] * there
            mod[depth + 2 + z, pl.ds(side, 2)] = high[0, z] * there
    for i in range(3):
        force[i, 0, body] = turned(up[2 + i])
        for side, low, high, there in (
            (first - 2, left_up, left_down, on_left),
            (last, right_up, right_down, on_right),
        ):
            force[i, 0, pl.ds(side, 2)] = low[1 + i, 1] * there
            for z in range(2):
                force[i, depth + 1 + z, pl.ds(side, 2)] = high[1 + i, z] * there
        for z in range(2):
            force[i, depth + 1 + z, body] = turned(down[2 + 3 * z + i])
    free[depth, body] = turned(down[8])
    free[depth, pl.ds(last, 2)] = right_down[4, 0] * on_right

    def divide(chunk, carry):
        row = pl.multiple_of(chunk * 8, 8)
        previous = None
        for z in range(depth + 4):
            here = mod[z, pl.ds(row + PAD, 8)] + mod[z, pl.ds(row + PAD - 1, 8)]
            here = here + pltpu.roll(here, 1, 1)
            if z >= 1 and z <= depth + 3:
                total = kappa * (here + previous)
                share = jnp.where(total > 0.0, 1.0 / jnp.where(total > 0.0, total, 1.0), 0.0)
                node = z - 1
                for i in range(3):
                    search[i, node, pl.ds(row + PAD, 8)] = force[i, node, pl.ds(row + PAD, 8)] * share
                if 1 <= node <= depth + 1:
                    inverse[node - 1, pl.ds(row + PAD, 8)] = free[node - 1, pl.ds(row + PAD, 8)] * share
            previous = here
        return carry

    lax.fori_loop(0, chunks + 1, divide, 0)
    for z in range(depth + 3):
        side = mod[z, pl.ds(0, 8)]
        if z + 1 < depth + 4:
            total = side + mod[z + 1, pl.ds(0, 8)]
            total = total + pltpu.roll(total, 1, 0)
            total = kappa * (total + pltpu.roll(total, 1, 1))
            share = jnp.where(total > 0.0, 1.0 / jnp.where(total > 0.0, total, 1.0), 0.0)
            for i in range(3):
                search[i, z, pl.ds(0, 8)] = force[i, z, pl.ds(0, 8)] * share

    for s in range(accumulate.shape[0]):
        accumulate[s] = jnp.zeros((8, LANES), jnp.float32)

    def elements(row, inner):
        below = layer_modes(search, 0, row)
        carried = None
        for node in range(1, depth + 3):
            above = layer_modes(search, node, row)
            modes = voxel_modes(below, above)
            strain = stresses(modes, k)
            scale = mod[node, pl.ds(row, 8)]
            voxel = node - 2
            if inner is not None and 0 <= voxel < depth:
                rows = pl.ds(row - PAD, 8)
                work = (0.5 * scale) * dotted(modes, strain)
                out_g[0, voxel, rows] = work
                for s in range(18):
                    stress[s, voxel, rows] = strain[s]
            strain = [scale * s for s in strain]
            carry = []
            for component in range(3):
                value = lambda bits: strain[SLOT[component, bits]]
                totals, tops = [], []
                for bits in (0, X, Y, XY):
                    slope = value(bits + Z)
                    low, high = (-slope, slope) if bits == 0 else (value(bits) - slope, value(bits) + slope)
                    tops.append(high)
                    if carried is not None:
                        totals.append(low + carried[component][len(totals)])
                carry.append(tops)
                if carried is not None:
                    plain = (totals[0] - totals[2]) + pltpu.roll(totals[0] + totals[2], 1, 1)
                    tilted = (totals[1] - totals[3]) + pltpu.roll(totals[1] + totals[3], 1, 1)
                    lower[component, voxel, pl.ds(row, 8)] = plain - tilted
                    upper[component, voxel, pl.ds(row, 8)] = plain + tilted
            carried = carry
            below = above

    def middle(chunk, carry):
        elements(pl.multiple_of(PAD + chunk * 8, 8), True)
        return carry

    elements(0, None)
    lax.fori_loop(0, chunks, middle, 0)
    elements(last, None)

    def gather(chunk, carry):
        row = pl.multiple_of(PAD + chunk * 8, 8)
        rows = pl.ds(row, 8)
        gamma, second = jnp.zeros((8, LANES), jnp.float32), jnp.zeros((8, LANES), jnp.float32)
        for node in range(depth + 1):
            share = inverse[node, rows]
            for i in range(3):
                pulled = lower[i, node, rows] + upper[i, node, pl.ds(row - 1, 8)]
                scaled = share * pulled
                image[i, node, rows] = scaled
                if node < depth:
                    second = second + scaled * pulled
                    gamma = gamma + force[i, node + 1, rows] * search[i, node + 1, rows]
        accumulate[0] = accumulate[0] + jnp.where(chunk < chunks, gamma, 0.0)
        accumulate[2] = accumulate[2] + jnp.where(chunk < chunks, second, 0.0)
        return carry

    lax.fori_loop(0, chunks + 1, gather, 0)

    def energies(chunk, carry):
        row = pl.multiple_of(PAD + chunk * 8, 8)
        rows = pl.ds(pl.multiple_of(chunk * 8, 8), 8)
        across_rows = pl.ds(pl.multiple_of(place[0] * width + chunk * 8, 8), 8)
        weight = cover_x[across_rows] * cover_y[...]
        sums = [jnp.zeros((8, LANES), jnp.float32) for _ in range(5)]
        below = layer_modes(image, 0, row)
        for voxel in range(depth):
            above = layer_modes(image, voxel + 1, row)
            modes = voxel_modes(below, above)
            half = 0.5 * mod[voxel + 2, pl.ds(row, 8)]
            first_work = out_g[0, voxel, rows]
            mixed = half * dotted(modes, [stress[s, voxel, rows] for s in range(18)])
            second_work = half * dotted(modes, stresses(modes, k))
            thick = fields[5, voxel, rows]
            flip = jnp.where(thick > 0.0, 1.0 / jnp.where(thick > 0.0, thick, 1.0), 0.0)
            spread = weight * cover_z[place[1] * depth + voxel]
            sums[0] = sums[0] + first_work
            sums[1] = sums[1] + second_work
            for i, work in enumerate((first_work, mixed, second_work)):
                value = work * flip
                out_g[i, voxel, rows] = value
                sums[2 + i] = sums[2 + i] + spread * value
            below = above
            for i in range(3):
                out_p[i, voxel, rows] = search[i, voxel + 1, pl.ds(row, 8)]
                out_w[i, voxel, rows] = image[i, voxel, pl.ds(row, 8)]
        for slot, value in zip((1, 3, 4, 5, 6), sums):
            accumulate[slot] = accumulate[slot] + value
        return carry

    lax.fori_loop(0, chunks, energies, 0)
    for i in range(3):
        for z in range(depth):
            low, high = out_g[i, z, pl.ds(0, RAD)], out_g[i, z, pl.ds(width - RAD, RAD)]
            sent = (jnp.where(place[0] == 0, high, low),) if len(out_edges) == 1 else (low, high)
            for ref, value in zip(out_edges, sent):
                ref[i, z] = value
    for s in range(8):
        out_stats[pl.ds(s, 1)] = jnp.sum(accumulate[s], axis=0, keepdims=True)


def run_messages(density, bone, fixed, load):
    depth, height, width = density.shape
    specs, arrays = [], []
    for array in (density, bone, fixed, load):
        lead = array.shape[:-3]
        for block in (0, depth // 2 - 1):
            spot = lambda _, block=block, lead=lead: (0,) * len(lead) + (block, 0, 0)
            specs.append(pl.BlockSpec(lead + (2, height, width), spot))
            arrays.append(array)
    return pl.pallas_call(
        message_kernel,
        grid=(1,),
        in_specs=specs,
        out_specs=[pl.BlockSpec((n, height, width), lambda _: (0, 0, 0)) for n in (5, 9)],
        out_shape=[jax.ShapeDtypeStruct((n, height, width), jnp.float32) for n in (5, 9)],
        name="messages",
    )(*arrays)


SCALAR = pl.BlockSpec(memory_space=pltpu.SMEM)
VECTOR = pl.BlockSpec(memory_space=pltpu.VMEM)


def run_prepare(place, density, bone, fixed, load):
    depth, _, width = density.shape
    swap = lax.axis_size("gx") == 2
    shapes = [(6, depth, width, LANES)]
    for layers in (depth, 2, 2):
        shapes += [(5, layers, 2, LANES)] * (1 if swap else 2)
    fields, *edges = pl.pallas_call(
        functools.partial(prepare_kernel, swap),
        in_specs=[SCALAR] + [VECTOR] * 4,
        out_specs=[VECTOR] * len(shapes),
        out_shape=[jax.ShapeDtypeStruct(s, jnp.float32) for s in shapes],
        name="prepare",
    )(place, density, bone, fixed, load)
    kinds = len(edges) // 3
    return fields, [edges[i * kinds : (i + 1) * kinds] for i in range(3)]


def run_krylov(table, place, fields, halos):
    depth, width = fields.shape[1], fields.shape[2]
    height = halos[0].shape[1]
    nx = lax.axis_size("gx")
    slabs = lax.axis_size("gy") * lax.axis_size("gz")
    rows = width + 3 * PAD
    shapes = [(3, depth, width, LANES)] * 3 + [(8, LANES)]
    shapes += [(3, depth, RAD, LANES)] * (1 if nx == 2 else 2)
    layers = [(depth + 4,), (3, depth + 3), (depth + 1,), (3, depth + 3), (depth + 1,)]
    layers += [(3, depth + 1)] * 3
    scratch = [pltpu.VMEM(lead + (rows, LANES), jnp.float32) for lead in layers]
    scratch += [
        pltpu.VMEM((18, depth, width, LANES), jnp.float32),
        pltpu.VMEM((8, 8, LANES), jnp.float32),
    ]
    cover_x = coverage(nx * width)[:, None]
    cover_y = np.pad(coverage(height), (0, LANES - height))[None]
    return pl.pallas_call(
        functools.partial(krylov_kernel, mode_constants(table), float(table[0, 0]), nx),
        in_specs=[SCALAR] * 2 + [VECTOR] * (len(halos) + 3),
        out_specs=[VECTOR] * len(shapes),
        out_shape=[jax.ShapeDtypeStruct(s, jnp.float32) for s in shapes],
        scratch_shapes=scratch,
        compiler_params=pltpu.CompilerParams(vmem_limit_bytes=56 * 1024 * 1024),
        name="krylov",
    )(place, jnp.asarray(coverage(slabs * depth)), fields, *halos, jnp.asarray(cover_x), jnp.asarray(cover_y))


def slab_route(steps, sideways=0):
    nx, ny, nz = (lax.axis_size(a) for a in ("gx", "gy", "gz"))
    pairs = []
    for x in range(nx):
        for slab in range(ny * nz):
            to, tx = slab + steps, x + sideways
            if 0 <= to < ny * nz and 0 <= tx < nx:
                spot = lambda i, s: (i * ny + s % ny) * nz + s // ny
                pairs.append((spot(x, slab), spot(tx, to)))
    return pairs


def to_slab(value, steps, sideways=0):
    return lax.ppermute(value, ("gx", "gy", "gz"), slab_route(steps, sideways))


def edges_swapped(low_edge, high_edge, steps):
    if lax.axis_size("gx") == 2:
        first = lax.axis_index("gx") == 0
        sent = jnp.where(first, high_edge, low_edge)
        spots = slab_route(steps, 1) + slab_route(steps, -1)
        got = lax.ppermute(sent, ("gx", "gy", "gz"), spots)
        none = jnp.zeros_like(got)
        return jnp.where(first, none, got), jnp.where(first, got, none)
    return to_slab(high_edge, steps, 1), to_slab(low_edge, steps, -1)


def edges_moved(sent, steps):
    if len(sent) == 1:
        spots = slab_route(steps, 1) + slab_route(steps, -1)
        got = lax.ppermute(sent[0], ("gx", "gy", "gz"), spots)
        return got, got
    return to_slab(sent[1], steps, 1), to_slab(sent[0], steps, -1)


def total_over_mesh(value):
    for axis in ("gz", "gy", "gx"):
        count = lax.axis_size(axis)
        if count & (count - 1):
            value = lax.psum(value, axis)
            continue
        step = 1
        while step < count:
            other = lax.ppermute(value, axis, [(i, i ^ step) for i in range(count)])
            value = value + other
            step *= 2
    return value


def inner_sum(values):
    return total_over_mesh(jnp.full((8, LANES), jnp.sum(values)))[0, 0]


def tap_table():
    offsets = np.abs(np.arange(2 * RAD + 1) - RAD)
    raw = np.exp(-offsets / (0.5 * RAD))
    return raw / raw.sum()


def banded(length_in, length_out, shift):
    taps = tap_table()
    matrix = np.zeros((length_in, length_out))
    for i in range(length_in):
        for o in range(length_out):
            distance = i - shift - o
            if abs(distance) <= RAD:
                matrix[i, o] = taps[distance + RAD]
    return matrix.astype(np.float32)


def coverage(length):
    ends = np.concatenate([[0.0], np.cumsum(tap_table())])
    position = np.arange(length)
    low = np.maximum(-RAD, -position) + RAD
    high = np.minimum(RAD, length - 1 - position) + RAD + 1
    return (ends[high] - ends[low]).astype(np.float32)


def depth_pieces(planar, low_plane, high_plane):
    depth = planar.shape[0]
    taps = tap_table()
    ratio = math.exp(-1.0 / (0.5 * RAD))
    pieces, blocks = [planar], [banded(depth, depth, 0)]
    near, far = [], []
    steps = 1
    while (steps - 1) * depth + 1 <= RAD:
        if steps * depth + depth - 1 <= RAD:
            away = steps * depth + np.arange(depth)
            near.append((high_plane, steps, taps[RAD] * ratio ** (away - (depth - 1))))
            away = steps * depth - np.arange(depth)
            near.append((low_plane, -steps, taps[RAD] * ratio ** away))
        else:
            far.append((steps, banded(depth, depth, steps * depth)))
            far.append((-steps, banded(depth, depth, -steps * depth)))
        steps += 1
    for move, block in far:
        pieces.append(to_slab(planar, move))
        blocks.append(block)
    for plane, move, weight in near:
        pieces.append(to_slab(plane, move)[None])
        blocks.append(weight[None].astype(np.float32))
    return pieces, blocks


def depth_decay(depth):
    return (math.exp(-1.0 / (0.5 * RAD)) ** np.arange(depth)).astype(np.float32)


def krylov_coefficients(sums):
    gamma, curve, mixed, curve_second = sums[0], 2.0 * sums[1], sums[2], 2.0 * sums[3]
    alpha = gamma / curve
    grown = alpha * mixed / curve
    beta = grown - 1.0
    bent = alpha * (alpha * (alpha * curve_second / gamma))
    rest = bent - grown * grown
    alpha_next = alpha * beta / rest
    by_first = alpha + alpha_next * grown
    by_second = -alpha_next * alpha
    squares = [by_first * by_first, 2.0 * by_first * by_second, by_second * by_second]
    parts = [f * s for f, s in zip(squares, sums[4:7])]
    total = parts[0] + parts[1] + parts[2]
    size = jnp.abs(parts[0]) + jnp.abs(parts[1]) + jnp.abs(parts[2])
    sound = (beta > GUARD * grown) & (rest > GUARD * bent) & (total > GUARD * size)
    return by_first, by_second, squares, total, jnp.where(sound, 1.0, 0.0)


def split(value):
    high = value.astype(jnp.bfloat16)
    return high, (value - high.astype(jnp.float32)).astype(jnp.bfloat16)


def split_dot(a, b, side):
    dot = lambda p, q: lax.dot_general(
        p, q, (((1,), (side,)), ((), ())), preferred_element_type=jnp.float32
    )
    return dot(a[0], b[0]) + (dot(a[0], b[1]) + dot(a[1], b[0]))


def smooth_kernel(
    plain, cells, nx, place, stats, basis, left, right, along_x, along_y, planar, low, high, factors, verdict
):
    on_left = jnp.where(place[0] > 0, 1.0, 0.0)
    on_right = jnp.where(place[0] < nx - 1, 1.0, 0.0)
    depth = basis.shape[1]
    decay = depth_decay(depth)
    matrix_x, matrix_y = split(along_x[...]), split(along_y[...])
    tile = stats[...]
    sums = [jnp.sum(tile[i : i + 1], axis=1, keepdims=True) for i in range(8)]
    if plain:
        one = jnp.ones((1, 1), jnp.float32)
        by_first, by_second, squares, total, sound = one, one, [one], sums[4], one
    else:
        by_first, by_second, squares, total, sound = krylov_coefficients(sums)
    scale = 1.0 / (total / cells + EPSILON)
    for i, value in enumerate((by_first, by_second, scale, sound)):
        factors[pl.ds(i, 1)] = jnp.broadcast_to(value, (1, LANES))
    factors[pl.ds(4, 4)] = jnp.zeros((4, LANES), jnp.float32)
    verdict[...] = sound
    for z in range(depth):
        wide = jnp.concatenate(
            [
                there * sum(f * v[i, z] for i, f in enumerate(squares))
                for v, there in ((left, on_left), (basis, 1.0), (right, on_right))
            ],
            axis=0,
        )
        half = split_dot(matrix_x, split(wide), 0)
        plane = split_dot(matrix_y, split(half), 1)
        planar[z] = plane
        for ref, weight in ((low, decay[z]), (high, decay[depth - 1 - z])):
            share = plane * float(weight)
            ref[...] = share if z == 0 else ref[...] + share


def run_smooth(plain, cells, place, stats, basis, sides, height):
    depth, width = basis.shape[1:3]
    along_x = banded(width + 2 * RAD, width, RAD).T
    along_y = np.zeros((height, LANES), np.float32)
    along_y[:, :height] = banded(height, height, 0).T
    shapes = ((depth, height, width), (height, width), (height, width), (8, LANES), (1, 1))
    return pl.pallas_call(
        functools.partial(smooth_kernel, plain, float(cells), lax.axis_size("gx")),
        in_specs=[SCALAR] + [VECTOR] * 6,
        out_specs=[VECTOR] * 5,
        out_shape=[jax.ShapeDtypeStruct(s, jnp.float32) for s in shapes],
        name="smooth",
    )(place, stats, basis, *sides, jnp.asarray(along_x), jnp.asarray(along_y))


def finish_kernel(blocks, factors, density, bone, *rest):
    pieces, out = rest[:-1], rest[-1]
    depth, height, _ = density.shape

    scale = factors[pl.ds(2, 1)]

    def chunk(index, carry):
        rows = pl.ds(pl.multiple_of(index * 8, 8), 8)
        totals = [None] * depth
        for piece, block in zip(pieces, blocks):
            for i in range(block.shape[0]):
                value = piece[i, rows]
                for o in range(depth):
                    if block[i, o] != 0.0:
                        term = value * float(block[i, o])
                        totals[o] = term if totals[o] is None else totals[o] + term
        for o in range(depth):
            share = REMODEL * bone[o, rows].astype(jnp.float32)
            moved = density[o, rows] + share * (totals[o] * scale - 1.0)
            out[o, rows] = jnp.clip(moved, FLOOR, CEILING)
        return carry

    lax.fori_loop(0, height // 8, chunk, 0)


def run_finish(factors, density, bone, pieces, blocks):
    return pl.pallas_call(
        functools.partial(finish_kernel, blocks),
        out_shape=jax.ShapeDtypeStruct(density.shape, jnp.float32),
        name="finish",
    )(factors, density, bone, *pieces)


def displacement_kernel(height, factors, first, second, out):
    by_first, by_second = factors[pl.ds(0, 1)], factors[pl.ds(1, 1)]

    def layer(z, carry):
        for i in range(3):
            moved = by_first * first[i, z] + by_second * second[i, z]
            out[i, z] = jnp.transpose(moved)[:height]
        return carry

    lax.fori_loop(0, first.shape[1], layer, 0)


def run_displacement(factors, first, second, height):
    depth, width = first.shape[1:3]
    return pl.pallas_call(
        functools.partial(displacement_kernel, height),
        out_shape=jax.ShapeDtypeStruct((3, depth, height, width), jnp.float32),
        name="displacement",
    )(factors, first, second)


def corners():
    return [(cz, cy, cx) for cz in range(2) for cy in range(2) for cx in range(2)]


def upper_nodes(field):
    column = lax.ppermute(field[:, :, :, :1], ("gx", "gy", "gz"), slab_route(0, -1))
    wide = jnp.concatenate([field, column], axis=3)
    wide = jnp.concatenate([wide, to_slab(wide[:, :1], -1)], axis=1)
    return jnp.pad(wide, ((0, 0), (0, 0), (0, 1), (0, 0)))


def fold_upper(values):
    depth, width = values.shape[1] - 1, values.shape[3] - 1
    carried = to_slab(values[:, depth:], 1)
    values = jnp.concatenate([values[:, :1] + carried, values[:, 1:depth]], axis=1)
    column = lax.ppermute(values[:, :, :, width:], ("gx", "gy", "gz"), slab_route(0, 1))
    return jnp.concatenate([values[:, :, :, :1] + column, values[:, :, :, 1:width]], axis=3)


def corner_columns(nodes, shape):
    depth, height, width = shape
    return jnp.stack(
        [
            nodes[c, cz : cz + depth, cy : cy + height, cx : cx + width]
            for c in range(3)
            for cz, cy, cx in corners()
        ]
    )


def element_products(columns, table):
    return jnp.einsum(
        "rc,czyx->rzyx", jnp.asarray(table, jnp.float32), columns, precision=lax.Precision.HIGHEST
    )


def spread_corner(values, corner):
    return jnp.pad(values, ((0, 0),) + tuple((c, 1 - c) for c in corner))


def plain_forces(field, modulus, table):
    _, height, _ = modulus.shape
    columns = corner_columns(upper_nodes(field), modulus.shape)
    products = element_products(columns, table) * modulus
    products = products.reshape((3, 8) + modulus.shape)
    total = sum(spread_corner(products[:, node], corner) for node, corner in enumerate(corners()))
    return fold_upper(total[:, :, :height])


def plain_path(table, fields, height):
    modulus, *force, free, density = jnp.swapaxes(fields[..., :height], 2, 3)
    _, height, _ = density.shape
    spread = sum(spread_corner(modulus[None], corner) for corner in corners())
    precondition = free / (float(table[0, 0]) * fold_upper(spread[:, :, :height]))
    residual = jnp.stack(force)
    search = precondition * residual
    start = (jnp.zeros_like(residual), residual, search, inner_sum(residual * search))

    def iterate(_, state):
        moved, residual, search, gamma = state
        image = free * plain_forces(free * search, modulus, table)
        alpha = gamma / inner_sum(search * image)
        moved = moved + alpha * search
        residual = residual - alpha * image
        scaled = precondition * residual
        gamma_next = inner_sum(residual * scaled)
        return moved, residual, scaled + gamma_next / gamma * search, gamma_next

    moved = lax.fori_loop(0, ITERS, iterate, start)[0]
    columns = corner_columns(upper_nodes(moved), modulus.shape)
    energy = 0.5 * modulus * jnp.sum(columns * element_products(columns, table), axis=0)
    specific = jnp.swapaxes(energy / density, 1, 2)
    return jnp.pad(specific, ((0, 0), (0, 0), (0, LANES - height))), moved


def side_halos(basis):
    width = basis.shape[2]
    return edges_swapped(basis[:, :, :RAD], basis[:, :, width - RAD :], 0)


def remodelled(plain, cells, place, density, bone, stats, basis, sides):
    planar, low, high, factors, verdict = run_smooth(plain, cells, place, stats, basis, sides, density.shape[1])
    pieces, blocks = depth_pieces(planar, low, high)
    return run_finish(factors, density, bone, pieces, blocks), factors, verdict


def on_device(density, bone, fixed, load):
    table = element_stiffness()
    density, bone, fixed, load = density[0], bone[0], fixed[0], load[:, 0]
    depth, height, width = density.shape
    slabs = lax.axis_size("gy") * lax.axis_size("gz")
    slab = lax.axis_index("gz") * lax.axis_size("gy") + lax.axis_index("gy")
    nx = lax.axis_size("gx")
    cells = density.size * nx * slabs
    place = jnp.stack([lax.axis_index("gx"), slab]).astype(jnp.int32)

    up, down = run_messages(density, bone, fixed, load)
    got_up = to_slab(up, 1)
    got_down = to_slab(down, -1)
    fields, edges = run_prepare(place, density, bone, fixed, load)
    around = [side for sent, steps in zip(edges, (0, 1, -1)) for side in edges_moved(sent, steps)]
    first, second, basis, stats, *ends = run_krylov(
        table, place, fields, (got_up, got_down, *around)
    )
    sides = edges_moved(ends, 0)
    stats = total_over_mesh(stats)
    updated, factors, verdict = remodelled(False, cells, place, density, bone, stats, basis, sides)
    moved = run_displacement(factors, first, second, height)

    shares = bone.reshape(-1, width)

    def repeated(state):
        specific, moved = plain_path(table, fields, height)
        thick = jnp.swapaxes(fields[5, ..., :height], 1, 2)
        cover = lambda length, start, count: lax.dynamic_slice(
            jnp.asarray(coverage(length)), (start,), (count,)
        )
        cover_x = cover(nx * width, place[0] * width, width)
        cover_z = cover(slabs * depth, place[1] * depth, depth)
        spread = cover_z[:, None, None] * cover_x[:, None] * jnp.asarray(coverage(height))
        total = inner_sum(specific[..., :height] * spread)
        row, lane = (lax.broadcasted_iota(jnp.int32, (8, LANES), i) for i in range(2))
        tile = jnp.where((row == 4) & (lane == 0), total, 0.0)
        again = specific[None]
        updated = remodelled(
            True, cells, place, thick, shares.reshape(bone.shape), tile, again, side_halos(again)
        )[0]
        return True, updated, moved.reshape(-1, width)

    sound = verdict.reshape(()) > 0.5
    _, updated, moved = lax.while_loop(lambda state: ~state[0], repeated, (sound, updated, moved.reshape(-1, width)))
    return updated[None], moved.reshape(3, 1, depth, height, width)


def solution(mesh):
    placed = (
        P("gz", "gy", None, "gx"),
        P("gz", "gy", None, "gx"),
        P("gz", "gy", None, "gx"),
        P(None, "gz", "gy", None, "gx"),
    )
    return jax.shard_map(
        on_device,
        mesh=mesh,
        in_specs=placed,
        out_specs=(P("gz", "gy", None, "gx"), P(None, "gz", "gy", None, "gx")),
        check_vma=False,
    )
```
